32 devices in a mesh: head: 4 (over z), blk: 8 (over y, x, core).
Axes of the slice: x: 2, y: 2, z: 4, core: 2. Of those that a mesh axis runs over, the one named last changes fastest.
Arguments:
- tokens: bfloat16 [4096, 768], P(('head', 'blk')), may hold values from -6 to 6
- cotangent: bfloat16 [4096, 768], P(('head', 'blk')), may hold values from -6 to 6
- doc_starts: int32 [16], replicated, may hold values from 0 to 4096, as said below
- norm_gain: bfloat16 [768], P(('head', 'blk')), may hold values from 0.5 to 1.5
- norm_shift: bfloat16 [768], P(('head', 'blk')), may hold values from -1.75 to 1.75
- triple_weight: bfloat16 [768, 2304], P(('head', 'blk')), may hold values from -0.21875 to 0.21875
- query_bias: bfloat16 [768], P(('head', 'blk')), may hold values from -1.75 to 1.75
- value_bias: bfloat16 [768], P(('head', 'blk')), may hold values from -1.75 to 1.75
- output_weight: bfloat16 [768, 768], P(('head', 'blk')), may hold values from -1.75 to 1.75
- output_bias: bfloat16 [768], P(('head', 'blk')), may hold values from -1.75 to 1.75
- final_gain: bfloat16 [768], P(('head', 'blk')), may hold values from 0.5 to 1.5
- final_shift: bfloat16 [768], P(('head', 'blk')), may hold values from -1.75 to 1.75
- up_weight: bfloat16 [768, 3072], P(('head', 'blk')), may hold values from -0.21875 to 0.21875
- up_bias: bfloat16 [3072], P(('head', 'blk')), may hold values from -1.75 to 1.75
- down_weight: bfloat16 [3072, 768], P(('head', 'blk')), may hold values from -0.109375 to 0.109375
- down_bias: bfloat16 [768], P(('head', 'blk')), may hold values from -1.75 to 1.75
Outputs:
- output_rows: bfloat16 [4096, 768], P(('head', 'blk'))
- input_grad: bfloat16 [4096, 768], P(('head', 'blk'))
- grad_norm_gain: float32 [768], P(('head', 'blk'))
- grad_norm_shift: float32 [768], P(('head', 'blk'))
- grad_triple_weight: float32 [768, 2304], P(('head', 'blk'))
- grad_query_bias: float32 [768], P(('head', 'blk'))
- grad_value_bias: float32 [768], P(('head', 'blk'))
- grad_output_weight: float32 [768, 768], P(('head', 'blk'))
- grad_output_bias: float32 [768], P(('head', 'blk'))
- grad_final_gain: float32 [768], P(('head', 'blk'))
- grad_final_shift: float32 [768], P(('head', 'blk'))
- grad_up_weight: float32 [768, 3072], P(('head', 'blk'))
- grad_up_bias: float32 [3072], P(('head', 'blk'))
- grad_down_weight: float32 [3072, 768], P(('head', 'blk'))
- grad_down_bias: float32 [768], P(('head', 'blk'))
The draws below stay inside these ranges and needn't reach their ends.
Inputs may be any that keep to these rules, and one draw needn't show every extreme that they name: `doc_starts`: 16 starts, never falling, the first 0; an entry may repeat (an empty document) and entries equal to 4096 start no document; every document holds at most 2048 patches and one holds exactly 2048.
All inputs are finite; a program needn't handle non-finite values.
Results may differ from the reference program's by a relative error of at most 0.03.
Values may be sent and summed in bfloat16 or wider, within the bound.
No kernel may reach another device: no remote copies, remote signals or barrier semaphores. Data moves between devices by JAX's collectives and lax.ppermute only.
A program may use at most 256 MiB of HBM per device.

```python
import jax
import jax.numpy as jnp
from jax import lax

D = 768
HEADS = 12
HEAD_DIM = 64
FF = 3072
TOK_DEV = 128
DOC_SLOTS = 16
TOKENS = 4096
DOC_MOST = 2048
N_BLK = 8


def draw_doc_starts(key, part):
    half_most = DOC_MOST // 2
    quarter_len = TOK_DEV * N_BLK
    grid_count = TOKENS // half_most
    random_count = DOC_SLOTS - grid_count - 2
    key_pick, key_place, key_extra = jax.random.split(key, 3)
    quarter_pick = jax.random.randint(key_pick, (), 0, TOKENS // quarter_len)
    low_end = jnp.maximum(0, (quarter_pick + 1) * quarter_len - DOC_MOST)
    high_end = jnp.minimum(quarter_pick * quarter_len, TOKENS - DOC_MOST)
    long_start = jax.random.randint(key_place, (), low_end, high_end + 1)
    grid_marks = jnp.arange(grid_count, dtype=jnp.int32) * half_most
    others = jax.random.randint(key_extra, (random_count,), 1, TOKENS)
    ends_pair = jnp.stack([long_start, long_start + DOC_MOST]).astype(jnp.int32)
    all_starts = jnp.concatenate([grid_marks, others.astype(jnp.int32), ends_pair])
    inside = (all_starts > long_start) & (all_starts < long_start + DOC_MOST)
    all_starts = jnp.where(inside, TOKENS, all_starts).astype(jnp.int32)
    return jnp.sort(all_starts)


def with_spikes(result, key, source, target, shards_of, factor):
    owner, partner = [(jnp.arange(result.shape[dim]) // (result.shape[dim] // shards_of)).reshape([-1 if axis == dim else 1 for axis in range(result.ndim)]) for dim in (source, target)]
    chosen = jax.random.permutation(key, shards_of)[partner]
    strong = (owner == chosen) | (owner == (partner + shards_of // 2) % shards_of)
    return jnp.where(strong, factor * result, result)


def steps_of(own_key, extent, cuts, low, largest):
    loudness = 1.0
    for dim, parts in cuts:
        heights = jax.random.uniform(jax.random.fold_in(jax.random.fold_in(own_key, 6), dim), (parts,), jnp.float32, low / len(cuts), largest / len(cuts))
        loudness = loudness * jnp.repeat(jnp.exp(heights), extent[dim] // parts).reshape((-1,) + (1,) * (len(extent) - 1 - dim))
    return loudness


def gaussian(key, shape, width, bound, cuts=(), kind=jnp.bfloat16):
    loudness = steps_of(key, shape, cuts, -0.22, 0.18) if cuts else 1.0
    values = jax.random.normal(key, shape, jnp.float32) * width * loudness
    return jnp.minimum(jnp.maximum(values, -bound), bound).astype(kind)


def bell_draw_with(rng, dims, deviation, bound, cuts, heavy, kind=jnp.bfloat16):
    drawn = deviation * jax.random.normal(rng, dims, jnp.float32)
    if cuts:
        drawn = drawn * steps_of(rng, dims, cuts, -0.22, 0.18)
    return jnp.clip(with_spikes(drawn, jax.random.fold_in(rng, 3), *heavy), -bound, bound).astype(kind)


def setup_inputs(seed: int = 0) -> dict:
    splits = jax.random.split(jax.random.key(seed), 17)
    return {
        "tokens": gaussian(splits[0], (TOKENS, D), 1.0, 6.0, ((0, 32),)),
        "cotangent": bell_draw_with(splits[1], (TOKENS, D), 1.0, 6.0, ((0, 32),), (0, 1, 32, 2.75)),
        "doc_starts": draw_doc_starts(jax.random.fold_in(splits[16], 71), 0),
        "norm_gain": jnp.clip(1.0 + 0.1 * jax.random.normal(splits[3], (D,), jnp.float32), 0.5, 1.5).astype(jnp.bfloat16),
        "norm_shift": gaussian(splits[4], (D,), 0.3, 1.75, ((0, 32),)),
        "triple_weight": gaussian(splits[5], (D, 3 * D), D ** -0.5, 0.21875, ((0, 32),)),
        "query_bias": gaussian(splits[6], (D,), 0.3, 1.75, ((0, 32),)),
        "value_bias": gaussian(splits[7], (D,), 0.3, 1.75, ((0, 32),)),
        "output_weight": gaussian(splits[8], (D, D), (D // 64) ** -0.5, 1.75, ((0, 32),)),
        "output_bias": gaussian(splits[9], (D,), 0.3, 1.75, ((0, 32),)),
        "final_gain": jnp.clip(1.0 + 0.1 * jax.random.normal(splits[10], (D,), jnp.float32), 0.5, 1.5).astype(jnp.bfloat16),
        "final_shift": gaussian(splits[11], (D,), 0.3, 1.75, ((0, 32),)),
        "up_weight": gaussian(splits[12], (D, FF), D ** -0.5, 0.21875, ((0, 32),)),
        "up_bias": gaussian(splits[13], (FF,), 0.3, 1.75, ((0, 32),)),
        "down_weight": gaussian(splits[14], (FF, D), FF ** -0.5, 0.109375, ((0, 32),)),
        "down_bias": gaussian(splits[15], (D,), 0.3, 1.75, ((0, 32),)),
    }


epsilon = 1e-06
neg_fill = -1e+30

@jax.custom_vjp
def low(v):
    return lax.optimization_barrier(v.astype(jnp.bfloat16)).astype(jnp.float32)

@jax.custom_vjp
def low_back(v):
    return v

def low_keep(v):
    return (low(v), None)

def low_pass(kept, grad):
    return (grad,)

def back_keep(v):
    return (v, None)

def back_low(kept, grad):
    return (low(grad),)
low.defvjp(low_keep, low_pass)
low_back.defvjp(back_keep, back_low)

def layer_norm(values, gain_full, shift_full):
    centre = lax.optimization_barrier(jnp.mean(values, axis=-1, keepdims=True))
    offset = values - centre
    scaled = offset * lax.rsqrt(lax.optimization_barrier(jnp.mean(offset * offset, axis=-1, keepdims=True)) + epsilon)
    return scaled * gain_full + shift_full

def matmul_high(left, right):
    return jnp.dot(left, right, precision=lax.Precision.HIGHEST)

def attention(queries, key_rows, value_rows, segment):
    total_rows = queries.shape[0]
    block_rows = min(512, total_rows)
    block_count = total_rows // block_rows
    score_scale = queries.shape[-1] ** (-0.5)

    def one_block(packed):
        query_block, seg_block = packed
        scores = jnp.einsum('qhd,khd->hqk', query_block, key_rows, precision=lax.Precision.HIGHEST) * score_scale
        allowed = seg_block[:, None] == segment[None, :]
        scores = jnp.where(allowed[None], scores, neg_fill)
        scores = low_back(scores)
        log_total = jax.nn.logsumexp(scores, axis=-1, keepdims=True)
        prob_rows = low(jnp.exp(scores - log_total))
        return jnp.einsum('hqk,khd->qhd', prob_rows, value_rows, precision=lax.Precision.HIGHEST)
    blocks_in = queries.reshape(block_count, block_rows, queries.shape[1], queries.shape[2])
    outcome = lax.map(jax.checkpoint(one_block), (blocks_in, segment.reshape(block_count, block_rows)))
    return outcome.reshape(queries.shape)

def reference(tokens, cotangent, doc_starts, norm_gain, norm_shift, triple_weight, query_bias, value_bias, output_weight, output_bias, final_gain, final_shift, up_weight, up_bias, down_weight, down_bias):
    position = jnp.arange(TOKENS, dtype=jnp.int32)
    segment = lax.optimization_barrier(jnp.sum((doc_starts[None, :] <= position[:, None]).astype(jnp.int32), axis=1))

    def forward(inputs, norm_gain, norm_shift, triple_weight, query_bias, value_bias, output_weight, output_bias, final_gain, final_shift, up_weight, up_bias, down_weight, down_bias):
        first_in = low(layer_norm(inputs, norm_gain, norm_shift))
        triple = matmul_high(first_in, triple_weight) + jnp.concatenate([query_bias, jnp.zeros_like(query_bias), value_bias])
        triple = low_back(low(triple))
        shaped = triple.reshape(TOKENS, 3, HEADS, HEAD_DIM)
        mixed_heads = attention(shaped[:, 0], shaped[:, 1], shaped[:, 2], segment)
        mixed_heads = low_back(low(mixed_heads.reshape(TOKENS, D)))
        branch = low_back(matmul_high(mixed_heads, output_weight) + output_bias)
        middle = inputs + branch
        second = low(layer_norm(middle, final_gain, final_shift))
        hidden = low_back(matmul_high(second, up_weight) + up_bias)
        active = low(jax.nn.gelu(hidden, approximate=False))
        return middle + low_back(matmul_high(active, down_weight) + down_bias)
    weights_wide = [norm_gain.astype(jnp.float32), norm_shift.astype(jnp.float32), triple_weight.astype(jnp.float32), query_bias.astype(jnp.float32), value_bias.astype(jnp.float32), output_weight.astype(jnp.float32), output_bias.astype(jnp.float32), final_gain.astype(jnp.float32), final_shift.astype(jnp.float32), up_weight.astype(jnp.float32), up_bias.astype(jnp.float32), down_weight.astype(jnp.float32), down_bias.astype(jnp.float32)]
    output_rows, pullback = jax.vjp(forward, tokens.astype(jnp.float32), *weights_wide)
    gradients = pullback(cotangent.astype(jnp.float32))
    return (output_rows.astype(jnp.bfloat16), gradients[0].astype(jnp.bfloat16), gradients[1], gradients[2], gradients[3], gradients[4], gradients[5], gradients[6], gradients[7], gradients[8], gradients[9], gradients[10], gradients[11], gradients[12], gradients[13])
```

```python
import functools

import jax
import jax.numpy as jnp
from jax import lax
from jax.experimental import pallas as pl
from jax.experimental.pallas import tpu as pltpu
from jax.sharding import PartitionSpec as P

HEADS = 12
HEAD_DIM = 64

epsilon = 1e-06
neg_fill = -1e30
root_half = 0.7071067811865476
inv_root_two_pi = 0.3989422804014327

F32 = jnp.float32
BF16 = jnp.bfloat16
WIN = 256
TILE_BLOCKS = 4
CONTRACT_LAST = (((1,), (1,)), ((), ()))
CONTRACT_FIRST = (((0,), (0,)), ((), ()))
PLAIN = (((1,), (0,)), ((), ()))


def norm_parts(values):
    centre = jnp.mean(values, axis=-1, keepdims=True)
    offset = values - centre
    inv_spread = lax.rsqrt(jnp.mean(offset * offset, axis=-1, keepdims=True) + epsilon)
    return (offset * inv_spread, inv_spread)


def norm_pull(grad_out, normed, inv_spread, gain_full):
    grad_normed = grad_out * gain_full
    return inv_spread * (
        grad_normed
        - jnp.mean(grad_normed, axis=-1, keepdims=True)
        - normed * jnp.mean(grad_normed * normed, axis=-1, keepdims=True)
    )


def gelu_pair(hidden):
    normal_cdf = 0.5 * (1.0 + lax.erf(hidden * root_half))
    return (
        hidden * normal_cdf,
        normal_cdf + hidden * inv_root_two_pi * jnp.exp(-0.5 * hidden * hidden),
    )


def mat(left, right, dims=PLAIN):
    return lax.dot_general(left, right, dims, preferred_element_type=F32)


def turn(x, step):
    size = lax.axis_size("head")
    return lax.ppermute(x, "head", [(i, (i + step) % size) for i in range(size)])


def swap(x, bits):
    size = lax.axis_size("blk")
    return lax.ppermute(x, "blk", [(i, i ^ bits) for i in range(size)])


def in_pair(bit, mine, other):
    return jnp.where(bit == 0, jnp.stack([mine, other]), jnp.stack([other, mine]))


def pick(x, index, axis):
    return lax.dynamic_index_in_dim(x, index, axis, keepdims=False)


def by_head(slots):
    size = len(slots)
    doubled = jnp.stack([slots[(size - 1 - i) % size] for i in range(2 * size - 1)])
    return lax.dynamic_slice_in_dim(doubled, size - 1 - lax.axis_index("head"), size, 0)


def by_group(slots):
    size = len(slots)
    doubled = jnp.stack([slots[i % size] for i in range(2 * size - 1)])
    start = lax.rem(size - lax.axis_index("head"), size)
    return lax.dynamic_slice_in_dim(doubled, start, size, 0)


def after(value, *earlier):
    flat, tree = jax.tree.flatten(value)
    held = lax.optimization_barrier((tuple(flat), earlier))[0]
    return jax.tree.unflatten(tree, held)


def gather_pieces(x):
    if lax.axis_size("blk") != 8:
        return [lax.all_gather(x, "blk", axis=0, tiled=False)]
    pieces = [None] * 8
    pieces[0] = x
    for bits in (2, 4, 6):
        pieces[bits] = swap(x, bits)
    for bits in (0, 2, 4, 6):
        pieces[bits + 1] = swap(pieces[bits], 1)
    return pieces


def doc_range(meta, first, last, total):
    low, high = jnp.int32(0), jnp.int32(total)
    for i in range(meta.shape[0] - 2):
        start = meta[2 + i]
        low = jnp.where(start <= first, start, low)
        high = jnp.where(start > last, jnp.minimum(high, start), high)
    return low, high


def row_ranges(meta, first, rows, total):
    place = first + lax.broadcasted_iota(jnp.int32, (rows, 1), 0)
    low = jnp.zeros((rows, 1), jnp.int32)
    high = jnp.full((rows, 1), total, jnp.int32)
    for i in range(meta.shape[0] - 2):
        start = meta[2 + i]
        low = jnp.where(place >= start, start, low)
        high = jnp.where(place < start, jnp.minimum(high, start), high)
    return low, high


def head_rows(width, shift, scale):
    lane = lax.broadcasted_iota(jnp.int32, (1, width), 1)
    return [
        jnp.where((lane >= shift + 64 * i) & (lane < shift + 64 * (i + 1)), scale, 0.0).astype(F32)
        for i in range(3)
    ]


def spread_heads(block, rows):
    wide = block.astype(F32)
    return jnp.concatenate([wide * row for row in rows], axis=0).astype(BF16)


def fold_heads(stack, rows):
    return stack[0] * rows[0] + stack[1] * rows[1] + stack[2] * rows[2]


def block_copies(meta, nh, nb, pieces, place, sems):
    h, b = meta[0], meta[1]
    copies = []
    if len(pieces) == nb:
        for m, piece in enumerate(pieces):
            for r in range(nh):
                block = lax.rem(h - r + nh, nh) * nb + jnp.bitwise_xor(b, m)
                copies.append(pltpu.make_async_copy(*place(piece, None, r, block), sems.at[m, r]))
        for copy in copies:
            copy.start()
        return copies

    def run(which):
        def one(i, carry):
            for r in range(nh):
                block = lax.rem(h - r + nh, nh) * nb + i
                copy = pltpu.make_async_copy(*place(pieces[0], i, r, block), sems.at[i, r])
                (copy.start if which == 0 else copy.wait)()
            return carry

        lax.fori_loop(0, nb, one, 0)

    run(0)

    class Rest:
        def wait(self):
            run(1)

    return [Rest()]


def row_place(target, rows):
    def place(piece, index, r, block):
        source = piece if index is None else piece.at[index]
        return source.at[pl.ds(r * rows, rows), :], target.at[block]

    return place


def lane_place(target, rows):
    def place(piece, index, r, block):
        source = piece if index is None else piece.at[index]
        return source.at[:, pl.ds(r * rows, rows)], target.at[block]

    return place


def tile_bounds(meta, first, rows, total):
    low, high = doc_range(meta, first, first + rows - 1, total)
    tile = TILE_BLOCKS * rows
    return lax.div(low, tile), lax.div(high + tile - 1, tile)


def column(row, rows):
    return jnp.transpose(jnp.broadcast_to(row, (rows, rows)))[:, :1]


def forward_kernel(nh, nb, count, meta, q_ref, *rest):
    pieces, (wide_ref, low_ref, lse_ref), (kv, sems) = rest[:count], rest[count : count + 3], rest[count + 3 :]
    rows = q_ref.shape[0] // nh
    total = nh * nb * rows
    tile = TILE_BLOCKS * rows
    h, b = meta[0], meta[1]
    for copy in block_copies(meta, nh, nb, pieces, row_place(kv, rows), sems):
        copy.wait()
    query_rows = head_rows(WIN, 0, HEAD_DIM**-0.5)
    value_rows = head_rows(WIN, 64, 1.0)
    for r in range(nh):
        first = (lax.rem(h - r + nh, nh) * nb + b) * rows
        tile_low, tile_high = tile_bounds(meta, first, rows, total)
        low, high = row_ranges(meta, first, rows, total)
        masked = spread_heads(q_ref[r * rows : (r + 1) * rows, :], query_rows)

        def step(t, state):
            top, norm, out = state
            keys = kv[pl.ds(t * TILE_BLOCKS, TILE_BLOCKS), :, 0:WIN].reshape(tile, WIN)
            values = kv[pl.ds(t * TILE_BLOCKS, TILE_BLOCKS), :, 128 : 128 + WIN].reshape(tile, WIN)
            place = t * tile + lax.broadcasted_iota(jnp.int32, (1, tile), 1)
            allowed = (place >= low) & (place < high)
            scores = mat(masked, keys, CONTRACT_LAST).reshape(3, rows, tile)
            scores = jnp.where(allowed[None], scores, neg_fill)
            new_top = jnp.maximum(top, jnp.max(scores, axis=-1, keepdims=True))
            weights = jnp.exp(scores - new_top)
            factor = jnp.exp(top - new_top)
            norm = norm * factor + jnp.sum(weights, axis=-1, keepdims=True)
            part = mat(weights.astype(BF16).reshape(3 * rows, tile), values)
            return new_top, norm, out * factor + part.reshape(3, rows, WIN)

        top, norm, out = lax.fori_loop(
            tile_low,
            tile_high,
            step,
            (
                jnp.full((3, rows, 1), neg_fill, F32),
                jnp.zeros((3, rows, 1), F32),
                jnp.zeros((3, rows, WIN), F32),
            ),
        )
        attended = fold_heads(out / norm, value_rows)
        wide_ref[r * rows : (r + 1) * rows, :] = attended
        low_ref[r * rows : (r + 1) * rows, :] = attended.astype(BF16)
        log_total = top + jnp.log(norm)
        for i in range(3):
            lse_ref[i : i + 1, r * rows : (r + 1) * rows] = jnp.transpose(
                jnp.broadcast_to(log_total[i], (rows, rows))
            )[:1]
    lse_ref[3:8, :] = jnp.zeros((5, nh * rows), F32)


def delta_kernel(nh, wide_ref, lse_ref, *rest):
    pieces, (grad_ref, stat_ref) = rest[:nh], rest[nh:]
    rows = pieces[0].shape[0]
    value_rows = head_rows(WIN, 64, 1.0)
    stat_ref[...] = lse_ref[...]
    for r in range(nh):
        span = slice(r * rows, (r + 1) * rows)
        grad = pieces[r][...]
        grad_ref[span, :] = grad
        product = grad.astype(F32) * wide_ref[span, :]
        for i in range(3):
            delta = jnp.sum(product * value_rows[i], axis=-1, keepdims=True)
            stat_ref[3 + i : 4 + i, span] = jnp.transpose(jnp.broadcast_to(delta, (rows, rows)))[:1]


def query_kernel(nh, nb, count, meta, q_ref, g_ref, stat_ref, *rest):
    pieces, out_ref, (kv, sems) = rest[:count], rest[count], rest[count + 1 :]
    rows = q_ref.shape[0] // nh
    total = nh * nb * rows
    tile = TILE_BLOCKS * rows
    h, b = meta[0], meta[1]
    for copy in block_copies(meta, nh, nb, pieces, row_place(kv, rows), sems):
        copy.wait()
    query_rows = head_rows(WIN, 0, HEAD_DIM**-0.5)
    value_rows = head_rows(WIN, 64, 1.0)
    for r in range(nh):
        span = slice(r * rows, (r + 1) * rows)
        first = (lax.rem(h - r + nh, nh) * nb + b) * rows
        tile_low, tile_high = tile_bounds(meta, first, rows, total)
        low, high = row_ranges(meta, first, rows, total)
        masked = spread_heads(q_ref[span, :], query_rows)
        grads = spread_heads(g_ref[span, :], value_rows)
        log_total = jnp.stack([column(stat_ref[i : i + 1, span], rows) for i in range(3)])
        delta = jnp.stack([column(stat_ref[3 + i : 4 + i, span], rows) for i in range(3)])

        def step(t, state):
            keys = kv[pl.ds(t * TILE_BLOCKS, TILE_BLOCKS), :, 0:WIN].reshape(tile, WIN)
            values = kv[pl.ds(t * TILE_BLOCKS, TILE_BLOCKS), :, 128 : 128 + WIN].reshape(tile, WIN)
            place = t * tile + lax.broadcasted_iota(jnp.int32, (1, tile), 1)
            allowed = (place >= low) & (place < high)
            scores = mat(masked, keys, CONTRACT_LAST).reshape(3, rows, tile)
            probs = jnp.exp(jnp.where(allowed[None], scores, neg_fill) - log_total)
            grad_probs = mat(grads, values, CONTRACT_LAST).reshape(3, rows, tile)
            grad_scores = (probs * (grad_probs - delta)).astype(BF16)
            part = mat(grad_scores.reshape(3 * rows, tile), keys)
            return state + part.reshape(3, rows, WIN)

        total_grad = lax.fori_loop(tile_low, tile_high, step, jnp.zeros((3, rows, WIN), F32))
        out_ref[span, :] = fold_heads(total_grad, query_rows).astype(BF16)


def key_kernel(nh, nb, count, meta, kv_ref, *rest):
    q_in, g_in, s_in = rest[:count], rest[count : 2 * count], rest[2 * count : 3 * count]
    out_ref = rest[3 * count]
    queries_all, grads_all, stats_all, q_sems, g_sems, s_sems = rest[3 * count + 1 :]
    rows = kv_ref.shape[0] // nh
    total = nh * nb * rows
    tile = TILE_BLOCKS * rows
    h, b = meta[0], meta[1]
    copies = block_copies(meta, nh, nb, q_in, row_place(queries_all, rows), q_sems)
    copies += block_copies(meta, nh, nb, g_in, row_place(grads_all, rows), g_sems)
    copies += block_copies(meta, nh, nb, s_in, lane_place(stats_all, rows), s_sems)
    for copy in copies:
        copy.wait()
    key_rows = head_rows(WIN, 0, HEAD_DIM**-0.5)
    value_rows = head_rows(WIN, 64, 1.0)
    for r in range(nh):
        span = slice(r * rows, (r + 1) * rows)
        first = (lax.rem(h - r + nh, nh) * nb + b) * rows
        tile_low, tile_high = tile_bounds(meta, first, rows, total)
        low, high = row_ranges(meta, first, rows, total)
        keys = spread_heads(kv_ref[span, 0:WIN], key_rows)
        values = spread_heads(kv_ref[span, 128 : 128 + WIN], value_rows)

        def step(t, state):
            grad_keys, grad_values = state
            queries = queries_all[pl.ds(t * TILE_BLOCKS, TILE_BLOCKS)].reshape(tile, WIN)
            grads = grads_all[pl.ds(t * TILE_BLOCKS, TILE_BLOCKS)].reshape(tile, WIN)
            stats = [stats_all[t * TILE_BLOCKS + i] for i in range(TILE_BLOCKS)]
            log_total = jnp.stack(
                [jnp.concatenate([s[i : i + 1] for s in stats], axis=1) for i in range(3)]
            )
            delta = jnp.stack(
                [jnp.concatenate([s[3 + i : 4 + i] for s in stats], axis=1) for i in range(3)]
            )
            place = t * tile + lax.broadcasted_iota(jnp.int32, (1, tile), 1)
            allowed = (place >= low) & (place < high)
            scores = mat(keys, queries, CONTRACT_LAST).reshape(3, rows, tile)
            probs = jnp.exp(jnp.where(allowed[None], scores, neg_fill) - log_total)
            grad_probs = mat(values, grads, CONTRACT_LAST).reshape(3, rows, tile)
            grad_scores = (probs * (grad_probs - delta)).astype(BF16)
            part_value = mat(probs.astype(BF16).reshape(3 * rows, tile), grads)
            part_key = mat(grad_scores.reshape(3 * rows, tile), queries)
            return (
                grad_keys + part_key.reshape(3, rows, WIN),
                grad_values + part_value.reshape(3, rows, WIN),
            )

        zero = jnp.zeros((3, rows, WIN), F32)
        grad_keys, grad_values = lax.fori_loop(tile_low, tile_high, step, (zero, zero))
        key_out = fold_heads(grad_keys, key_rows)
        value_out = fold_heads(grad_values, value_rows)
        out_ref[span, 0:128] = key_out[:, 0:128].astype(BF16)
        out_ref[span, 128:256] = (key_out[:, 128:256] + value_out[:, 0:128]).astype(BF16)
        out_ref[span, 256:384] = value_out[:, 128:256].astype(BF16)


SMEM_SPEC = pl.BlockSpec(memory_space=pltpu.SMEM)
VMEM_SPEC = pl.BlockSpec(memory_space=pltpu.VMEM)
ANY_SPEC = pl.BlockSpec(memory_space=pl.ANY)


def kernel_params():
    return pltpu.CompilerParams(vmem_limit_bytes=56 * 1024 * 1024)


def cost(matmuls, nh, nb, rows):
    flops = matmuls * 2 * 3 * rows * WIN * 9 * TILE_BLOCKS * rows
    return pl.CostEstimate(flops=flops, bytes_accessed=nh * nb * rows * 384 * 2, transcendentals=0)


def attend(meta, queries, pieces, nh, nb):
    length = queries.shape[0]
    rows = length // nh
    count = len(pieces)
    return pl.pallas_call(
        functools.partial(forward_kernel, nh, nb, count),
        out_shape=(
            jax.ShapeDtypeStruct((length, WIN), F32),
            jax.ShapeDtypeStruct((length, WIN), BF16),
            jax.ShapeDtypeStruct((8, length), F32),
        ),
        in_specs=[SMEM_SPEC, VMEM_SPEC] + [ANY_SPEC] * count,
        out_specs=(VMEM_SPEC,) * 3,
        scratch_shapes=[
            pltpu.VMEM((nh * nb, rows, 384), BF16),
            pltpu.SemaphoreType.DMA((nb, nh)),
        ],
        compiler_params=kernel_params(),
        cost_estimate=cost(2, nh, nb, rows),
        name="attend",
    )(meta, queries, *pieces)


def delta_rows(wide, log_total, grads):
    nh = len(grads)
    length = wide.shape[0]
    return pl.pallas_call(
        functools.partial(delta_kernel, nh),
        out_shape=(
            jax.ShapeDtypeStruct((length, WIN), BF16),
            jax.ShapeDtypeStruct((8, length), F32),
        ),
        in_specs=[VMEM_SPEC] * (2 + nh),
        out_specs=(VMEM_SPEC,) * 2,
        compiler_params=kernel_params(),
        name="delta",
    )(wide, log_total, *grads)


def query_grads(meta, queries, grads, stats, pieces, nh, nb):
    length = queries.shape[0]
    rows = length // nh
    count = len(pieces)
    return pl.pallas_call(
        functools.partial(query_kernel, nh, nb, count),
        out_shape=jax.ShapeDtypeStruct((length, WIN), BF16),
        in_specs=[SMEM_SPEC] + [VMEM_SPEC] * 3 + [ANY_SPEC] * count,
        out_specs=VMEM_SPEC,
        scratch_shapes=[
            pltpu.VMEM((nh * nb, rows, 384), BF16),
            pltpu.SemaphoreType.DMA((nb, nh)),
        ],
        compiler_params=kernel_params(),
        cost_estimate=cost(3, nh, nb, rows),
        name="query_grads",
    )(meta, queries, grads, stats, *pieces)


def key_grads(meta, own, queries, grads, stats, nh, nb):
    length = own.shape[0]
    rows = length // nh
    count = len(queries)
    return pl.pallas_call(
        functools.partial(key_kernel, nh, nb, count),
        out_shape=jax.ShapeDtypeStruct((length, 384), BF16),
        in_specs=[SMEM_SPEC, VMEM_SPEC] + [ANY_SPEC] * (3 * count),
        out_specs=VMEM_SPEC,
        scratch_shapes=[
            pltpu.VMEM((nh * nb, rows, WIN), BF16),
            pltpu.VMEM((nh * nb, rows, WIN), BF16),
            pltpu.VMEM((nh * nb, 8, rows), F32),
            pltpu.SemaphoreType.DMA((nb, nh)),
            pltpu.SemaphoreType.DMA((nb, nh)),
            pltpu.SemaphoreType.DMA((nb, nh)),
        ],
        compiler_params=kernel_params(),
        cost_estimate=cost(4, nh, nb, rows),
        name="key_grads",
    )(meta, own, *queries, *grads, *stats)


def gather_group_rows(slots, nh, nb):
    here = by_head(slots)
    if nb != 8:
        whole = lax.all_gather(here, "blk", axis=0, tiled=False)
        return jnp.moveaxis(whole, 0, 1).reshape(-1, here.shape[-1])
    b = lax.axis_index("blk")
    core, x_bit, y_bit = b & 1, (b >> 1) & 1, b >> 2
    side, up, cross = swap(here, 2), swap(here, 4), swap(here, 6)
    square = in_pair(y_bit, in_pair(x_bit, here, side), in_pair(x_bit, up, cross))
    whole = in_pair(core, square, swap(square, 1))
    return whole.transpose(3, 1, 2, 0, 4, 5).reshape(-1, here.shape[-1])


def scatter_group_rows(grad, nh, nb):
    width = grad.shape[-1]
    h, b = lax.axis_index("head"), lax.axis_index("blk")
    if nb != 8:
        parts = grad.reshape(nh, nb, -1, width)
        mine = lax.psum_scatter(parts, "blk", scatter_dimension=1, tiled=False)
        mine = mine.astype(BF16)
    else:
        core, x_bit, y_bit = b & 1, (b >> 1) & 1, b >> 2
        parts = grad.astype(BF16).reshape(nh, 2, 2, 2, -1, width)
        sent = swap(pick(parts, 1 - core, 3), 1)
        chip = (pick(parts, core, 3).astype(F32) + sent.astype(F32)).astype(BF16)

        def part(y, x):
            return pick(pick(chip, y, 1), x, 1)

        side = swap(part(y_bit, 1 - x_bit), 2)
        up = swap(part(1 - y_bit, x_bit), 4)
        cross = swap(part(1 - y_bit, 1 - x_bit), 6)
        mine = part(y_bit, x_bit).astype(F32) + side.astype(F32)
        mine = (mine + up.astype(F32) + cross.astype(F32)).astype(BF16)
    out = []
    for r in range(nh):
        slot = pick(mine, lax.rem(h - r + nh, nh), 0)
        out.append(turn(slot, -r) if r else slot)
    return out


def gather_chips(x, nh, nb, first_bits):
    b = lax.axis_index("blk")
    slots = [x] + [turn(x, r) for r in range(1, nh)]
    here = by_head(slots)
    last_bits = 6 - first_bits
    first_bit, last_bit = (b // first_bits) & 1, (b // last_bits) & 1
    return here, first_bits, last_bits, first_bit, last_bit


def finish_gather(held):
    here, first_bits, last_bits, first_bit, last_bit = held
    line = in_pair(first_bit, here, swap(here, first_bits))
    square = in_pair(last_bit, line, swap(line, last_bits))
    if first_bits == 2:
        return jnp.moveaxis(square, 2, 0)
    return square.transpose((2, 1, 0) + tuple(range(3, square.ndim)))


def scatter_chips(grad, nh, first_bits):
    h, b = lax.axis_index("head"), lax.axis_index("blk")
    x_bit, y_bit = (b >> 1) & 1, b >> 2
    low = grad.astype(BF16)
    order = ((2, x_bit, 2), (1, y_bit, 4)) if first_bits == 2 else ((1, y_bit, 4), (1, x_bit, 2))
    for axis, bit, bits in order:
        sent = swap(pick(low, 1 - bit, axis), bits)
        low = (pick(low, bit, axis).astype(F32) + sent.astype(F32)).astype(BF16)
    total = pick(low, h, 0).astype(F32)
    for r in range(1, nh):
        total = total + turn(pick(low, lax.rem(h - r + nh, nh), 0), -r).astype(F32)
    return total


def shards(
    tokens,
    cotangent,
    doc_starts,
    norm_gain,
    norm_shift,
    triple_weight,
    query_bias,
    value_bias,
    output_weight,
    output_bias,
    final_gain,
    final_shift,
    up_weight,
    up_bias,
    down_weight,
    down_bias,
):
    nh = lax.axis_size("head")
    nb = lax.axis_size("blk")
    devices = nh * nb
    h = lax.axis_index("head")
    b = lax.axis_index("blk")
    core = b & 1
    rows, width = tokens.shape
    part = norm_gain.shape[0]
    group = HEADS // nh * HEAD_DIM
    ff_part = up_bias.shape[0]
    meta = jnp.concatenate([jnp.stack([h, b]).astype(jnp.int32), doc_starts])

    packed = jnp.concatenate(
        [
            norm_gain,
            norm_shift,
            query_bias,
            value_bias,
            output_bias,
            final_gain,
            final_shift,
            down_bias,
            up_bias,
        ]
    ).reshape(12, part)
    vectors = lax.all_to_all(
        jnp.broadcast_to(packed[None], (devices, 12, part)), ("head", "blk"), 0, 0, tiled=True
    )
    up_bias_all = vectors[:, 8:].reshape(devices // 2, 2, ff_part).astype(F32)
    up_bias_half = pick(up_bias_all, core, 1).reshape(-1)
    lines = vectors[:, :8].transpose(1, 0, 2).reshape(8, width).astype(F32)
    gain_one, shift_one, query_all, value_all, out_bias, gain_two, shift_two, down_bias_all = (
        lines[i] for i in range(8)
    )

    token_slots = [tokens] + [turn(tokens, r) for r in range(1, nh)]
    token_rows = jnp.concatenate(token_slots, axis=0)

    columns = triple_weight.reshape(part, 3, nh, group)
    columns = jnp.concatenate([columns[:, 1], columns[:, 2], columns[:, 0]], axis=-1)
    columns = columns.transpose(1, 0, 2)
    column_slots = [pick(columns, h, 0)]
    for r in range(1, nh):
        column_slots.append(turn(pick(columns, lax.rem(h + r, nh), 0), r))
    group_weight = gather_group_rows(column_slots, nh, nb)
    key_value_weight = group_weight[:, : 2 * group]
    query_weight = jnp.pad(group_weight[:, 2 * group :], ((0, 0), (0, WIN - group)))

    ff_half = devices // 2 * ff_part
    up_parts = up_weight.reshape(part, devices // 2, 2, ff_part)
    if nb == 8:
        up_mine = pick(up_parts, core, 2).reshape(part, ff_half)
        up_other = swap(pick(up_parts, 1 - core, 2).reshape(part, ff_half), 1)
        up_chip = in_pair(core, up_mine, up_other)
        lower = jnp.concatenate([down_weight, output_weight], axis=0)
        cot_other = swap(cotangent, 1)
        up_chip, lower = after((up_chip, lower), *token_slots)
        up_held = gather_chips(up_chip, nh, nb, 2)
        low_held = gather_chips(lower, nh, nb, 4)
    else:
        cot_other = swap(cotangent, 1)

    token_wide = token_rows.astype(F32)
    normed_one, spread_one = norm_parts(token_wide)
    first_low = (normed_one * gain_one + shift_one).astype(BF16)
    value_bias_own = lax.dynamic_slice_in_dim(value_all, h * group, group)
    query_bias_own = lax.dynamic_slice_in_dim(query_all, h * group, group)
    kv_bias = jnp.concatenate([jnp.zeros((group,), F32), value_bias_own])
    key_values = (mat(first_low, key_value_weight) + kv_bias).astype(BF16)
    kv_pieces = gather_pieces(key_values)
    q_bias = jnp.pad(query_bias_own, (0, WIN - group))
    queries = (mat(first_low, query_weight) + q_bias).astype(BF16)

    wide, attended, log_total = attend(meta, queries, kv_pieces, nh, nb)

    if nb == 8:
        up_held, low_held = (
            (after(held[0], *kv_pieces),) + held[1:] for held in (up_held, low_held)
        )
        up_half = finish_gather(up_held).reshape(width, ff_half)
        low_all = finish_gather(low_held)
        down_half = low_all[..., :ff_part, :].reshape(ff_half, width)
        out_mine = low_all[..., ff_part:, :]
        out_all = in_pair(core, out_mine, swap(out_mine, 1))
        out_weight = out_all.transpose(1, 2, 3, 0, 4, 5).reshape(width, width)
    else:
        up_all = lax.all_gather(up_weight, ("head", "blk"), axis=0, tiled=True)
        up_half = pick(up_all.reshape(width, devices // 2, 2, ff_part), core, 2)
        up_half = up_half.reshape(width, ff_half)
        down_all = lax.all_gather(down_weight, ("head", "blk"), axis=0, tiled=True)
        down_half = pick(down_all.reshape(devices // 2, 2, ff_part, width), core, 1)
        down_half = down_half.reshape(ff_half, width)
        out_weight = lax.all_gather(output_weight, ("head", "blk"), axis=0, tiled=True)
    out_groups = jnp.pad(out_weight.reshape(nh, group, width), ((0, 0), (WIN - group, 0), (0, 0)))
    out_turned = jnp.concatenate([out_groups, out_groups], axis=0)
    out_turned = lax.dynamic_slice_in_dim(out_turned, h, nh, 0).reshape(nh * WIN, width)

    query_pieces = gather_pieces(after(queries, up_half, down_half))

    back = [attended[:rows]]
    for r in range(1, nh):
        back.append(turn(attended[r * rows : (r + 1) * rows], -r))
    joined = jnp.concatenate(back, axis=1)
    tokens_own = tokens.astype(F32)
    middle = tokens_own + (mat(joined, out_turned) + out_bias)
    normed_two, spread_two = norm_parts(middle)
    second_low = (normed_two * gain_two + shift_two).astype(BF16)

    second_pair = jnp.concatenate([second_low, swap(second_low, 1)], axis=0)
    cot_pair = jnp.concatenate([cotangent, cot_other], axis=0)
    hidden = mat(second_pair, up_half) + up_bias_half
    active, slope = gelu_pair(hidden)
    active_low = active.astype(BF16)
    grad_hidden = (mat(cot_pair, down_half, CONTRACT_LAST) * slope).astype(BF16)
    grad_second_part = mat(grad_hidden, up_half, CONTRACT_LAST)
    grad_second = grad_second_part[:rows] + swap(grad_second_part[rows:], 1)
    cot_wide = cotangent.astype(F32)
    grad_middle = cot_wide + norm_pull(grad_second, normed_two, spread_two, gain_two)
    branch_grad = grad_middle.astype(BF16)
    grad_joined = mat(branch_grad, out_turned, CONTRACT_LAST).astype(BF16)
    grad_slots = [grad_joined[:, :WIN]]
    for r in range(1, nh):
        grad_slots.append(turn(grad_joined[:, r * WIN : (r + 1) * WIN], r))

    output_part = mat(active_low, down_half)
    output_sum = output_part[:rows] + swap(output_part[rows:], 1)
    output_rows = (middle + output_sum + down_bias_all).astype(BF16)
    grad_down_half = mat(active_low, cot_pair, CONTRACT_FIRST)
    grad_up_half = mat(second_pair, grad_hidden, CONTRACT_FIRST)
    grad_out_turned = mat(joined, branch_grad, CONTRACT_FIRST)

    grad_attended, stats = delta_rows(wide, log_total, grad_slots)
    grad_pieces = gather_pieces(grad_attended)
    stat_pieces = gather_pieces(stats)
    grad_queries = query_grads(meta, queries, grad_attended, stats, kv_pieces, nh, nb)
    grad_key_values = key_grads(meta, key_values, query_pieces, grad_pieces, stat_pieces, nh, nb)

    grad_out_groups = grad_out_turned.astype(BF16).reshape(nh, WIN, width)[:, WIN - group :]
    grad_out_twice = jnp.concatenate([grad_out_groups, grad_out_groups], axis=0)
    grad_out = lax.dynamic_slice_in_dim(grad_out_twice, lax.rem(nh - h, nh), nh, 0)
    if nb == 8:
        grad_up_half, grad_down_half, grad_out = after(
            (grad_up_half.astype(BF16), grad_down_half.astype(BF16), grad_out),
            *grad_pieces,
            *stat_pieces,
        )
        grad_out = grad_out.reshape(nh, 2, 2, 2, part, width)
        out_sent = swap(pick(grad_out, 1 - core, 3), 1)
        out_chip = pick(grad_out, core, 3).astype(F32) + out_sent.astype(F32)
        low_chip = jnp.concatenate(
            [grad_down_half.reshape(nh, 2, 2, ff_part, width), out_chip.astype(BF16)], axis=3
        )
        low_sum = scatter_chips(low_chip, nh, 4)
        sum_down_w, sum_out_w = low_sum[:ff_part], low_sum[ff_part:]
        up_sum = scatter_chips(grad_up_half.reshape(nh, 2, 2, 2 * part, ff_half), nh, 2)
        up_sum = up_sum.reshape(2, part, ff_half)
        up_got = swap(pick(up_sum, 1 - core, 0), 1)
        up_rows = in_pair(core, pick(up_sum, core, 0), up_got)
        up_rows = up_rows.reshape(2, part, devices // 2, ff_part)
        sum_up_w = up_rows.transpose(1, 2, 0, 3).reshape(part, 2 * ff_half)
    else:
        grad_out = grad_out.reshape(width, width).astype(F32)
        sum_out_w = lax.psum_scatter(grad_out, ("head", "blk"), scatter_dimension=0, tiled=True)
        zero_first = jnp.zeros((width, devices // 2, 2, ff_part), F32)
        up_placed = lax.dynamic_update_slice_in_dim(
            zero_first, grad_up_half.reshape(width, devices // 2, 1, ff_part), core, 2
        ).reshape(width, 2 * ff_half)
        sum_up_w = lax.psum_scatter(up_placed, ("head", "blk"), scatter_dimension=0, tiled=True)
        zero_rows = jnp.zeros((devices // 2, 2, ff_part, width), F32)
        down_placed = lax.dynamic_update_slice_in_dim(
            zero_rows, grad_down_half.reshape(devices // 2, 1, ff_part, width), core, 1
        ).reshape(2 * ff_half, width)
        sum_down_w = lax.psum_scatter(down_placed, ("head", "blk"), scatter_dimension=0, tiled=True)

    grad_q_low = grad_queries[:, :group]
    grad_group = jnp.concatenate([grad_key_values, grad_q_low], axis=1)
    first_part = mat(grad_group, group_weight, CONTRACT_LAST)
    first_low_part = first_part.astype(BF16)
    grad_first = first_part[:rows]
    for r in range(1, nh):
        grad_first = grad_first + turn(first_low_part[r * rows : (r + 1) * rows], -r).astype(F32)
    grad_triple_part = mat(first_low, grad_group, CONTRACT_FIRST)
    triple_slots = scatter_group_rows(grad_triple_part, nh, nb)
    triple_sum = by_group(triple_slots).astype(F32)
    sum_triple = jnp.concatenate(
        [
            triple_sum[:, :, 2 * group :].transpose(1, 0, 2).reshape(part, width),
            triple_sum[:, :, :group].transpose(1, 0, 2).reshape(part, width),
            triple_sum[:, :, group : 2 * group].transpose(1, 0, 2).reshape(part, width),
        ],
        axis=1,
    )
    grad_in = norm_pull(grad_first, normed_one[:rows], spread_one[:rows], gain_one)
    input_grad = (grad_middle + grad_in).astype(BF16)

    group_sums = jnp.sum(grad_group.astype(F32), axis=0)
    placed = jnp.zeros((2, nh, group), F32)
    placed = lax.dynamic_update_slice_in_dim(
        placed,
        jnp.stack([group_sums[2 * group :], group_sums[group : 2 * group]])[:, None],
        h,
        1,
    ).reshape(2, width)
    up_b = jnp.sum(grad_hidden.astype(F32), axis=0).reshape(devices // 2, 1, 4, part)
    up_b = lax.dynamic_update_slice_in_dim(
        jnp.zeros((devices // 2, 2, 4, part), F32), up_b, core, 1
    ).reshape(devices, 4, part)
    sums = jnp.stack(
        [
            jnp.sum(first_part * normed_one, axis=0),
            jnp.sum(first_part, axis=0),
            placed[0],
            placed[1],
            jnp.sum(branch_grad.astype(F32), axis=0),
            jnp.sum(grad_second * normed_two, axis=0),
            jnp.sum(grad_second, axis=0),
            jnp.sum(cot_wide, axis=0),
        ]
    )
    sums = jnp.concatenate([sums.reshape(8, devices, part).transpose(1, 0, 2), up_b], axis=1)
    sums = lax.all_to_all(sums, ("head", "blk"), 0, 0, tiled=True)
    sums = jnp.sum(sums, axis=0)
    return (
        output_rows,
        input_grad,
        sums[0],
        sums[1],
        sum_triple,
        sums[2],
        sums[3],
        sum_out_w,
        sums[4],
        sums[5],
        sums[6],
        sum_up_w,
        sums[8:].reshape(ff_part),
        sum_down_w,
        sums[7],
    )


def solution(mesh):
    wide = P(("head", "blk"), None)
    thin = P(("head", "blk"))
    in_specs = (
        wide,
        wide,
        P(),
        thin,
        thin,
        wide,
        thin,
        thin,
        wide,
        thin,
        thin,
        thin,
        wide,
        thin,
        wide,
        thin,
    )
    out_specs = (
        wide,
        wide,
        thin,
        thin,
        wide,
        thin,
        thin,
        wide,
        thin,
        thin,
        thin,
        wide,
        thin,
        wide,
        thin,
    )
    return jax.shard_map(shards, mesh=mesh, in_specs=in_specs, out_specs=out_specs, check_vma=False)
```

```python
import functools

import jax
import jax.numpy as jnp
from jax import lax
from jax.experimental import pallas as pl
from jax.experimental.pallas import tpu as pltpu
from jax.sharding import PartitionSpec as P

HEADS = 12
HEAD_DIM = 64

epsilon = 1e-06
neg_fill = -1e30
root_half = 0.7071067811865476
inv_root_two_pi = 0.3989422804014327

F32 = jnp.float32
BF16 = jnp.bfloat16
WIN = 256
TILE_BLOCKS = 4
CONTRACT_LAST = (((1,), (1,)), ((), ()))
CONTRACT_FIRST = (((0,), (0,)), ((), ()))
PLAIN = (((1,), (0,)), ((), ()))


def norm_parts(values):
    centre = jnp.mean(values, axis=-1, keepdims=True)
    offset = values - centre
    inv_spread = lax.rsqrt(jnp.mean(offset * offset, axis=-1, keepdims=True) + epsilon)
    return (offset * inv_spread, inv_spread)


def norm_pull(grad_out, normed, inv_spread, gain_full):
    grad_normed = grad_out * gain_full
    return inv_spread * (
        grad_normed
        - jnp.mean(grad_normed, axis=-1, keepdims=True)
        - normed * jnp.mean(grad_normed * normed, axis=-1, keepdims=True)
    )


def gelu_pair(hidden):
    normal_cdf = 0.5 * (1.0 + lax.erf(hidden * root_half))
    return (
        hidden * normal_cdf,
        normal_cdf + hidden * inv_root_two_pi * jnp.exp(-0.5 * hidden * hidden),
    )


def mat(left, right, dims=PLAIN):
    return lax.dot_general(left, right, dims, preferred_element_type=F32)


def exchange(x):
    return lax.all_to_all(x, "head", 0, 0, tiled=True)


def share(x):
    return exchange(jnp.broadcast_to(x[None], (lax.axis_size("head"),) + x.shape))


def turn(x, step):
    size = lax.axis_size("head")
    return lax.ppermute(x, "head", [(i, (i + step) % size) for i in range(size)])


def by_group(slots):
    size = len(slots)
    doubled = jnp.stack([slots[i % size] for i in range(2 * size - 1)])
    start = lax.rem(size - lax.axis_index("head"), size)
    return lax.dynamic_slice_in_dim(doubled, start, size, 0)


def swap(x, bits):
    size = lax.axis_size("blk")
    return lax.ppermute(x, "blk", [(i, i ^ bits) for i in range(size)])


def in_pair(bit, mine, other):
    return jnp.where(bit == 0, jnp.stack([mine, other]), jnp.stack([other, mine]))


def pick(x, index, axis):
    return lax.dynamic_index_in_dim(x, index, axis, keepdims=False)


def after(value, *earlier):
    flat, tree = jax.tree.flatten(value)
    held = lax.optimization_barrier((tuple(flat), earlier))[0]
    return jax.tree.unflatten(tree, held)


def gather_pieces(x, *earlier):
    if lax.axis_size("blk") != 8:
        return [lax.all_gather(x, "blk", axis=0, tiled=False)]
    pieces = [None] * 8
    pieces[0] = x
    for bits in (2, 4, 6):
        pieces[bits] = swap(x, bits)
    for bits in (0, 2, 4, 6):
        pieces[bits + 1] = swap(after(pieces[bits], *earlier) if bits else x, 1)
    return pieces


def doc_range(meta, first, last, total):
    low, high = jnp.int32(0), jnp.int32(total)
    for i in range(meta.shape[0] - 1):
        start = meta[1 + i]
        low = jnp.where(start <= first, start, low)
        high = jnp.where(start > last, jnp.minimum(high, start), high)
    return low, high


def row_ranges(meta, first, rows, total):
    place = first + lax.broadcasted_iota(jnp.int32, (rows, 1), 0)
    low = jnp.zeros((rows, 1), jnp.int32)
    high = jnp.full((rows, 1), total, jnp.int32)
    for i in range(meta.shape[0] - 1):
        start = meta[1 + i]
        low = jnp.where(place >= start, start, low)
        high = jnp.where(place < start, jnp.minimum(high, start), high)
    return low, high


def head_rows(width, shift, scale):
    lane = lax.broadcasted_iota(jnp.int32, (1, width), 1)
    return [
        jnp.where((lane >= shift + 64 * i) & (lane < shift + 64 * (i + 1)), scale, 0.0).astype(F32)
        for i in range(3)
    ]


def spread_heads(block, rows):
    wide = block.astype(F32)
    return jnp.concatenate([wide * row for row in rows], axis=0).astype(BF16)


def fold_heads(stack, rows):
    return stack[0] * rows[0] + stack[1] * rows[1] + stack[2] * rows[2]


def block_copies(meta, nh, nb, pieces, place, sems):
    b = meta[0]
    copies = []
    if len(pieces) == nb:
        for m, piece in enumerate(pieces):
            for r in range(nh):
                block = r * nb + jnp.bitwise_xor(b, m)
                copies.append(pltpu.make_async_copy(*place(piece, None, r, block), sems.at[m, r]))
        for copy in copies:
            copy.start()
        return copies

    def run(which):
        def one(i, carry):
            for r in range(nh):
                block = r * nb + i
                copy = pltpu.make_async_copy(*place(pieces[0], i, r, block), sems.at[i, r])
                (copy.start if which == 0 else copy.wait)()
            return carry

        lax.fori_loop(0, nb, one, 0)

    run(0)

    class Rest:
        def wait(self):
            run(1)

    return [Rest()]


def row_place(target, rows):
    def place(piece, index, r, block):
        source = piece if index is None else piece.at[index]
        return source.at[pl.ds(r * rows, rows), :], target.at[block]

    return place


def tile_bounds(meta, first, rows, total):
    low, high = doc_range(meta, first, first + rows - 1, total)
    tile = TILE_BLOCKS * rows
    return lax.div(low, tile), lax.div(high + tile - 1, tile)


def lane_is(index):
    lane = lax.broadcasted_iota(jnp.int32, (1, 128), 1)
    return jnp.where(lane == index, 1.0, 0.0).astype(F32)


def in_lanes(columns):
    total = columns[0] * lane_is(0)
    for i in range(1, len(columns)):
        total = total + columns[i] * lane_is(i)
    return total


def three_parts(column):
    high = column.astype(BF16).astype(F32)
    middle = (column - high).astype(BF16).astype(F32)
    return [high, middle, (column - high - middle).astype(BF16).astype(F32)]


def add_parts(block, index):
    lane = 3 * index
    return block[:, lane : lane + 1] + block[:, lane + 1 : lane + 2] + block[:, lane + 2 : lane + 3]


def forward_kernel(nh, nb, count, meta, q_ref, *rest):
    pieces, (wide_ref, low_ref), (kv, sems) = rest[:count], rest[count : count + 2], rest[count + 2 :]
    rows = q_ref.shape[0] // nh
    total = nh * nb * rows
    tile = TILE_BLOCKS * rows
    b = meta[0]
    for copy in block_copies(meta, nh, nb, pieces, row_place(kv, rows), sems):
        copy.wait()
    query_rows = head_rows(WIN, 0, HEAD_DIM**-0.5)
    value_rows = head_rows(WIN, 64, 1.0)

    def one_block(r):
        first = (r * nb + b) * rows
        tile_low, tile_high = tile_bounds(meta, first, rows, total)
        low, high = row_ranges(meta, first, rows, total)
        masked = spread_heads(q_ref[r * rows : (r + 1) * rows, :], query_rows)

        def step(t, state):
            top, norm, out = state
            keys = kv[pl.ds(t * TILE_BLOCKS, TILE_BLOCKS), :, 0:WIN].reshape(tile, WIN)
            values = kv[pl.ds(t * TILE_BLOCKS, TILE_BLOCKS), :, 128 : 128 + WIN].reshape(tile, WIN)
            place = t * tile + lax.broadcasted_iota(jnp.int32, (1, tile), 1)
            allowed = (place >= low) & (place < high)
            scores = mat(masked, keys, CONTRACT_LAST).reshape(3, rows, tile)
            scores = jnp.where(allowed[None], scores, neg_fill)
            new_top = jnp.maximum(top, jnp.max(scores, axis=-1, keepdims=True))
            weights = jnp.exp(scores - new_top)
            factor = jnp.exp(top - new_top)
            norm = norm * factor + jnp.sum(weights, axis=-1, keepdims=True)
            part = mat(weights.astype(BF16).reshape(3 * rows, tile), values)
            return new_top, norm, out * factor + part.reshape(3, rows, WIN)

        top, norm, out = lax.fori_loop(
            tile_low,
            tile_high,
            step,
            (
                jnp.full((3, rows, 1), neg_fill, F32),
                jnp.zeros((3, rows, 1), F32),
                jnp.zeros((3, rows, WIN), F32),
            ),
        )
        attended = fold_heads(out / norm, value_rows)
        log_total = top + jnp.log(norm)
        extra = in_lanes([log_total[i] for i in range(3)])
        wide_ref[r * rows : (r + 1) * rows, 0:128] = attended[:, 0:128] + extra
        wide_ref[r * rows : (r + 1) * rows, 128:256] = attended[:, 128:256]
        return attended

    half = nh // 2
    for r in range(half):
        left = pltpu.roll(one_block(r), WIN - 64, axis=1)
        right = one_block(r + half)
        span = slice(r * rows, (r + 1) * rows)
        for i in range(nh):
            low_ref[i, span, 0:128] = left[:, 0:128].astype(BF16)
            low_ref[i, span, 128:256] = (left[:, 128:256] + right[:, 0:128]).astype(BF16)
            low_ref[i, span, 256:384] = right[:, 128:256].astype(BF16)


def delta_kernel(nh, wide_ref, g_ref, grad_ref):
    rows = wide_ref.shape[0] // nh
    half = nh // 2
    value_rows = head_rows(WIN, 64, 1.0)
    every = value_rows[0] + value_rows[1] + value_rows[2]

    def one_block(r, grad):
        span = slice(r * rows, (r + 1) * rows)
        grad = (grad * every).astype(BF16).astype(F32)
        wide = wide_ref[span, :]
        product = grad * wide
        parts = []
        for i in range(3):
            parts += three_parts(wide[:, i : i + 1])
        for i in range(3):
            parts += three_parts(jnp.sum(product * value_rows[i], axis=-1, keepdims=True))
        grad_ref[span, 0:128] = (grad[:, 0:128] + in_lanes(parts)).astype(BF16)
        grad_ref[span, 128:256] = grad[:, 128:256].astype(BF16)

    for r in range(half):
        total = g_ref[0, r * rows : (r + 1) * rows, :].astype(F32)
        for i in range(1, nh):
            total = total + g_ref[i, r * rows : (r + 1) * rows, :].astype(F32)
        one_block(r, pltpu.roll(total[:, 0:WIN], 64, axis=1))
        one_block(r + half, total[:, 128 : 128 + WIN])


def query_kernel(nh, nb, count, meta, q_ref, g_ref, *rest):
    pieces, out_ref, (kv, sems) = rest[:count], rest[count], rest[count + 1 :]
    rows = q_ref.shape[0] // nh
    total = nh * nb * rows
    tile = TILE_BLOCKS * rows
    b = meta[0]
    for copy in block_copies(meta, nh, nb, pieces, row_place(kv, rows), sems):
        copy.wait()
    query_rows = head_rows(WIN, 0, HEAD_DIM**-0.5)
    value_rows = head_rows(WIN, 64, 1.0)
    for r in range(nh):
        span = slice(r * rows, (r + 1) * rows)
        first = (r * nb + b) * rows
        tile_low, tile_high = tile_bounds(meta, first, rows, total)
        low, high = row_ranges(meta, first, rows, total)
        masked = spread_heads(q_ref[span, :], query_rows)
        grads = spread_heads(g_ref[span, :], value_rows)
        stats = g_ref[span, 0:128].astype(F32)
        log_total = jnp.stack([add_parts(stats, i) for i in range(3)])
        delta = jnp.stack([add_parts(stats, 3 + i) for i in range(3)])

        def step(t, state):
            keys = kv[pl.ds(t * TILE_BLOCKS, TILE_BLOCKS), :, 0:WIN].reshape(tile, WIN)
            values = kv[pl.ds(t * TILE_BLOCKS, TILE_BLOCKS), :, 128 : 128 + WIN].reshape(tile, WIN)
            place = t * tile + lax.broadcasted_iota(jnp.int32, (1, tile), 1)
            allowed = (place >= low) & (place < high)
            scores = mat(masked, keys, CONTRACT_LAST).reshape(3, rows, tile)
            probs = jnp.exp(jnp.where(allowed[None], scores, neg_fill) - log_total)
            grad_probs = mat(grads, values, CONTRACT_LAST).reshape(3, rows, tile)
            grad_scores = (probs * (grad_probs - delta)).astype(BF16)
            part = mat(grad_scores.reshape(3 * rows, tile), keys)
            return state + part.reshape(3, rows, WIN)

        total_grad = lax.fori_loop(tile_low, tile_high, step, jnp.zeros((3, rows, WIN), F32))
        out_ref[span, :] = fold_heads(total_grad, query_rows).astype(BF16)


def key_kernel(nh, nb, counts, meta, kv_ref, *rest):
    both = counts[0] + counts[1]
    q_in, g_in, out_ref = rest[: counts[0]], rest[counts[0] : both], rest[both]
    queries_all, grads_all, q_sems, g_sems = rest[both + 1 :]
    rows = kv_ref.shape[0] // nh
    total = nh * nb * rows
    tile = TILE_BLOCKS * rows
    b = meta[0]
    copies = block_copies(meta, nh, nb, q_in, row_place(queries_all, rows), q_sems)
    copies += block_copies(meta, nh, nb, g_in, row_place(grads_all, rows), g_sems)
    for copy in copies:
        copy.wait()
    key_rows = head_rows(WIN, 0, HEAD_DIM**-0.5)
    value_rows = head_rows(WIN, 64, 1.0)
    line = lax.broadcasted_iota(jnp.int32, (8, WIN), 0) * 3
    lane = lax.broadcasted_iota(jnp.int32, (8, WIN), 1)
    choose = jnp.where((lane >= line) & (lane < line + 3), 1.0, 0.0).astype(BF16)
    for r in range(nh):
        span = slice(r * rows, (r + 1) * rows)
        first = (r * nb + b) * rows
        tile_low, tile_high = tile_bounds(meta, first, rows, total)
        low, high = row_ranges(meta, first, rows, total)
        keys = spread_heads(kv_ref[span, 0:WIN], key_rows)
        values = spread_heads(kv_ref[span, 128 : 128 + WIN], value_rows)

        def step(t, state):
            grad_keys, grad_values = state
            queries = queries_all[pl.ds(t * TILE_BLOCKS, TILE_BLOCKS)].reshape(tile, WIN)
            grads = grads_all[pl.ds(t * TILE_BLOCKS, TILE_BLOCKS)].reshape(tile, WIN)
            stats = mat(choose, grads, CONTRACT_LAST)
            log_total = jnp.stack([stats[i : i + 1] for i in range(3)])
            delta = jnp.stack([stats[3 + i : 4 + i] for i in range(3)])
            place = t * tile + lax.broadcasted_iota(jnp.int32, (1, tile), 1)
            allowed = (place >= low) & (place < high)
            scores = mat(keys, queries, CONTRACT_LAST).reshape(3, rows, tile)
            probs = jnp.exp(jnp.where(allowed[None], scores, neg_fill) - log_total)
            grad_probs = mat(values, grads, CONTRACT_LAST).reshape(3, rows, tile)
            grad_scores = (probs * (grad_probs - delta)).astype(BF16)
            part_value = mat(probs.astype(BF16).reshape(3 * rows, tile), grads)
            part_key = mat(grad_scores.reshape(3 * rows, tile), queries)
            return (
                grad_keys + part_key.reshape(3, rows, WIN),
                grad_values + part_value.reshape(3, rows, WIN),
            )

        zero = jnp.zeros((3, rows, WIN), F32)
        grad_keys, grad_values = lax.fori_loop(tile_low, tile_high, step, (zero, zero))
        key_out = fold_heads(grad_keys, key_rows)
        value_out = fold_heads(grad_values, value_rows)
        out_ref[span, 0:128] = key_out[:, 0:128].astype(BF16)
        out_ref[span, 128:256] = (key_out[:, 128:256] + value_out[:, 0:128]).astype(BF16)
        out_ref[span, 256:384] = value_out[:, 128:256].astype(BF16)


SMEM_SPEC = pl.BlockSpec(memory_space=pltpu.SMEM)
VMEM_SPEC = pl.BlockSpec(memory_space=pltpu.VMEM)
ANY_SPEC = pl.BlockSpec(memory_space=pl.ANY)


def kernel_params():
    return pltpu.CompilerParams(vmem_limit_bytes=56 * 1024 * 1024)


def cost(matmuls, nh, nb, rows):
    flops = matmuls * 2 * 3 * rows * WIN * 32 * TILE_BLOCKS * rows * nh // 4 * 2
    return pl.CostEstimate(flops=flops, bytes_accessed=nh * nb * rows * 384 * 2, transcendentals=0)


def attend(meta, queries, pieces, nh, nb):
    length = queries.shape[0]
    rows = length // nh
    count = len(pieces)
    return pl.pallas_call(
        functools.partial(forward_kernel, nh, nb, count),
        out_shape=(
            jax.ShapeDtypeStruct((length, WIN), F32),
            jax.ShapeDtypeStruct((nh, length // 2, 384), BF16),
        ),
        in_specs=[SMEM_SPEC, VMEM_SPEC] + [ANY_SPEC] * count,
        out_specs=(VMEM_SPEC,) * 2,
        scratch_shapes=[
            pltpu.VMEM((nh * nb, rows, 384), BF16),
            pltpu.SemaphoreType.DMA((nb, nh)),
        ],
        compiler_params=kernel_params(),
        cost_estimate=cost(2, nh, nb, rows),
        name="attend",
    )(meta, queries, *pieces)


def delta_rows(wide, grads, nh):
    return pl.pallas_call(
        functools.partial(delta_kernel, nh),
        out_shape=jax.ShapeDtypeStruct(wide.shape, BF16),
        in_specs=[VMEM_SPEC] * 2,
        out_specs=VMEM_SPEC,
        compiler_params=kernel_params(),
        name="delta",
    )(wide, grads)


def query_grads(meta, queries, grads, pieces, nh, nb):
    length = queries.shape[0]
    rows = length // nh
    count = len(pieces)
    return pl.pallas_call(
        functools.partial(query_kernel, nh, nb, count),
        out_shape=jax.ShapeDtypeStruct((length, WIN), BF16),
        in_specs=[SMEM_SPEC] + [VMEM_SPEC] * 2 + [ANY_SPEC] * count,
        out_specs=VMEM_SPEC,
        scratch_shapes=[
            pltpu.VMEM((nh * nb, rows, 384), BF16),
            pltpu.SemaphoreType.DMA((nb, nh)),
        ],
        compiler_params=kernel_params(),
        cost_estimate=cost(3, nh, nb, rows),
        name="query_grads",
    )(meta, queries, grads, *pieces)


def key_grads(meta, own, queries, grads, nh, nb):
    length = own.shape[0]
    rows = length // nh
    counts = (len(queries), len(grads))
    return pl.pallas_call(
        functools.partial(key_kernel, nh, nb, counts),
        out_shape=jax.ShapeDtypeStruct((length, 384), BF16),
        in_specs=[SMEM_SPEC, VMEM_SPEC] + [ANY_SPEC] * sum(counts),
        out_specs=VMEM_SPEC,
        scratch_shapes=[
            pltpu.VMEM((nh * nb, rows, WIN), BF16),
            pltpu.VMEM((nh * nb, rows, WIN), BF16),
            pltpu.SemaphoreType.DMA((nb, nh)),
            pltpu.SemaphoreType.DMA((nb, nh)),
        ],
        compiler_params=kernel_params(),
        cost_estimate=cost(4, nh, nb, rows),
        name="key_grads",
    )(meta, own, *queries, *grads)


def gather_blk_rows(here):
    if lax.axis_size("blk") != 8:
        whole = lax.all_gather(here, "blk", axis=0, tiled=False)
        return jnp.moveaxis(whole, 0, 1).reshape(-1, here.shape[-1])
    b = lax.axis_index("blk")
    core, x_bit, y_bit = b & 1, (b >> 1) & 1, b >> 2
    side, up, cross = swap(here, 2), swap(here, 4), swap(here, 6)
    square = in_pair(y_bit, in_pair(x_bit, here, side), in_pair(x_bit, up, cross))
    whole = in_pair(core, square, swap(square, 1))
    return whole.transpose(3, 1, 2, 0, 4, 5).reshape(-1, here.shape[-1])


def scatter_blk_rows(grad, nh, nb):
    width = grad.shape[-1]
    if nb != 8:
        parts = grad.reshape(nh, nb, -1, width)
        return lax.psum_scatter(parts, "blk", scatter_dimension=1, tiled=False).astype(BF16)
    b = lax.axis_index("blk")
    core, x_bit, y_bit = b & 1, (b >> 1) & 1, b >> 2
    parts = grad.astype(BF16).reshape(nh, 2, 2, 2, -1, width)
    sent = swap(pick(parts, 1 - core, 3), 1)
    chip = (pick(parts, core, 3).astype(F32) + sent.astype(F32)).astype(BF16)

    def part(y, x):
        return pick(pick(chip, y, 1), x, 1)

    side = swap(part(y_bit, 1 - x_bit), 2)
    up = swap(part(1 - y_bit, x_bit), 4)
    cross = swap(part(1 - y_bit, 1 - x_bit), 6)
    mine = part(y_bit, x_bit).astype(F32) + side.astype(F32)
    return (mine + up.astype(F32) + cross.astype(F32)).astype(BF16)


def shards(
    tokens,
    cotangent,
    doc_starts,
    norm_gain,
    norm_shift,
    triple_weight,
    query_bias,
    value_bias,
    output_weight,
    output_bias,
    final_gain,
    final_shift,
    up_weight,
    up_bias,
    down_weight,
    down_bias,
):
    nh = lax.axis_size("head")
    nb = lax.axis_size("blk")
    h = lax.axis_index("head")
    b = lax.axis_index("blk")
    rows, width = tokens.shape
    part = norm_gain.shape[0]
    group = HEADS // nh * HEAD_DIM
    ff_part = up_bias.shape[0]
    ff_group = nb * ff_part
    extra = max(part, 12)
    meta = jnp.concatenate([b.astype(jnp.int32)[None], doc_starts])

    packed = jnp.stack(
        [
            norm_gain,
            norm_shift,
            query_bias,
            value_bias,
            output_bias,
            final_gain,
            final_shift,
            down_bias,
        ]
    )
    packed = jnp.concatenate([packed, up_bias.reshape(4, part)], axis=0)
    if extra > 12:
        packed = jnp.pad(packed, ((0, extra - 12), (0, 0)))
    columns = triple_weight.reshape(part, 3, nh, group)
    pieces = [columns[:, 1], columns[:, 2], columns[:, 0]]
    if part == extra:
        pieces.append(jnp.broadcast_to(packed[:, None], (part, nh, part)))
    pieces.append(up_weight.reshape(part, nh, ff_group))
    pieces.append(jnp.broadcast_to(output_weight[:, None], (part, nh, width)))
    columns = exchange(jnp.concatenate(pieces, axis=-1).transpose(1, 0, 2))
    token_rows = share(after(tokens, columns)).reshape(nh * rows, width)
    first_width = 3 * group + (part if part == extra else 0)
    group_weight = gather_blk_rows(columns[..., :first_width])

    late = jnp.concatenate(
        [
            columns[..., first_width : first_width + ff_group].reshape(-1, ff_group),
            down_weight,
            columns[..., first_width + ff_group :].reshape(-1, width),
        ],
        axis=0,
    )
    if part == extra:
        vectors = group_weight[:, 3 * group :].reshape(nh * nb, extra, part)[:, :12]
    else:
        vectors = lax.all_gather(packed, ("head", "blk"), axis=0, tiled=False)
    group_weight = group_weight[:, : 3 * group]
    lines = vectors[:, :8].transpose(1, 0, 2).reshape(8, width).astype(F32)
    gain_one, shift_one, query_all, value_all, out_bias, gain_two, shift_two, down_bias_all = (
        lines[i] for i in range(8)
    )
    up_bias_own = pick(vectors[:, 8:].reshape(nh, nb * ff_part), h, 0).astype(F32)

    key_value_weight = group_weight[:, : 2 * group]
    query_weight = jnp.pad(group_weight[:, 2 * group :], ((0, 0), (0, WIN - group)))
    token_wide = token_rows.astype(F32)
    normed_one, spread_one = norm_parts(token_wide)
    first_low = (normed_one * gain_one + shift_one).astype(BF16)
    value_bias_own = lax.dynamic_slice_in_dim(value_all, h * group, group)
    query_bias_own = lax.dynamic_slice_in_dim(query_all, h * group, group)
    kv_bias = jnp.concatenate([jnp.zeros((group,), F32), value_bias_own])
    key_values = (mat(first_low, key_value_weight) + kv_bias).astype(BF16)
    kv_pieces = gather_pieces(key_values)
    q_bias = jnp.pad(query_bias_own, (0, WIN - group))
    queries = (mat(first_low, query_weight) + q_bias).astype(BF16)
    late = lax.all_gather(after(late, *kv_pieces), "blk", axis=0, tiled=False)
    up_own = jnp.moveaxis(late[:, : nh * part].reshape(nb, nh, part, ff_group), 0, 1)
    up_own = up_own.reshape(width, ff_group)
    down_own = late[:, nh * part : nh * part + ff_part].reshape(ff_group, width)
    out_own = jnp.moveaxis(late[:, nh * part + ff_part :].reshape(nb, nh, part, width), 0, 1)
    out_own = out_own.reshape(width, width)
    slow = jnp.concatenate([cotangent, jnp.zeros((rows // 8 * 3, width), BF16)], axis=0)
    slow = lax.all_gather(after(slow, token_rows), "head", axis=0, tiled=False)
    cot_all = slow[:, :rows].reshape(nh * rows, width)
    wide, attended = attend(meta, queries, kv_pieces, nh, nb)
    query_pieces = [lax.all_gather(after(queries, attended), "blk", axis=0, tiled=False)]

    both = exchange(attended).reshape(nh, nh // 2 * rows, 2, group)
    joined = both.transpose(2, 1, 0, 3).reshape(nh * rows, width)
    middle = token_wide + (mat(joined, out_own) + out_bias)
    normed_two, spread_two = norm_parts(middle)
    second_low = (normed_two * gain_two + shift_two).astype(BF16)

    hidden = mat(second_low, up_own) + up_bias_own
    active, slope = gelu_pair(hidden)
    active_low = active.astype(BF16)
    grad_hidden = (mat(cot_all, down_own, CONTRACT_LAST) * slope).astype(BF16)
    grad_second = mat(grad_hidden, up_own, CONTRACT_LAST)
    is_own = jnp.repeat(jnp.arange(nh) == h, rows)[:, None]
    cot_part = jnp.where(is_own, cot_all, jnp.zeros((), BF16)).astype(F32)
    grad_middle = cot_part + norm_pull(grad_second, normed_two, spread_two, gain_two)
    branch_grad = grad_middle.astype(BF16)
    grad_joined = mat(branch_grad, out_own, CONTRACT_LAST).astype(BF16)
    grad_here = grad_joined.reshape(2, nh // 2 * rows, nh, group).transpose(2, 1, 0, 3)
    grad_here = exchange(grad_here.reshape(nh, nh // 2 * rows, 2 * group))

    active_low, cot_late, second_late, grad_hidden, branch_late, joined_late = after(
        (active_low, cot_all, second_low, grad_hidden, branch_grad, joined), grad_joined
    )
    output_part = mat(active_low, down_own).astype(BF16).reshape(nh, rows, width)
    grad_up_own = mat(second_late, grad_hidden, CONTRACT_FIRST).astype(BF16)
    grad_down_own = mat(active_low, cot_late, CONTRACT_FIRST).astype(BF16)
    grad_out = mat(joined_late, branch_late, CONTRACT_FIRST).astype(BF16).reshape(nh, nb, part, width)
    late_grads = jnp.concatenate(
        [
            jnp.moveaxis(grad_up_own.reshape(nh, nb, part, ff_group), 0, 1).reshape(nb, -1, width),
            grad_down_own.reshape(nb, ff_part, width),
            jnp.moveaxis(grad_out, 0, 1).reshape(nb, -1, width),
        ],
        axis=1,
    )
    late_sums = lax.psum_scatter(late_grads, "blk", scatter_dimension=0, tiled=False)

    grad_attended = delta_rows(wide, after(grad_here, late_grads, output_part), nh)
    grad_queries = query_grads(meta, queries, grad_attended, kv_pieces, nh, nb)
    grad_pieces = gather_pieces(grad_attended, grad_queries)
    grad_key_values = key_grads(meta, key_values, query_pieces, grad_pieces, nh, nb)

    grad_group = jnp.concatenate([grad_key_values, grad_queries[:, :group]], axis=1)
    grad_group, late_sums = after((grad_group, late_sums))
    sum_down_w = late_sums[nh * part : nh * part + ff_part].astype(F32)
    first_part = mat(grad_group, group_weight, CONTRACT_LAST)
    grad_in = grad_middle + norm_pull(first_part, normed_one, spread_one, gain_one)
    grad_in = grad_in.astype(BF16).reshape(nh, rows, width)
    both = jnp.concatenate([grad_in, output_part], axis=1)
    both = lax.psum_scatter(both, "head", scatter_dimension=0, tiled=False)
    input_grad = both[:rows].astype(BF16)
    output_own = pick(middle.reshape(nh, rows, width), h, 0)
    output_rows = (output_own + both[rows:].astype(F32) + down_bias_all).astype(BF16)
    first_late, grad_group = after((first_low, grad_group), grad_in)
    grad_triple_part = mat(first_late, grad_group, CONTRACT_FIRST).astype(BF16)

    group_sums = jnp.sum(grad_group.astype(F32), axis=0)
    placed = jnp.where(
        jnp.arange(nh)[None, :, None] == h,
        jnp.stack([group_sums[2 * group :], group_sums[group : 2 * group]])[:, None],
        0.0,
    ).reshape(2, width)
    up_b = jnp.sum(grad_hidden.astype(F32), axis=0)
    up_b = jnp.where(jnp.arange(nh)[:, None] == h, up_b[None], 0.0).reshape(nh * nb, 4, part)
    sums = jnp.stack(
        [
            jnp.sum(first_part * normed_one, axis=0),
            jnp.sum(first_part, axis=0),
            placed[0],
            placed[1],
            jnp.sum(branch_grad.astype(F32), axis=0),
            jnp.sum(grad_second * normed_two, axis=0),
            jnp.sum(grad_second, axis=0),
            jnp.sum(cotangent.astype(F32), axis=0),
        ]
    )
    sums = sums.reshape(8, nh * nb, part).transpose(1, 0, 2)
    sums = jnp.concatenate([sums, up_b], axis=1)
    if part == extra:
        low_sums = jnp.pad(sums.astype(BF16), ((0, 0), (0, extra - 12), (0, 0)))
        low_sums = low_sums.reshape(width, part)
        here = scatter_blk_rows(jnp.concatenate([grad_triple_part, low_sums], axis=1), nh, nb)
    else:
        sums = lax.psum(sums, ("head", "blk"))
        sums = pick(sums, h * nb + b, 0)
        here = scatter_blk_rows(grad_triple_part, nh, nb)
    final = [
        here,
        late_sums[: nh * part].reshape(nh, part, ff_group),
        late_sums[nh * part + ff_part :].reshape(nh, part, width),
    ]
    final = jnp.concatenate(final, axis=-1)
    slots = [pick(final, h, 0)]
    for r in range(1, nh):
        slots.append(turn(pick(final, lax.rem(h - r + nh, nh), 0), -r))
    final = by_group(slots).astype(F32)
    if part == extra:
        sums = jnp.sum(final[:, :12, 3 * group : first_width], axis=0)
    sum_triple = jnp.concatenate(
        [
            final[:, :, 2 * group : 3 * group].transpose(1, 0, 2).reshape(part, width),
            final[:, :, :group].transpose(1, 0, 2).reshape(part, width),
            final[:, :, group : 2 * group].transpose(1, 0, 2).reshape(part, width),
        ],
        axis=1,
    )
    sum_up_w = final[:, :, first_width : first_width + ff_group]
    sum_up_w = sum_up_w.transpose(1, 0, 2).reshape(part, nh * ff_group)
    sum_out_w = jnp.sum(final[:, :, first_width + ff_group :], axis=0)
    return (
        output_rows,
        input_grad,
        sums[0],
        sums[1],
        sum_triple,
        sums[2],
        sums[3],
        sum_out_w,
        sums[4],
        sums[5],
        sums[6],
        sum_up_w,
        sums[8:].reshape(ff_part),
        sum_down_w,
        sums[7],
    )


def solution(mesh):
    wide = P(("head", "blk"), None)
    thin = P(("head", "blk"))
    in_specs = (
        wide,
        wide,
        P(),
        thin,
        thin,
        wide,
        thin,
        thin,
        wide,
        thin,
        thin,
        thin,
        wide,
        thin,
        wide,
        thin,
    )
    out_specs = (
        wide,
        wide,
        thin,
        thin,
        wide,
        thin,
        thin,
        wide,
        thin,
        thin,
        thin,
        wide,
        thin,
        wide,
        thin,
    )
    return jax.shard_map(shards, mesh=mesh, in_specs=in_specs, out_specs=out_specs, check_vma=False)
```

```python
import functools

import jax
import jax.numpy as jnp
from jax import lax
from jax.experimental import pallas as pl
from jax.experimental.pallas import tpu as pltpu
from jax.sharding import PartitionSpec as P

HEADS = 12
HEAD_DIM = 64

epsilon = 1e-06
neg_fill = -1e30
root_half = 0.7071067811865476
inv_root_two_pi = 0.3989422804014327

F32 = jnp.float32
BF16 = jnp.bfloat16
WIN = 256
TILE_BLOCKS = 6
TILE_PARTS = ((0, 4), (4, 2))
CONTRACT_LAST = (((1,), (1,)), ((), ()))
CONTRACT_FIRST = (((0,), (0,)), ((), ()))
PLAIN = (((1,), (0,)), ((), ()))


def norm_parts(values):
    centre = jnp.mean(values, axis=-1, keepdims=True)
    offset = values - centre
    inv_spread = lax.rsqrt(jnp.mean(offset * offset, axis=-1, keepdims=True) + epsilon)
    return (offset * inv_spread, inv_spread)


def norm_pull(grad_out, normed, inv_spread, gain_full):
    grad_normed = grad_out * gain_full
    return inv_spread * (
        grad_normed
        - jnp.mean(grad_normed, axis=-1, keepdims=True)
        - normed * jnp.mean(grad_normed * normed, axis=-1, keepdims=True)
    )


def gelu_pair(hidden):
    normal_cdf = 0.5 * (1.0 + lax.erf(hidden * root_half))
    return (
        hidden * normal_cdf,
        normal_cdf + hidden * inv_root_two_pi * jnp.exp(-0.5 * hidden * hidden),
    )


def mat(left, right, dims=PLAIN):
    return lax.dot_general(left, right, dims, preferred_element_type=F32)


def exchange(x):
    return lax.all_to_all(x, "head", 0, 0, tiled=True)


def share(x):
    return exchange(jnp.broadcast_to(x[None], (lax.axis_size("head"),) + x.shape))


def turn(x, step):
    size = lax.axis_size("head")
    return lax.ppermute(x, "head", [(i, (i + step) % size) for i in range(size)])


def by_head(slots):
    size = len(slots)
    doubled = jnp.stack([slots[(size - 1 - i) % size] for i in range(2 * size - 1)])
    return lax.dynamic_slice_in_dim(doubled, size - 1 - lax.axis_index("head"), size, 0)


def spread(x):
    return by_head([x] + [turn(x, r) for r in range(1, lax.axis_size("head"))])


def by_group(slots):
    size = len(slots)
    doubled = jnp.stack([slots[i % size] for i in range(2 * size - 1)])
    start = lax.rem(size - lax.axis_index("head"), size)
    return lax.dynamic_slice_in_dim(doubled, start, size, 0)


def swap(x, bits):
    size = lax.axis_size("blk")
    return lax.ppermute(x, "blk", [(i, i ^ bits) for i in range(size)])


def in_pair(bit, mine, other):
    return jnp.where(bit == 0, jnp.stack([mine, other]), jnp.stack([other, mine]))


def pick(x, index, axis):
    return lax.dynamic_index_in_dim(x, index, axis, keepdims=False)


def after(value, *earlier):
    flat, tree = jax.tree.flatten(value)
    held = lax.optimization_barrier((tuple(flat), earlier))[0]
    return jax.tree.unflatten(tree, held)


def gather_pieces(x, *earlier):
    if lax.axis_size("blk") != 8:
        return [lax.all_gather(x, "blk", axis=0, tiled=False)]
    pieces = [None] * 8
    pieces[0] = x
    for bits in (2, 4, 6):
        pieces[bits] = swap(x, bits)
    for bits in (0, 2, 4, 6):
        pieces[bits + 1] = swap(after(pieces[bits], *earlier) if bits else x, 1)
    return pieces


def doc_range(meta, first, last, total):
    low, high = jnp.int32(0), jnp.int32(total)
    for i in range(meta.shape[0] - 1):
        start = meta[1 + i]
        low = jnp.where(start <= first, start, low)
        high = jnp.where(start > last, jnp.minimum(high, start), high)
    return low, high


def row_ranges(meta, first, rows, total):
    place = first + lax.broadcasted_iota(jnp.int32, (rows, 1), 0)
    low = jnp.zeros((rows, 1), jnp.int32)
    high = jnp.full((rows, 1), total, jnp.int32)
    for i in range(meta.shape[0] - 1):
        start = meta[1 + i]
        low = jnp.where(place >= start, start, low)
        high = jnp.where(place < start, jnp.minimum(high, start), high)
    return low, high


def head_rows(width, shift, scale):
    lane = lax.broadcasted_iota(jnp.int32, (1, width), 1)
    return [
        jnp.where((lane >= shift + 64 * i) & (lane < shift + 64 * (i + 1)), scale, 0.0).astype(F32)
        for i in range(3)
    ]


def spread_heads(block, rows):
    wide = block.astype(F32)
    return jnp.concatenate([wide * row for row in rows], axis=0).astype(BF16)


def block_of(stack, i, rows):
    return stack[i * rows : (i + 1) * rows]


def fold_heads(stack, rows):
    return stack[0] * rows[0] + stack[1] * rows[1] + stack[2] * rows[2]


def block_copies(meta, nh, nb, pieces, place, sems):
    b = meta[0]
    copies = []
    if len(pieces) == nb:
        for m, piece in enumerate(pieces):
            for r in range(nh):
                block = r * nb + jnp.bitwise_xor(b, m)
                copies.append(pltpu.make_async_copy(*place(piece, None, r, block), sems.at[m, r]))
        for copy in copies:
            copy.start()
        return copies

    def run(which):
        def one(i, carry):
            for r in range(nh):
                block = r * nb + i
                copy = pltpu.make_async_copy(*place(pieces[0], i, r, block), sems.at[i, r])
                (copy.start if which == 0 else copy.wait)()
            return carry

        lax.fori_loop(0, nb, one, 0)

    run(0)

    class Rest:
        def wait(self):
            run(1)

    return [Rest()]


def row_place(target, rows):
    def place(piece, index, r, block):
        source = piece if index is None else piece.at[index]
        return source.at[pl.ds(r * rows, rows), :], target.at[block]

    return place


def tile_bounds(meta, first, rows, total):
    low, high = doc_range(meta, first, first + rows - 1, total)
    start = lax.div(low, rows)
    tile = TILE_BLOCKS * rows
    return start, lax.div(high - start * rows + tile - 1, tile)


def tile_at(start, t, rows, total):
    begin = start + t * TILE_BLOCKS
    block = jnp.minimum(begin, total // rows - TILE_BLOCKS)
    place = block * rows + lax.broadcasted_iota(jnp.int32, (1, TILE_BLOCKS * rows), 1)
    return block, begin * rows, place


def lane_is(index):
    lane = lax.broadcasted_iota(jnp.int32, (1, 128), 1)
    return jnp.where(lane == index, 1.0, 0.0).astype(F32)


def in_lanes(columns):
    total = columns[0] * lane_is(0)
    for i in range(1, len(columns)):
        total = total + columns[i] * lane_is(i)
    return total


def three_parts(column):
    high = column.astype(BF16).astype(F32)
    middle = (column - high).astype(BF16).astype(F32)
    return [high, middle, (column - high - middle).astype(BF16).astype(F32)]


def add_parts(block, index):
    lane = 3 * index
    return block[:, lane : lane + 1] + block[:, lane + 1 : lane + 2] + block[:, lane + 2 : lane + 3]


def forward_kernel(nh, nb, count, meta, q_ref, *rest):
    pieces, (wide_ref, low_ref), (kv, sems) = rest[:count], rest[count : count + 2], rest[count + 2 :]
    rows = q_ref.shape[0] // nh
    total = nh * nb * rows
    tile = TILE_BLOCKS * rows
    b = meta[0]
    for copy in block_copies(meta, nh, nb, pieces, row_place(kv, rows), sems):
        copy.wait()
    query_rows = head_rows(WIN, 0, HEAD_DIM**-0.5)
    value_rows = head_rows(WIN, 64, 1.0)

    def one_block(r):
        first = (r * nb + b) * rows
        start, tiles = tile_bounds(meta, first, rows, total)
        low, high = row_ranges(meta, first, rows, total)
        masked = spread_heads(q_ref[r * rows : (r + 1) * rows, :], query_rows)

        def step(t, state):
            top, norm, out = state
            block, begin, place = tile_at(start, t, rows, total)
            keys = kv[pl.ds(block, TILE_BLOCKS), :, 0:WIN].reshape(tile, WIN)
            values = kv[pl.ds(block, TILE_BLOCKS), :, 128 : 128 + WIN].reshape(tile, WIN)
            allowed = (place >= jnp.maximum(low, begin)) & (place < high)
            scores = [mat(block_of(masked, i, rows), keys, CONTRACT_LAST) for i in range(3)]
            result = []
            for i in range(3):
                score = jnp.where(allowed, scores[i], neg_fill)
                new_top = jnp.maximum(top[i], jnp.max(score, axis=-1, keepdims=True))
                weights = jnp.exp(score - new_top)
                factor = jnp.exp(top[i] - new_top)
                new_norm = norm[i] * factor + jnp.sum(weights, axis=-1, keepdims=True)
                result.append((new_top, new_norm, out[i] * factor + mat(weights.astype(BF16), values)))
            return tuple(zip(*result))

        top, norm, out = lax.fori_loop(
            0,
            tiles,
            step,
            (
                (jnp.full((rows, 1), neg_fill, F32),) * 3,
                (jnp.zeros((rows, 1), F32),) * 3,
                (jnp.zeros((rows, WIN), F32),) * 3,
            ),
        )
        attended = fold_heads([out[i] / norm[i] for i in range(3)], value_rows)
        log_total = [top[i] + jnp.log(norm[i]) for i in range(3)]
        extra = in_lanes(log_total)
        wide_ref[r * rows : (r + 1) * rows, 0:128] = attended[:, 0:128] + extra
        wide_ref[r * rows : (r + 1) * rows, 128:256] = attended[:, 128:256]
        return attended

    half = nh // 2
    for r in range(half):
        left = pltpu.roll(one_block(r), WIN - 64, axis=1)
        right = one_block(r + half)
        span = slice(r * rows, (r + 1) * rows)
        low_ref[span, 0:128] = left[:, 0:128].astype(BF16)
        low_ref[span, 128:256] = (left[:, 128:256] + right[:, 0:128]).astype(BF16)
        low_ref[span, 256:384] = right[:, 128:256].astype(BF16)


def delta_kernel(nh, wide_ref, *rest):
    slots, grad_ref = rest[:nh], rest[nh]
    rows = wide_ref.shape[0] // nh
    half = nh // 2
    value_rows = head_rows(WIN, 64, 1.0)
    every = value_rows[0] + value_rows[1] + value_rows[2]

    def one_block(r, grad):
        span = slice(r * rows, (r + 1) * rows)
        grad = (grad * every).astype(BF16).astype(F32)
        wide = wide_ref[span, :]
        product = grad * wide
        parts = []
        for i in range(3):
            parts += three_parts(wide[:, i : i + 1])
        for i in range(3):
            parts += three_parts(jnp.sum(product * value_rows[i], axis=-1, keepdims=True))
        grad_ref[span, 0:128] = (grad[:, 0:128] + in_lanes(parts)).astype(BF16)
        grad_ref[span, 128:256] = grad[:, 128:256].astype(BF16)

    for r in range(half):
        total = slots[0][r * rows : (r + 1) * rows, :].astype(F32)
        for i in range(1, nh):
            total = total + slots[i][r * rows : (r + 1) * rows, :].astype(F32)
        one_block(r, pltpu.roll(total[:, 0:WIN], 64, axis=1))
        one_block(r + half, total[:, 128 : 128 + WIN])


def query_kernel(nh, nb, count, meta, q_ref, g_ref, *rest):
    pieces, out_ref, (kv, sems) = rest[:count], rest[count], rest[count + 1 :]
    rows = q_ref.shape[0] // nh
    total = nh * nb * rows
    tile = TILE_BLOCKS * rows
    b = meta[0]
    for copy in block_copies(meta, nh, nb, pieces, row_place(kv, rows), sems):
        copy.wait()
    query_rows = head_rows(WIN, 0, HEAD_DIM**-0.5)
    value_rows = head_rows(WIN, 64, 1.0)
    for r in range(nh):
        span = slice(r * rows, (r + 1) * rows)
        first = (r * nb + b) * rows
        start, tiles = tile_bounds(meta, first, rows, total)
        low, high = row_ranges(meta, first, rows, total)
        masked = spread_heads(q_ref[span, :], query_rows)
        grads = spread_heads(g_ref[span, :], value_rows)
        stats = g_ref[span, 0:128].astype(F32)
        log_total = jnp.stack([add_parts(stats, i) for i in range(3)])
        delta = jnp.stack([add_parts(stats, 3 + i) for i in range(3)])

        def step(t, state):
            block, begin, place = tile_at(start, t, rows, total)
            allowed = (place >= jnp.maximum(low, begin)) & (place < high)
            parts = []
            for first_one, count_now in TILE_PARTS:
                keys = kv[pl.ds(block + first_one, count_now), :, 0:WIN].reshape(-1, WIN)
                values = kv[pl.ds(block + first_one, count_now), :, 128 : 128 + WIN].reshape(-1, WIN)
                scores = mat(masked, keys, CONTRACT_LAST)
                parts.append((keys, scores, mat(grads, values, CONTRACT_LAST)))
            for (first_one, count_now), (keys, scores, grad_probs) in zip(TILE_PARTS, parts):
                inside = allowed[:, first_one * rows : (first_one + count_now) * rows]
                scores = scores.reshape(3, rows, count_now * rows)
                grad_probs = grad_probs.reshape(3, rows, count_now * rows)
                probs = jnp.exp(jnp.where(inside[None], scores, neg_fill) - log_total)
                grad_scores = (probs * (grad_probs - delta)).astype(BF16)
                part = mat(grad_scores.reshape(3 * rows, count_now * rows), keys)
                state = state + part.reshape(3, rows, WIN)
            return state

        total_grad = lax.fori_loop(0, tiles, step, jnp.zeros((3, rows, WIN), F32))
        out_ref[span, :] = fold_heads(total_grad, query_rows).astype(BF16)


def key_kernel(nh, nb, counts, meta, kv_ref, *rest):
    both = counts[0] + counts[1]
    q_in, g_in, out_ref = rest[: counts[0]], rest[counts[0] : both], rest[both]
    queries_all, grads_all, q_sems, g_sems = rest[both + 1 :]
    rows = kv_ref.shape[0] // nh
    total = nh * nb * rows
    tile = TILE_BLOCKS * rows
    b = meta[0]
    copies = block_copies(meta, nh, nb, q_in, row_place(queries_all, rows), q_sems)
    copies += block_copies(meta, nh, nb, g_in, row_place(grads_all, rows), g_sems)
    for copy in copies:
        copy.wait()
    key_rows = head_rows(WIN, 0, HEAD_DIM**-0.5)
    value_rows = head_rows(WIN, 64, 1.0)
    line = lax.broadcasted_iota(jnp.int32, (8, WIN), 0) * 3
    lane = lax.broadcasted_iota(jnp.int32, (8, WIN), 1)
    choose = jnp.where((lane >= line) & (lane < line + 3), 1.0, 0.0).astype(BF16)
    for r in range(nh):
        span = slice(r * rows, (r + 1) * rows)
        first = (r * nb + b) * rows
        start, tiles = tile_bounds(meta, first, rows, total)
        low, high = row_ranges(meta, first, rows, total)
        keys = spread_heads(kv_ref[span, 0:WIN], key_rows)
        values = spread_heads(kv_ref[span, 128 : 128 + WIN], value_rows)

        def step(t, state):
            grad_keys, grad_values = state
            block, begin, place = tile_at(start, t, rows, total)
            allowed = (place >= jnp.maximum(low, begin)) & (place < high)
            parts = []
            for first_one, count_now in TILE_PARTS:
                queries = queries_all[pl.ds(block + first_one, count_now)].reshape(-1, WIN)
                grads = grads_all[pl.ds(block + first_one, count_now)].reshape(-1, WIN)
                stats = mat(choose, grads, CONTRACT_LAST)
                scores = mat(keys, queries, CONTRACT_LAST)
                parts.append((queries, grads, stats, scores, mat(values, grads, CONTRACT_LAST)))
            for (first_one, count_now), (queries, grads, stats, scores, grad_probs) in zip(TILE_PARTS, parts):
                inside = allowed[:, first_one * rows : (first_one + count_now) * rows]
                scores = scores.reshape(3, rows, count_now * rows)
                grad_probs = grad_probs.reshape(3, rows, count_now * rows)
                log_total = jnp.stack([stats[i : i + 1] for i in range(3)])
                delta = jnp.stack([stats[3 + i : 4 + i] for i in range(3)])
                probs = jnp.exp(jnp.where(inside[None], scores, neg_fill) - log_total)
                grad_scores = (probs * (grad_probs - delta)).astype(BF16)
                part_value = mat(probs.astype(BF16).reshape(3 * rows, count_now * rows), grads)
                part_key = mat(grad_scores.reshape(3 * rows, count_now * rows), queries)
                grad_keys = grad_keys + part_key.reshape(3, rows, WIN)
                grad_values = grad_values + part_value.reshape(3, rows, WIN)
            return grad_keys, grad_values

        zero = jnp.zeros((3, rows, WIN), F32)
        grad_keys, grad_values = lax.fori_loop(0, tiles, step, (zero, zero))
        key_out = fold_heads(grad_keys, key_rows)
        value_out = fold_heads(grad_values, value_rows)
        out_ref[span, 0:128] = key_out[:, 0:128].astype(BF16)
        out_ref[span, 128:256] = (key_out[:, 128:256] + value_out[:, 0:128]).astype(BF16)
        out_ref[span, 256:384] = value_out[:, 128:256].astype(BF16)


SMEM_SPEC = pl.BlockSpec(memory_space=pltpu.SMEM)
VMEM_SPEC = pl.BlockSpec(memory_space=pltpu.VMEM)
ANY_SPEC = pl.BlockSpec(memory_space=pl.ANY)


def kernel_params():
    return pltpu.CompilerParams(vmem_limit_bytes=56 * 1024 * 1024)


def cost(matmuls, nh, nb, rows):
    flops = matmuls * 2 * 3 * rows * WIN * 32 * TILE_BLOCKS * rows * nh // 4 * 2
    return pl.CostEstimate(flops=flops, bytes_accessed=nh * nb * rows * 384 * 2, transcendentals=0)


def attend(meta, queries, pieces, nh, nb):
    length = queries.shape[0]
    rows = length // nh
    count = len(pieces)
    return pl.pallas_call(
        functools.partial(forward_kernel, nh, nb, count),
        out_shape=(
            jax.ShapeDtypeStruct((length, WIN), F32),
            jax.ShapeDtypeStruct((length // 2, 384), BF16),
        ),
        in_specs=[SMEM_SPEC, VMEM_SPEC] + [ANY_SPEC] * count,
        out_specs=(VMEM_SPEC,) * 2,
        scratch_shapes=[
            pltpu.VMEM((nh * nb, rows, 384), BF16),
            pltpu.SemaphoreType.DMA((nb, nh)),
        ],
        compiler_params=kernel_params(),
        cost_estimate=cost(2, nh, nb, rows),
        name="attend",
    )(meta, queries, *pieces)


def delta_rows(wide, slots):
    nh = len(slots)
    return pl.pallas_call(
        functools.partial(delta_kernel, nh),
        out_shape=jax.ShapeDtypeStruct(wide.shape, BF16),
        in_specs=[VMEM_SPEC] * (1 + nh),
        out_specs=VMEM_SPEC,
        compiler_params=kernel_params(),
        name="delta",
    )(wide, *slots)


def middle_kernel(
    nh, place, att_ref, x_ref, cot_ref, wo_ref, up_ref, down_ref, line_ref, joined_ref, own_ref, a2_ref, act_ref,
    hid_ref, low_ref, grad_ref, sum_ref, *rest
):
    outs, (mid, wide, packed) = rest[:nh], rest[nh:]
    h = place[0]
    length, width = x_ref.shape
    half = length // 2
    rows = length // nh
    group = width // nh
    lane = lax.broadcasted_iota(jnp.int32, (1, 128), 1)
    left = jnp.where(lane < 64, 1.0, 0.0).astype(F32)
    right = 1.0 - left
    for side in range(2):
        span = slice(side * half, (side + 1) * half)
        for pair in range(nh // 2):
            first = att_ref[2 * pair, :, 128 * side : 128 * side + WIN].astype(F32)
            second = att_ref[2 * pair + 1, :, 128 * side : 128 * side + WIN].astype(F32)
            if side == 0:
                second = pltpu.roll(second, 64, axis=1)
            else:
                first = pltpu.roll(first, WIN - 64, axis=1)
            at = 2 * pair * group
            joined_ref[span, at : at + 128] = first[:, 0:128].astype(BF16)
            joined_ref[span, at + 128 : at + 256] = (first[:, 128:256] * left + second[:, 0:128] * right).astype(BF16)
            joined_ref[span, at + 256 : at + 384] = second[:, 128:256].astype(BF16)
    out_bias, gain, shift, up_bias = (line_ref[i : i + 1, :] for i in range(4))
    sum_ref[...] = jnp.zeros(sum_ref.shape, F32)

    def mean(value):
        return jnp.mean(value, axis=-1, keepdims=True)

    def one_half(side, carry):
        span = pl.ds(pl.multiple_of(side * half, half), half)
        middle = x_ref[span, :].astype(F32) + (mat(joined_ref[span, :], wo_ref[...]) + out_bias)
        mid[span, :] = middle
        normed, inv_spread = norm_parts(middle)
        second_low = (normed * gain + shift).astype(BF16)
        a2_ref[span, :] = second_low
        active, slope = gelu_pair(mat(second_low, up_ref[...]) + up_bias)
        act_ref[span, :] = active.astype(BF16)
        cot = cot_ref[span, :]
        grad_hidden = (mat(cot, down_ref[...], CONTRACT_LAST) * slope).astype(BF16)
        hid_ref[span, :] = grad_hidden
        grad_second = mat(grad_hidden, up_ref[...], CONTRACT_LAST)
        row = side * half + lax.broadcasted_iota(jnp.int32, (half, 1), 0)
        is_own = (row >= h * rows) & (row < (h + 1) * rows)
        grad_middle = norm_pull(grad_second, normed, inv_spread, gain)
        grad_middle = grad_middle + jnp.where(is_own, cot.astype(F32), 0.0)
        grad_ref[span, :] = grad_middle
        low = grad_middle.astype(BF16)
        low_ref[span, :] = low
        wide[span, :] = mat(low, wo_ref[...], CONTRACT_LAST)
        sum_ref[0:1, :] += jnp.sum(low.astype(F32), axis=0, keepdims=True)
        sum_ref[1:2, :] += jnp.sum(grad_second * normed, axis=0, keepdims=True)
        sum_ref[2:3, :] += jnp.sum(grad_second, axis=0, keepdims=True)
        sum_ref[3:4, :] += jnp.sum(grad_hidden.astype(F32), axis=0, keepdims=True)
        return carry

    lax.fori_loop(0, 2, one_half, 0)
    own_ref[...] = mid[pl.ds(pl.multiple_of(h * rows, rows), rows), :]
    for g in range(nh):
        shift_now = g * group % 128
        at = g * group - shift_now
        top = wide[0:half, at : at + WIN]
        if shift_now:
            top = pltpu.roll(top, WIN - shift_now, axis=1)
        bottom = wide[half:length, at : at + WIN]
        if shift_now != 64:
            bottom = pltpu.roll(bottom, 64 - shift_now, axis=1)
        packed[g, :, 0:128] = top[:, 0:128].astype(BF16)
        packed[g, :, 128:256] = (top[:, 128:256] * left + bottom[:, 0:128] * right).astype(BF16)
        packed[g, :, 256:384] = bottom[:, 128:256].astype(BF16)
    for r in range(nh):
        outs[r][...] = packed[lax.rem(h - r + nh, nh)]


def middle_stage(place, attended, tokens, cot, wo, up, down, lines, nh):
    length, width = tokens.shape
    full = jax.ShapeDtypeStruct((length, width), BF16)
    piece = jax.ShapeDtypeStruct(attended.shape[1:], BF16)
    shapes = (
        full,
        jax.ShapeDtypeStruct((length // nh, width), F32),
        full,
        full,
        full,
        full,
        jax.ShapeDtypeStruct((length, width), F32),
        jax.ShapeDtypeStruct((8, width), F32),
    ) + (piece,) * nh
    return pl.pallas_call(
        functools.partial(middle_kernel, nh),
        out_shape=shapes,
        in_specs=[SMEM_SPEC] + [VMEM_SPEC] * 7,
        out_specs=(VMEM_SPEC,) * len(shapes),
        scratch_shapes=[
            pltpu.VMEM((length, width), F32),
            pltpu.VMEM((length, width), F32),
            pltpu.VMEM(attended.shape, BF16),
        ],
        compiler_params=kernel_params(),
        cost_estimate=pl.CostEstimate(flops=12 * length * width * width, bytes_accessed=12 * 2**20, transcendentals=0),
        name="middle",
    )(place, attended, tokens, cot, wo, up, down, lines)


def query_grads(meta, queries, grads, pieces, nh, nb):
    length = queries.shape[0]
    rows = length // nh
    count = len(pieces)
    return pl.pallas_call(
        functools.partial(query_kernel, nh, nb, count),
        out_shape=jax.ShapeDtypeStruct((length, WIN), BF16),
        in_specs=[SMEM_SPEC] + [VMEM_SPEC] * 2 + [ANY_SPEC] * count,
        out_specs=VMEM_SPEC,
        scratch_shapes=[
            pltpu.VMEM((nh * nb, rows, 384), BF16),
            pltpu.SemaphoreType.DMA((nb, nh)),
        ],
        compiler_params=kernel_params(),
        cost_estimate=cost(3, nh, nb, rows),
        name="query_grads",
    )(meta, queries, grads, *pieces)


def key_grads(meta, own, queries, grads, nh, nb):
    length = own.shape[0]
    rows = length // nh
    counts = (len(queries), len(grads))
    return pl.pallas_call(
        functools.partial(key_kernel, nh, nb, counts),
        out_shape=jax.ShapeDtypeStruct((length, 384), BF16),
        in_specs=[SMEM_SPEC, VMEM_SPEC] + [ANY_SPEC] * sum(counts),
        out_specs=VMEM_SPEC,
        scratch_shapes=[
            pltpu.VMEM((nh * nb, rows, WIN), BF16),
            pltpu.VMEM((nh * nb, rows, WIN), BF16),
            pltpu.SemaphoreType.DMA((nb, nh)),
            pltpu.SemaphoreType.DMA((nb, nh)),
        ],
        compiler_params=kernel_params(),
        cost_estimate=cost(4, nh, nb, rows),
        name="key_grads",
    )(meta, own, *queries, *grads)


def gather_blk_rows(here):
    if lax.axis_size("blk") != 8:
        whole = lax.all_gather(here, "blk", axis=0, tiled=False)
        return jnp.moveaxis(whole, 0, 1).reshape(-1, here.shape[-1])
    b = lax.axis_index("blk")
    core, x_bit, y_bit = b & 1, (b >> 1) & 1, b >> 2
    side, up, cross = swap(here, 2), swap(here, 4), swap(here, 6)
    square = in_pair(y_bit, in_pair(x_bit, here, side), in_pair(x_bit, up, cross))
    whole = in_pair(core, square, swap(square, 1))
    return whole.transpose(3, 1, 2, 0, 4, 5).reshape(-1, here.shape[-1])


def scatter_blk_rows(grad, nh, nb):
    width = grad.shape[-1]
    if nb != 8:
        parts = grad.reshape(nh, nb, -1, width)
        return lax.psum_scatter(parts, "blk", scatter_dimension=1, tiled=False).astype(BF16)
    b = lax.axis_index("blk")
    core, x_bit, y_bit = b & 1, (b >> 1) & 1, b >> 2
    parts = grad.astype(BF16).reshape(nh, 2, 2, 2, -1, width)
    sent = swap(pick(parts, 1 - core, 3), 1)
    chip = (pick(parts, core, 3).astype(F32) + sent.astype(F32)).astype(BF16)

    def part(y, x):
        return pick(pick(chip, y, 1), x, 1)

    side = swap(part(y_bit, 1 - x_bit), 2)
    up = swap(part(1 - y_bit, x_bit), 4)
    cross = swap(part(1 - y_bit, 1 - x_bit), 6)
    mine = part(y_bit, x_bit).astype(F32) + side.astype(F32)
    return (mine + up.astype(F32) + cross.astype(F32)).astype(BF16)


def shards(
    tokens,
    cotangent,
    doc_starts,
    norm_gain,
    norm_shift,
    triple_weight,
    query_bias,
    value_bias,
    output_weight,
    output_bias,
    final_gain,
    final_shift,
    up_weight,
    up_bias,
    down_weight,
    down_bias,
):
    nh = lax.axis_size("head")
    nb = lax.axis_size("blk")
    h = lax.axis_index("head")
    b = lax.axis_index("blk")
    rows, width = tokens.shape
    part = norm_gain.shape[0]
    group = HEADS // nh * HEAD_DIM
    ff_part = up_bias.shape[0]
    ff_group = nb * ff_part
    extra = max(part, 12)
    meta = jnp.concatenate([b.astype(jnp.int32)[None], doc_starts])

    packed = jnp.stack(
        [
            norm_gain,
            norm_shift,
            query_bias,
            value_bias,
            output_bias,
            final_gain,
            final_shift,
            down_bias,
        ]
    )
    packed = jnp.concatenate([packed, up_bias.reshape(4, part)], axis=0)
    if extra > 12:
        packed = jnp.pad(packed, ((0, extra - 12), (0, 0)))
    columns = triple_weight.reshape(part, 3, nh, group)
    pieces = [columns[:, 1], columns[:, 2], columns[:, 0]]
    if part == extra:
        pieces.append(jnp.broadcast_to(packed[:, None], (part, nh, part)))
    pieces.append(up_weight.reshape(part, nh, ff_group))
    pieces.append(jnp.broadcast_to(output_weight[:, None], (part, nh, width)))
    columns = exchange(jnp.concatenate(pieces, axis=-1).transpose(1, 0, 2))
    token_rows = spread(tokens).reshape(nh * rows, width)
    first_width = 3 * group + (part if part == extra else 0)
    group_weight = gather_blk_rows(columns[..., :first_width])

    late = jnp.concatenate(
        [
            columns[..., first_width : first_width + ff_group].reshape(-1, ff_group),
            down_weight,
            columns[..., first_width + ff_group :].reshape(-1, width),
        ],
        axis=0,
    )
    if part == extra:
        vectors = group_weight[:, 3 * group :].reshape(nh * nb, extra, part)[:, :12]
    else:
        vectors = lax.all_gather(packed, ("head", "blk"), axis=0, tiled=False)
    group_weight = group_weight[:, : 3 * group]
    lines = vectors[:, :8].transpose(1, 0, 2).reshape(8, width).astype(F32)
    gain_one, shift_one, query_all, value_all, out_bias, gain_two, shift_two, down_bias_all = (
        lines[i] for i in range(8)
    )
    up_bias_own = pick(vectors[:, 8:].reshape(nh, nb * ff_part), h, 0).astype(F32)

    key_value_weight = group_weight[:, : 2 * group]
    query_weight = jnp.pad(group_weight[:, 2 * group :], ((0, 0), (0, WIN - group)))
    token_wide = token_rows.astype(F32)
    normed_one, spread_one = norm_parts(token_wide)
    first_low = (normed_one * gain_one + shift_one).astype(BF16)
    value_bias_own = lax.dynamic_slice_in_dim(value_all, h * group, group)
    query_bias_own = lax.dynamic_slice_in_dim(query_all, h * group, group)
    kv_bias = jnp.concatenate([jnp.zeros((group,), F32), value_bias_own])
    key_values = (mat(first_low, key_value_weight) + kv_bias).astype(BF16)
    kv_pieces = gather_pieces(key_values)
    q_bias = jnp.pad(query_bias_own, (0, WIN - group))
    queries = (mat(first_low, query_weight) + q_bias).astype(BF16)
    late = lax.all_gather(after(late, *kv_pieces), "blk", axis=0, tiled=False)
    up_own = jnp.moveaxis(late[:, : nh * part].reshape(nb, nh, part, ff_group), 0, 1)
    up_own = up_own.reshape(width, ff_group)
    down_own = late[:, nh * part : nh * part + ff_part].reshape(ff_group, width)
    out_own = jnp.moveaxis(late[:, nh * part + ff_part :].reshape(nb, nh, part, width), 0, 1)
    out_own = out_own.reshape(width, width)
    slow = jnp.concatenate([cotangent, jnp.zeros((rows // 8 * 3, width), BF16)], axis=0)
    slow = lax.all_gather(after(slow, token_rows), "head", axis=0, tiled=False)
    cot_all = slow[:, :rows].reshape(nh * rows, width)
    wide, attended = attend(meta, queries, kv_pieces, nh, nb)
    query_pieces = [lax.all_gather(after(queries, attended), "blk", axis=0, tiled=False)]

    lines_two = jnp.stack([out_bias, gain_two, shift_two, up_bias_own])
    (
        joined,
        output_own,
        second_low,
        active_low,
        grad_hidden,
        branch_grad,
        grad_middle,
        middle_sums,
        *grad_slots,
    ) = middle_stage(
        h.astype(jnp.int32)[None], spread(attended), token_rows, cot_all, out_own, up_own, down_own, lines_two, nh
    )
    for r in range(1, nh):
        grad_slots[r] = turn(grad_slots[r], -r)

    active_low, cot_late, second_late, grad_hidden, branch_late, joined_late = after(
        (active_low, cot_all, second_low, grad_hidden, branch_grad, joined)
    )
    output_part = mat(active_low, down_own).astype(BF16).reshape(nh, rows, width)
    grad_up_own = mat(second_late, grad_hidden, CONTRACT_FIRST).astype(BF16)
    grad_down_own = mat(active_low, cot_late, CONTRACT_FIRST).astype(BF16)
    grad_out = mat(joined_late, branch_late, CONTRACT_FIRST).astype(BF16).reshape(nh, nb, part, width)
    late_grads = jnp.concatenate(
        [
            jnp.moveaxis(grad_up_own.reshape(nh, nb, part, ff_group), 0, 1).reshape(nb, -1, width),
            grad_down_own.reshape(nb, ff_part, width),
            jnp.moveaxis(grad_out, 0, 1).reshape(nb, -1, width),
        ],
        axis=1,
    )
    late_sums = lax.psum_scatter(late_grads, "blk", scatter_dimension=0, tiled=False)

    grad_attended = delta_rows(wide, after(grad_slots, late_grads, output_part))
    grad_queries = query_grads(meta, queries, grad_attended, kv_pieces, nh, nb)
    grad_pieces = gather_pieces(grad_attended, grad_queries)
    grad_key_values = key_grads(meta, key_values, query_pieces, grad_pieces, nh, nb)

    grad_group = jnp.concatenate([grad_key_values, grad_queries[:, :group]], axis=1)
    grad_group, late_sums = after((grad_group, late_sums))
    sum_down_w = late_sums[nh * part : nh * part + ff_part].astype(F32)
    first_part = mat(grad_group, group_weight, CONTRACT_LAST)
    grad_in = grad_middle + norm_pull(first_part, normed_one, spread_one, gain_one)
    grad_in = grad_in.astype(BF16).reshape(nh, rows, width)
    late_rows = jnp.concatenate([grad_in, output_part], axis=1)
    row_sums = lax.psum_scatter(late_rows, "head", scatter_dimension=0, tiled=False)
    first_late, grad_group = after((first_low, grad_group), late_rows)
    grad_triple_part = mat(first_late, grad_group, CONTRACT_FIRST).astype(BF16)

    group_sums = jnp.sum(grad_group.astype(F32), axis=0)
    placed = jnp.where(
        jnp.arange(nh)[None, :, None] == h,
        jnp.stack([group_sums[2 * group :], group_sums[group : 2 * group]])[:, None],
        0.0,
    ).reshape(2, width)
    up_b = middle_sums[3]
    up_b = jnp.where(jnp.arange(nh)[:, None] == h, up_b[None], 0.0).reshape(nh * nb, 4, part)
    sums = jnp.stack(
        [
            jnp.sum(first_part * normed_one, axis=0),
            jnp.sum(first_part, axis=0),
            placed[0],
            placed[1],
            middle_sums[0],
            middle_sums[1],
            middle_sums[2],
            jnp.sum(cotangent.astype(F32), axis=0),
        ]
    )
    sums = sums.reshape(8, nh * nb, part).transpose(1, 0, 2)
    sums = jnp.concatenate([sums, up_b], axis=1)
    if part == extra:
        low_sums = jnp.pad(sums.astype(BF16), ((0, 0), (0, extra - 12), (0, 0)))
        low_sums = low_sums.reshape(width, part)
        here = scatter_blk_rows(jnp.concatenate([grad_triple_part, low_sums], axis=1), nh, nb)
    else:
        sums = lax.psum(sums, ("head", "blk"))
        sums = pick(sums, h * nb + b, 0)
        here = scatter_blk_rows(grad_triple_part, nh, nb)
    final = [
        here,
        late_sums[: nh * part].reshape(nh, part, ff_group),
        late_sums[nh * part + ff_part :].reshape(nh, part, width),
    ]
    final = jnp.concatenate(final, axis=-1)
    slots = [pick(final, h, 0)]
    for r in range(1, nh):
        slots.append(turn(pick(final, lax.rem(h - r + nh, nh), 0), -r))
    slots, row_sums = after((slots, row_sums))
    input_grad = row_sums[:rows].astype(BF16)
    output_rows = (output_own + row_sums[rows:].astype(F32) + down_bias_all).astype(BF16)
    final = by_group(slots).astype(F32)
    if part == extra:
        sums = jnp.sum(final[:, :12, 3 * group : first_width], axis=0)
    sum_triple = jnp.concatenate(
        [
            final[:, :, 2 * group : 3 * group].transpose(1, 0, 2).reshape(part, width),
            final[:, :, :group].transpose(1, 0, 2).reshape(part, width),
            final[:, :, group : 2 * group].transpose(1, 0, 2).reshape(part, width),
        ],
        axis=1,
    )
    sum_up_w = final[:, :, first_width : first_width + ff_group]
    sum_up_w = sum_up_w.transpose(1, 0, 2).reshape(part, nh * ff_group)
    sum_out_w = jnp.sum(final[:, :, first_width + ff_group :], axis=0)
    return (
        output_rows,
        input_grad,
        sums[0],
        sums[1],
        sum_triple,
        sums[2],
        sums[3],
        sum_out_w,
        sums[4],
        sums[5],
        sums[6],
        sum_up_w,
        sums[8:].reshape(ff_part),
        sum_down_w,
        sums[7],
    )


def solution(mesh):
    wide = P(("head", "blk"), None)
    thin = P(("head", "blk"))
    in_specs = (
        wide,
        wide,
        P(),
        thin,
        thin,
        wide,
        thin,
        thin,
        wide,
        thin,
        thin,
        thin,
        wide,
        thin,
        wide,
        thin,
    )
    out_specs = (
        wide,
        wide,
        thin,
        thin,
        wide,
        thin,
        thin,
        wide,
        thin,
        thin,
        thin,
        wide,
        thin,
        wide,
        thin,
    )
    return jax.shard_map(shards, mesh=mesh, in_specs=in_specs, out_specs=out_specs, check_vma=False)
```

```python
import functools

import jax
import jax.numpy as jnp
from jax import lax
from jax.experimental import pallas as pl
from jax.experimental.pallas import tpu as pltpu
from jax.sharding import PartitionSpec as P

HEADS = 12
HEAD_DIM = 64

epsilon = 1e-06
neg_fill = -1e30
root_half = 0.7071067811865476
inv_root_two_pi = 0.3989422804014327

F32 = jnp.float32
BF16 = jnp.bfloat16
WIN = 256
TILE_BLOCKS = 6
TILE_PARTS = ((0, 4), (4, 2))
CONTRACT_LAST = (((1,), (1,)), ((), ()))
CONTRACT_FIRST = (((0,), (0,)), ((), ()))
PLAIN = (((1,), (0,)), ((), ()))


def norm_parts(values):
    centre = jnp.mean(values, axis=-1, keepdims=True)
    offset = values - centre
    inv_spread = lax.rsqrt(jnp.mean(offset * offset, axis=-1, keepdims=True) + epsilon)
    return (offset * inv_spread, inv_spread)


def norm_pull(grad_out, normed, inv_spread, gain_full):
    grad_normed = grad_out * gain_full
    return inv_spread * (
        grad_normed
        - jnp.mean(grad_normed, axis=-1, keepdims=True)
        - normed * jnp.mean(grad_normed * normed, axis=-1, keepdims=True)
    )


def gelu_pair(hidden):
    normal_cdf = 0.5 * (1.0 + lax.erf(hidden * root_half))
    return (
        hidden * normal_cdf,
        normal_cdf + hidden * inv_root_two_pi * jnp.exp(-0.5 * hidden * hidden),
    )


def mat(left, right, dims=PLAIN):
    return lax.dot_general(left, right, dims, preferred_element_type=F32)


def exchange(x):
    return lax.all_to_all(x, "head", 0, 0, tiled=True)


def share(x):
    return exchange(jnp.broadcast_to(x[None], (lax.axis_size("head"),) + x.shape))


def turn(x, step):
    size = lax.axis_size("head")
    return lax.ppermute(x, "head", [(i, (i + step) % size) for i in range(size)])


def by_head(slots):
    size = len(slots)
    doubled = jnp.stack([slots[(size - 1 - i) % size] for i in range(2 * size - 1)])
    return lax.dynamic_slice_in_dim(doubled, size - 1 - lax.axis_index("head"), size, 0)


def spread(x):
    return by_head([x] + [turn(x, r) for r in range(1, lax.axis_size("head"))])


def by_group(slots):
    size = len(slots)
    doubled = jnp.stack([slots[i % size] for i in range(2 * size - 1)])
    start = lax.rem(size - lax.axis_index("head"), size)
    return lax.dynamic_slice_in_dim(doubled, start, size, 0)


def swap(x, bits):
    size = lax.axis_size("blk")
    return lax.ppermute(x, "blk", [(i, i ^ bits) for i in range(size)])


def in_pair(bit, mine, other):
    return jnp.where(bit == 0, jnp.stack([mine, other]), jnp.stack([other, mine]))


def pick(x, index, axis):
    return lax.dynamic_index_in_dim(x, index, axis, keepdims=False)


def after(value, *earlier):
    flat, tree = jax.tree.flatten(value)
    held = lax.optimization_barrier((tuple(flat), earlier))[0]
    return jax.tree.unflatten(tree, held)


def gather_pieces(x, *earlier):
    if lax.axis_size("blk") != 8:
        return [lax.all_gather(x, "blk", axis=0, tiled=False)]
    pieces = [None] * 8
    pieces[0] = x
    for bits in (2, 4, 6):
        pieces[bits] = swap(x, bits)
    for bits in (0, 2, 4, 6):
        pieces[bits + 1] = swap(after(pieces[bits], *earlier) if bits else x, 1)
    return pieces


def doc_range(meta, first, last, total):
    low, high = jnp.int32(0), jnp.int32(total)
    for i in range(meta.shape[0] - 1):
        start = meta[1 + i]
        low = jnp.where(start <= first, start, low)
        high = jnp.where(start > last, jnp.minimum(high, start), high)
    return low, high


def row_ranges(meta, first, rows, total):
    place = first + lax.broadcasted_iota(jnp.int32, (rows, 1), 0)
    low = jnp.zeros((rows, 1), jnp.int32)
    high = jnp.full((rows, 1), total, jnp.int32)
    for i in range(meta.shape[0] - 1):
        start = meta[1 + i]
        low = jnp.where(place >= start, start, low)
        high = jnp.where(place < start, jnp.minimum(high, start), high)
    return low, high


def head_rows(width, shift, scale):
    lane = lax.broadcasted_iota(jnp.int32, (1, width), 1)
    return [
        jnp.where((lane >= shift + 64 * i) & (lane < shift + 64 * (i + 1)), scale, 0.0).astype(F32)
        for i in range(3)
    ]


def spread_heads(block, rows):
    wide = block.astype(F32)
    return jnp.concatenate([wide * row for row in rows], axis=0).astype(BF16)


def block_of(stack, i, rows):
    return stack[i * rows : (i + 1) * rows]


def fold_heads(stack, rows):
    return stack[0] * rows[0] + stack[1] * rows[1] + stack[2] * rows[2]


def block_copies(meta, nh, nb, pieces, place, sems):
    b = meta[0]
    copies = []
    if len(pieces) == nb:
        for m, piece in enumerate(pieces):
            for r in range(nh):
                block = r * nb + jnp.bitwise_xor(b, m)
                copies.append(pltpu.make_async_copy(*place(piece, None, r, block), sems.at[m, r]))
        for copy in copies:
            copy.start()
        return copies

    def run(which):
        def one(i, carry):
            for r in range(nh):
                block = r * nb + i
                copy = pltpu.make_async_copy(*place(pieces[0], i, r, block), sems.at[i, r])
                (copy.start if which == 0 else copy.wait)()
            return carry

        lax.fori_loop(0, nb, one, 0)

    run(0)

    class Rest:
        def wait(self):
            run(1)

    return [Rest()]


def row_place(target, rows):
    def place(piece, index, r, block):
        source = piece if index is None else piece.at[index]
        return source.at[pl.ds(r * rows, rows), :], target.at[block]

    return place


def tile_bounds(meta, first, rows, total):
    low, high = doc_range(meta, first, first + rows - 1, total)
    start = lax.div(low, rows)
    tile = TILE_BLOCKS * rows
    return start, lax.div(high - start * rows + tile - 1, tile)


def tile_at(start, t, rows, total):
    begin = start + t * TILE_BLOCKS
    block = jnp.minimum(begin, total // rows - TILE_BLOCKS)
    place = block * rows + lax.broadcasted_iota(jnp.int32, (1, TILE_BLOCKS * rows), 1)
    return block, begin * rows, place


def lane_is(index):
    lane = lax.broadcasted_iota(jnp.int32, (1, 128), 1)
    return jnp.where(lane == index, 1.0, 0.0).astype(F32)


def in_lanes(columns):
    total = columns[0] * lane_is(0)
    for i in range(1, len(columns)):
        total = total + columns[i] * lane_is(i)
    return total


def three_parts(column):
    high = column.astype(BF16).astype(F32)
    middle = (column - high).astype(BF16).astype(F32)
    return [high, middle, (column - high - middle).astype(BF16).astype(F32)]


def add_parts(block, index):
    lane = 3 * index
    return block[:, lane : lane + 1] + block[:, lane + 1 : lane + 2] + block[:, lane + 2 : lane + 3]


def forward_kernel(nh, nb, count, meta, q_ref, *rest):
    pieces, (wide_ref, low_ref), (kv, sems) = rest[:count], rest[count : count + 2], rest[count + 2 :]
    rows = q_ref.shape[0] // nh
    total = nh * nb * rows
    tile = TILE_BLOCKS * rows
    b = meta[0]
    for copy in block_copies(meta, nh, nb, pieces, row_place(kv, rows), sems):
        copy.wait()
    query_rows = head_rows(WIN, 0, HEAD_DIM**-0.5)
    value_rows = head_rows(WIN, 64, 1.0)

    def one_block(r):
        first = (r * nb + b) * rows
        start, tiles = tile_bounds(meta, first, rows, total)
        low, high = row_ranges(meta, first, rows, total)
        masked = spread_heads(q_ref[r * rows : (r + 1) * rows, :], query_rows)

        def step(t, state):
            top, norm, out = state
            block, begin, place = tile_at(start, t, rows, total)
            keys = kv[pl.ds(block, TILE_BLOCKS), :, 0:WIN].reshape(tile, WIN)
            values = kv[pl.ds(block, TILE_BLOCKS), :, 128 : 128 + WIN].reshape(tile, WIN)
            allowed = (place >= jnp.maximum(low, begin)) & (place < high)
            scores = [mat(block_of(masked, i, rows), keys, CONTRACT_LAST) for i in range(3)]
            result = []
            for i in range(3):
                score = jnp.where(allowed, scores[i], neg_fill)
                new_top = jnp.maximum(top[i], jnp.max(score, axis=-1, keepdims=True))
                weights = jnp.exp(score - new_top)
                factor = jnp.exp(top[i] - new_top)
                new_norm = norm[i] * factor + jnp.sum(weights, axis=-1, keepdims=True)
                result.append((new_top, new_norm, out[i] * factor + mat(weights.astype(BF16), values)))
            return tuple(zip(*result))

        top, norm, out = lax.fori_loop(
            0,
            tiles,
            step,
            (
                (jnp.full((rows, 1), neg_fill, F32),) * 3,
                (jnp.zeros((rows, 1), F32),) * 3,
                (jnp.zeros((rows, WIN), F32),) * 3,
            ),
        )
        attended = fold_heads([out[i] / norm[i] for i in range(3)], value_rows)
        log_total = [top[i] + jnp.log(norm[i]) for i in range(3)]
        extra = in_lanes(log_total)
        wide_ref[r * rows : (r + 1) * rows, 0:128] = attended[:, 0:128] + extra
        wide_ref[r * rows : (r + 1) * rows, 128:256] = attended[:, 128:256]
        return attended

    half = nh // 2
    for r in range(half):
        left = pltpu.roll(one_block(r), WIN - 64, axis=1)
        right = one_block(r + half)
        span = slice(r * rows, (r + 1) * rows)
        low_ref[span, 0:128] = left[:, 0:128].astype(BF16)
        low_ref[span, 128:256] = (left[:, 128:256] + right[:, 0:128]).astype(BF16)
        low_ref[span, 256:384] = right[:, 128:256].astype(BF16)


def delta_kernel(nh, wide_ref, *rest):
    slots, grad_ref = rest[:nh], rest[nh]
    rows = wide_ref.shape[0] // nh
    half = nh // 2
    value_rows = head_rows(WIN, 64, 1.0)
    every = value_rows[0] + value_rows[1] + value_rows[2]

    def one_block(r, grad):
        span = slice(r * rows, (r + 1) * rows)
        grad = (grad * every).astype(BF16).astype(F32)
        wide = wide_ref[span, :]
        product = grad * wide
        parts = []
        for i in range(3):
            parts += three_parts(wide[:, i : i + 1])
        for i in range(3):
            parts += three_parts(jnp.sum(product * value_rows[i], axis=-1, keepdims=True))
        grad_ref[span, 0:128] = (grad[:, 0:128] + in_lanes(parts)).astype(BF16)
        grad_ref[span, 128:256] = grad[:, 128:256].astype(BF16)

    for r in range(half):
        total = slots[0][r * rows : (r + 1) * rows, :].astype(F32)
        for i in range(1, nh):
            total = total + slots[i][r * rows : (r + 1) * rows, :].astype(F32)
        one_block(r, pltpu.roll(total[:, 0:WIN], 64, axis=1))
        one_block(r + half, total[:, 128 : 128 + WIN])


def query_kernel(nh, nb, count, meta, q_ref, g_ref, *rest):
    pieces, out_ref, (kv, sems) = rest[:count], rest[count], rest[count + 1 :]
    rows = q_ref.shape[0] // nh
    total = nh * nb * rows
    tile = TILE_BLOCKS * rows
    b = meta[0]
    for copy in block_copies(meta, nh, nb, pieces, row_place(kv, rows), sems):
        copy.wait()
    query_rows = head_rows(WIN, 0, HEAD_DIM**-0.5)
    value_rows = head_rows(WIN, 64, 1.0)
    for r in range(nh):
        span = slice(r * rows, (r + 1) * rows)
        first = (r * nb + b) * rows
        start, tiles = tile_bounds(meta, first, rows, total)
        low, high = row_ranges(meta, first, rows, total)
        masked = spread_heads(q_ref[span, :], query_rows)
        grads = spread_heads(g_ref[span, :], value_rows)
        stats = g_ref[span, 0:128].astype(F32)
        log_total = jnp.stack([add_parts(stats, i) for i in range(3)])
        delta = jnp.stack([add_parts(stats, 3 + i) for i in range(3)])

        def step(t, state):
            block, begin, place = tile_at(start, t, rows, total)
            allowed = (place >= jnp.maximum(low, begin)) & (place < high)
            parts = []
            for first_one, count_now in TILE_PARTS:
                keys = kv[pl.ds(block + first_one, count_now), :, 0:WIN].reshape(-1, WIN)
                values = kv[pl.ds(block + first_one, count_now), :, 128 : 128 + WIN].reshape(-1, WIN)
                scores = mat(masked, keys, CONTRACT_LAST)
                parts.append((keys, scores, mat(grads, values, CONTRACT_LAST)))
            for (first_one, count_now), (keys, scores, grad_probs) in zip(TILE_PARTS, parts):
                inside = allowed[:, first_one * rows : (first_one + count_now) * rows]
                scores = scores.reshape(3, rows, count_now * rows)
                grad_probs = grad_probs.reshape(3, rows, count_now * rows)
                probs = jnp.exp(jnp.where(inside[None], scores, neg_fill) - log_total)
                grad_scores = (probs * (grad_probs - delta)).astype(BF16)
                part = mat(grad_scores.reshape(3 * rows, count_now * rows), keys)
                state = state + part.reshape(3, rows, WIN)
            return state

        total_grad = lax.fori_loop(0, tiles, step, jnp.zeros((3, rows, WIN), F32))
        out_ref[span, :] = fold_heads(total_grad, query_rows).astype(BF16)


def key_kernel(nh, nb, counts, meta, kv_ref, *rest):
    both = counts[0] + counts[1]
    q_in, g_in, out_ref = rest[: counts[0]], rest[counts[0] : both], rest[both]
    queries_all, grads_all, q_sems, g_sems = rest[both + 1 :]
    rows = kv_ref.shape[0] // nh
    total = nh * nb * rows
    tile = TILE_BLOCKS * rows
    b = meta[0]
    copies = block_copies(meta, nh, nb, q_in, row_place(queries_all, rows), q_sems)
    copies += block_copies(meta, nh, nb, g_in, row_place(grads_all, rows), g_sems)
    for copy in copies:
        copy.wait()
    key_rows = head_rows(WIN, 0, HEAD_DIM**-0.5)
    value_rows = head_rows(WIN, 64, 1.0)
    line = lax.broadcasted_iota(jnp.int32, (8, WIN), 0) * 3
    lane = lax.broadcasted_iota(jnp.int32, (8, WIN), 1)
    choose = jnp.where((lane >= line) & (lane < line + 3), 1.0, 0.0).astype(BF16)
    for r in range(nh):
        span = slice(r * rows, (r + 1) * rows)
        first = (r * nb + b) * rows
        start, tiles = tile_bounds(meta, first, rows, total)
        low, high = row_ranges(meta, first, rows, total)
        keys = spread_heads(kv_ref[span, 0:WIN], key_rows)
        values = spread_heads(kv_ref[span, 128 : 128 + WIN], value_rows)

        def step(t, state):
            grad_keys, grad_values = state
            block, begin, place = tile_at(start, t, rows, total)
            allowed = (place >= jnp.maximum(low, begin)) & (place < high)
            parts = []
            for first_one, count_now in TILE_PARTS:
                queries = queries_all[pl.ds(block + first_one, count_now)].reshape(-1, WIN)
                grads = grads_all[pl.ds(block + first_one, count_now)].reshape(-1, WIN)
                stats = mat(choose, grads, CONTRACT_LAST)
                scores = mat(keys, queries, CONTRACT_LAST)
                parts.append((queries, grads, stats, scores, mat(values, grads, CONTRACT_LAST)))
            for (first_one, count_now), (queries, grads, stats, scores, grad_probs) in zip(TILE_PARTS, parts):
                inside = allowed[:, first_one * rows : (first_one + count_now) * rows]
                scores = scores.reshape(3, rows, count_now * rows)
                grad_probs = grad_probs.reshape(3, rows, count_now * rows)
                log_total = jnp.stack([stats[i : i + 1] for i in range(3)])
                delta = jnp.stack([stats[3 + i : 4 + i] for i in range(3)])
                probs = jnp.exp(jnp.where(inside[None], scores, neg_fill) - log_total)
                grad_scores = (probs * (grad_probs - delta)).astype(BF16)
                part_value = mat(probs.astype(BF16).reshape(3 * rows, count_now * rows), grads)
                part_key = mat(grad_scores.reshape(3 * rows, count_now * rows), queries)
                grad_keys = grad_keys + part_key.reshape(3, rows, WIN)
                grad_values = grad_values + part_value.reshape(3, rows, WIN)
            return grad_keys, grad_values

        zero = jnp.zeros((3, rows, WIN), F32)
        grad_keys, grad_values = lax.fori_loop(0, tiles, step, (zero, zero))
        key_out = fold_heads(grad_keys, key_rows)
        value_out = fold_heads(grad_values, value_rows)
        out_ref[span, 0:128] = key_out[:, 0:128].astype(BF16)
        out_ref[span, 128:256] = (key_out[:, 128:256] + value_out[:, 0:128]).astype(BF16)
        out_ref[span, 256:384] = value_out[:, 128:256].astype(BF16)


SMEM_SPEC = pl.BlockSpec(memory_space=pltpu.SMEM)
VMEM_SPEC = pl.BlockSpec(memory_space=pltpu.VMEM)
ANY_SPEC = pl.BlockSpec(memory_space=pl.ANY)


def kernel_params():
    return pltpu.CompilerParams(vmem_limit_bytes=56 * 1024 * 1024)


def cost(matmuls, nh, nb, rows):
    flops = matmuls * 2 * 3 * rows * WIN * 1 * TILE_BLOCKS * rows * nh
    return pl.CostEstimate(flops=flops, bytes_accessed=nh * nb * rows * 384 * 2, transcendentals=0)


def attend(meta, queries, pieces, nh, nb):
    length = queries.shape[0]
    rows = length // nh
    count = len(pieces)
    return pl.pallas_call(
        functools.partial(forward_kernel, nh, nb, count),
        out_shape=(
            jax.ShapeDtypeStruct((length, WIN), F32),
            jax.ShapeDtypeStruct((length // 2, 384), BF16),
        ),
        in_specs=[SMEM_SPEC, VMEM_SPEC] + [ANY_SPEC] * count,
        out_specs=(VMEM_SPEC,) * 2,
        scratch_shapes=[
            pltpu.VMEM((nh * nb, rows, 384), BF16),
            pltpu.SemaphoreType.DMA((nb, nh)),
        ],
        compiler_params=kernel_params(),
        cost_estimate=cost(2, nh, nb, rows),
        name="attend",
    )(meta, queries, *pieces)


def delta_rows(wide, slots):
    nh = len(slots)
    return pl.pallas_call(
        functools.partial(delta_kernel, nh),
        out_shape=jax.ShapeDtypeStruct(wide.shape, BF16),
        in_specs=[VMEM_SPEC] * (1 + nh),
        out_specs=VMEM_SPEC,
        compiler_params=kernel_params(),
        name="delta",
    )(wide, *slots)


def middle_kernel(
    nh, place, att_ref, x_ref, cot_ref, wo_ref, up_ref, down_ref, line_ref, joined_ref, own_ref, a2_ref, act_ref,
    hid_ref, low_ref, grad_ref, sum_ref, *rest
):
    outs, (mid, wide, packed) = rest[:nh], rest[nh:]
    h = place[0]
    length, width = x_ref.shape
    half = length // 2
    rows = length // nh
    group = width // nh
    lane = lax.broadcasted_iota(jnp.int32, (1, 128), 1)
    left = jnp.where(lane < 64, 1.0, 0.0).astype(F32)
    right = 1.0 - left
    for side in range(2):
        span = slice(side * half, (side + 1) * half)
        for pair in range(nh // 2):
            first = att_ref[2 * pair, :, 128 * side : 128 * side + WIN].astype(F32)
            second = att_ref[2 * pair + 1, :, 128 * side : 128 * side + WIN].astype(F32)
            if side == 0:
                second = pltpu.roll(second, 64, axis=1)
            else:
                first = pltpu.roll(first, WIN - 64, axis=1)
            at = 2 * pair * group
            joined_ref[span, at : at + 128] = first[:, 0:128].astype(BF16)
            joined_ref[span, at + 128 : at + 256] = (first[:, 128:256] * left + second[:, 0:128] * right).astype(BF16)
            joined_ref[span, at + 256 : at + 384] = second[:, 128:256].astype(BF16)
    out_bias, gain, shift, up_bias = (line_ref[i : i + 1, :] for i in range(4))
    sum_ref[...] = jnp.zeros(sum_ref.shape, F32)

    def mean(value):
        return jnp.mean(value, axis=-1, keepdims=True)

    def one_half(side, carry):
        span = pl.ds(pl.multiple_of(side * half, half), half)
        middle = x_ref[span, :].astype(F32) + (mat(joined_ref[span, :], wo_ref[...]) + out_bias)
        mid[span, :] = middle
        normed, inv_spread = norm_parts(middle)
        second_low = (normed * gain + shift).astype(BF16)
        a2_ref[span, :] = second_low
        active, slope = gelu_pair(mat(second_low, up_ref[...]) + up_bias)
        act_ref[span, :] = active.astype(BF16)
        cot = cot_ref[span, :]
        grad_hidden = (mat(cot, down_ref[...], CONTRACT_LAST) * slope).astype(BF16)
        hid_ref[span, :] = grad_hidden
        grad_second = mat(grad_hidden, up_ref[...], CONTRACT_LAST)
        row = side * half + lax.broadcasted_iota(jnp.int32, (half, 1), 0)
        is_own = (row >= h * rows) & (row < (h + 1) * rows)
        grad_middle = norm_pull(grad_second, normed, inv_spread, gain)
        grad_middle = grad_middle + jnp.where(is_own, cot.astype(F32), 0.0)
        grad_ref[span, :] = grad_middle
        low = grad_middle.astype(BF16)
        low_ref[span, :] = low
        wide[span, :] = mat(low, wo_ref[...], CONTRACT_LAST)
        sum_ref[0:1, :] += jnp.sum(low.astype(F32), axis=0, keepdims=True)
        sum_ref[1:2, :] += jnp.sum(grad_second * normed, axis=0, keepdims=True)
        sum_ref[2:3, :] += jnp.sum(grad_second, axis=0, keepdims=True)
        sum_ref[3:4, :] += jnp.sum(grad_hidden.astype(F32), axis=0, keepdims=True)
        return carry

    lax.fori_loop(0, 2, one_half, 0)
    own_ref[...] = mid[pl.ds(pl.multiple_of(h * rows, rows), rows), :]
    for g in range(nh):
        shift_now = g * group % 128
        at = g * group - shift_now
        top = wide[0:half, at : at + WIN]
        if shift_now:
            top = pltpu.roll(top, WIN - shift_now, axis=1)
        bottom = wide[half:length, at : at + WIN]
        if shift_now != 64:
            bottom = pltpu.roll(bottom, 64 - shift_now, axis=1)
        packed[g, :, 0:128] = top[:, 0:128].astype(BF16)
        packed[g, :, 128:256] = (top[:, 128:256] * left + bottom[:, 0:128] * right).astype(BF16)
        packed[g, :, 256:384] = bottom[:, 128:256].astype(BF16)
    for r in range(nh):
        outs[r][...] = packed[lax.rem(h - r + nh, nh)]


def middle_stage(place, attended, tokens, cot, wo, up, down, lines, nh):
    length, width = tokens.shape
    full = jax.ShapeDtypeStruct((length, width), BF16)
    piece = jax.ShapeDtypeStruct(attended.shape[1:], BF16)
    shapes = (
        full,
        jax.ShapeDtypeStruct((length // nh, width), F32),
        full,
        full,
        full,
        full,
        jax.ShapeDtypeStruct((length, width), F32),
        jax.ShapeDtypeStruct((8, width), F32),
    ) + (piece,) * nh
    return pl.pallas_call(
        functools.partial(middle_kernel, nh),
        out_shape=shapes,
        in_specs=[SMEM_SPEC] + [VMEM_SPEC] * 7,
        out_specs=(VMEM_SPEC,) * len(shapes),
        scratch_shapes=[
            pltpu.VMEM((length, width), F32),
            pltpu.VMEM((length, width), F32),
            pltpu.VMEM(attended.shape, BF16),
        ],
        compiler_params=kernel_params(),
        cost_estimate=pl.CostEstimate(flops=12 * length * width * width, bytes_accessed=12 * 2**20, transcendentals=0),
        name="middle",
    )(place, attended, tokens, cot, wo, up, down, lines)


def query_grads(meta, queries, grads, pieces, nh, nb):
    length = queries.shape[0]
    rows = length // nh
    count = len(pieces)
    return pl.pallas_call(
        functools.partial(query_kernel, nh, nb, count),
        out_shape=jax.ShapeDtypeStruct((length, WIN), BF16),
        in_specs=[SMEM_SPEC] + [VMEM_SPEC] * 2 + [ANY_SPEC] * count,
        out_specs=VMEM_SPEC,
        scratch_shapes=[
            pltpu.VMEM((nh * nb, rows, 384), BF16),
            pltpu.SemaphoreType.DMA((nb, nh)),
        ],
        compiler_params=kernel_params(),
        cost_estimate=cost(3, nh, nb, rows),
        name="query_grads",
    )(meta, queries, grads, *pieces)


def key_grads(meta, own, queries, grads, nh, nb):
    length = own.shape[0]
    rows = length // nh
    counts = (len(queries), len(grads))
    return pl.pallas_call(
        functools.partial(key_kernel, nh, nb, counts),
        out_shape=jax.ShapeDtypeStruct((length, 384), BF16),
        in_specs=[SMEM_SPEC, VMEM_SPEC] + [ANY_SPEC] * sum(counts),
        out_specs=VMEM_SPEC,
        scratch_shapes=[
            pltpu.VMEM((nh * nb, rows, WIN), BF16),
            pltpu.VMEM((nh * nb, rows, WIN), BF16),
            pltpu.SemaphoreType.DMA((nb, nh)),
            pltpu.SemaphoreType.DMA((nb, nh)),
        ],
        compiler_params=kernel_params(),
        cost_estimate=cost(4, nh, nb, rows),
        name="key_grads",
    )(meta, own, *queries, *grads)


def gather_blk_rows(here):
    if lax.axis_size("blk") != 8:
        whole = lax.all_gather(here, "blk", axis=0, tiled=False)
        return jnp.moveaxis(whole, 0, 1).reshape(-1, here.shape[-1])
    b = lax.axis_index("blk")
    core, x_bit, y_bit = b & 1, (b >> 1) & 1, b >> 2
    side, up, cross = swap(here, 2), swap(here, 4), swap(here, 6)
    square = in_pair(y_bit, in_pair(x_bit, here, side), in_pair(x_bit, up, cross))
    whole = in_pair(core, square, swap(square, 1))
    return whole.transpose(3, 1, 2, 0, 4, 5).reshape(-1, here.shape[-1])


def scatter_blk_rows(grad, nh, nb, late):
    width = grad.shape[-1]
    if nb != 8:
        parts = grad.reshape(nh, nb, -1, width)
        return lax.psum_scatter(parts, "blk", scatter_dimension=1, tiled=False).astype(BF16), late
    b = lax.axis_index("blk")
    core, x_bit, y_bit = b & 1, (b >> 1) & 1, b >> 2
    parts = grad.astype(BF16).reshape(nh, 2, 2, 2, -1, width)
    sent = swap(pick(parts, 1 - core, 3), 1)
    chip = (pick(parts, core, 3).astype(F32) + sent.astype(F32)).astype(BF16)
    chip, late = after((chip, late))

    def part(y, x):
        return pick(pick(chip, y, 1), x, 1)

    side = swap(part(y_bit, 1 - x_bit), 2)
    up = swap(part(1 - y_bit, x_bit), 4)
    cross = swap(part(1 - y_bit, 1 - x_bit), 6)
    mine = part(y_bit, x_bit).astype(F32) + side.astype(F32)
    return (mine + up.astype(F32) + cross.astype(F32)).astype(BF16), late


def shards(
    tokens,
    cotangent,
    doc_starts,
    norm_gain,
    norm_shift,
    triple_weight,
    query_bias,
    value_bias,
    output_weight,
    output_bias,
    final_gain,
    final_shift,
    up_weight,
    up_bias,
    down_weight,
    down_bias,
):
    nh = lax.axis_size("head")
    nb = lax.axis_size("blk")
    h = lax.axis_index("head")
    b = lax.axis_index("blk")
    rows, width = tokens.shape
    part = norm_gain.shape[0]
    group = HEADS // nh * HEAD_DIM
    ff_part = up_bias.shape[0]
    ff_group = nb * ff_part
    extra = max(part, 12)
    meta = jnp.concatenate([b.astype(jnp.int32)[None], doc_starts])

    packed = jnp.stack(
        [
            norm_gain,
            norm_shift,
            query_bias,
            value_bias,
            output_bias,
            final_gain,
            final_shift,
            down_bias,
        ]
    )
    packed = jnp.concatenate([packed, up_bias.reshape(4, part)], axis=0)
    if extra > 12:
        packed = jnp.pad(packed, ((0, extra - 12), (0, 0)))
    columns = triple_weight.reshape(part, 3, nh, group)
    pieces = [columns[:, 1], columns[:, 2], columns[:, 0]]
    if part == extra:
        pieces.append(jnp.broadcast_to(packed[:, None], (part, nh, part)))
    pieces.append(up_weight.reshape(part, nh, ff_group))
    pieces.append(jnp.broadcast_to(output_weight[:, None], (part, nh, width)))
    columns = exchange(jnp.concatenate(pieces, axis=-1).transpose(1, 0, 2))
    token_rows = spread(tokens).reshape(nh * rows, width)
    first_width = 3 * group + (part if part == extra else 0)
    group_weight = gather_blk_rows(columns[..., :first_width])

    late = jnp.concatenate(
        [
            columns[..., first_width : first_width + ff_group].reshape(-1, ff_group),
            down_weight,
            columns[..., first_width + ff_group :].reshape(-1, width),
        ],
        axis=0,
    )
    if part == extra:
        vectors = group_weight[:, 3 * group :].reshape(nh * nb, extra, part)[:, :12]
    else:
        vectors = lax.all_gather(packed, ("head", "blk"), axis=0, tiled=False)
    group_weight = group_weight[:, : 3 * group]
    lines = vectors[:, :8].transpose(1, 0, 2).reshape(8, width).astype(F32)
    gain_one, shift_one, query_all, value_all, out_bias, gain_two, shift_two, down_bias_all = (
        lines[i] for i in range(8)
    )
    up_bias_own = pick(vectors[:, 8:].reshape(nh, nb * ff_part), h, 0).astype(F32)

    key_value_weight = group_weight[:, : 2 * group]
    query_weight = jnp.pad(group_weight[:, 2 * group :], ((0, 0), (0, WIN - group)))
    token_wide = token_rows.astype(F32)
    normed_one, spread_one = norm_parts(token_wide)
    first_low = (normed_one * gain_one + shift_one).astype(BF16)
    value_bias_own = lax.dynamic_slice_in_dim(value_all, h * group, group)
    query_bias_own = lax.dynamic_slice_in_dim(query_all, h * group, group)
    kv_bias = jnp.concatenate([jnp.zeros((group,), F32), value_bias_own])
    key_values = (mat(first_low, key_value_weight) + kv_bias).astype(BF16)
    kv_pieces = gather_pieces(key_values)
    q_bias = jnp.pad(query_bias_own, (0, WIN - group))
    queries = (mat(first_low, query_weight) + q_bias).astype(BF16)
    late = lax.all_gather(after(late, kv_pieces[1 if nb == 8 else 0]), "blk", axis=0, tiled=False)
    up_own = jnp.moveaxis(late[:, : nh * part].reshape(nb, nh, part, ff_group), 0, 1)
    up_own = up_own.reshape(width, ff_group)
    down_own = late[:, nh * part : nh * part + ff_part].reshape(ff_group, width)
    out_own = jnp.moveaxis(late[:, nh * part + ff_part :].reshape(nb, nh, part, width), 0, 1)
    out_own = out_own.reshape(width, width)
    slow = jnp.concatenate([cotangent, jnp.zeros((rows // 8 * 3, width), BF16)], axis=0)
    slow = lax.all_gather(after(slow, token_rows), "head", axis=0, tiled=False)
    cot_all = slow[:, :rows].reshape(nh * rows, width)
    wide, attended = attend(meta, queries, kv_pieces, nh, nb)
    query_pieces = [lax.all_gather(after(queries, attended), "blk", axis=0, tiled=False)]

    lines_two = jnp.stack([out_bias, gain_two, shift_two, up_bias_own])
    head_slots = [attended] + [turn(attended, r) for r in range(1, nh)]
    head_slots, out_own, up_own, down_own = after((head_slots, out_own, up_own, down_own))
    (
        joined,
        output_own,
        second_low,
        active_low,
        grad_hidden,
        branch_grad,
        grad_middle,
        middle_sums,
        *grad_slots,
    ) = middle_stage(
        h.astype(jnp.int32)[None], by_head(head_slots), token_rows, cot_all, out_own, up_own, down_own, lines_two, nh
    )
    for r in range(1, nh):
        grad_slots[r] = turn(grad_slots[r], -r)

    branch_late, joined_late = branch_grad, joined
    cot_late, second_late, grad_slots[1] = after((cot_all, second_low, grad_slots[1]))
    output_part = mat(active_low, down_own).astype(BF16).reshape(nh, rows, width)
    grad_up_own = mat(second_late, grad_hidden, CONTRACT_FIRST).astype(BF16)
    grad_down_own = mat(active_low, cot_late, CONTRACT_FIRST).astype(BF16)
    grad_out = mat(joined_late, branch_late, CONTRACT_FIRST).astype(BF16).reshape(nh, nb, part, width)
    late_grads = jnp.concatenate(
        [
            jnp.moveaxis(grad_up_own.reshape(nh, nb, part, ff_group), 0, 1).reshape(nb, -1, width),
            grad_down_own.reshape(nb, ff_part, width),
            jnp.moveaxis(grad_out, 0, 1).reshape(nb, -1, width),
        ],
        axis=1,
    )
    late_sums = lax.psum_scatter(late_grads, "blk", scatter_dimension=0, tiled=False)

    grad_attended = delta_rows(wide, after(grad_slots, late_grads, output_part))
    grad_queries = query_grads(meta, queries, grad_attended, kv_pieces, nh, nb)
    grad_pieces = gather_pieces(grad_attended, grad_queries)
    output_blocks = exchange(after(output_part, grad_attended))
    query_pieces[0], output_blocks = after((query_pieces[0], output_blocks))
    grad_key_values = key_grads(meta, key_values, query_pieces, grad_pieces, nh, nb)

    grad_group = jnp.concatenate([grad_key_values, grad_queries[:, :group]], axis=1)
    first_part = mat(grad_group, group_weight, CONTRACT_LAST)
    grad_in = grad_middle + norm_pull(first_part, normed_one, spread_one, gain_one)
    grad_in = grad_in.astype(BF16).reshape(nh, rows, width)
    output_sum = jnp.sum(output_blocks.astype(F32), axis=0)
    output_rows = (output_own + output_sum + down_bias_all).astype(BF16)
    row_sums = pick(grad_in, h, 0).astype(F32)
    for r in range(1, nh):
        row_sums = row_sums + turn(pick(grad_in, lax.rem(h - r + nh, nh), 0), -r).astype(F32)
    first_late, grad_group = after((first_low, grad_group), grad_in)
    grad_triple_part = mat(first_late, grad_group, CONTRACT_FIRST).astype(BF16)

    group_sums = jnp.sum(grad_group.astype(F32), axis=0)
    placed = jnp.where(
        jnp.arange(nh)[None, :, None] == h,
        jnp.stack([group_sums[2 * group :], group_sums[group : 2 * group]])[:, None],
        0.0,
    ).reshape(2, width)
    up_b = middle_sums[3]
    up_b = jnp.where(jnp.arange(nh)[:, None] == h, up_b[None], 0.0).reshape(nh * nb, 4, part)
    sums = jnp.stack(
        [
            jnp.sum(first_part * normed_one, axis=0),
            jnp.sum(first_part, axis=0),
            placed[0],
            placed[1],
            middle_sums[0],
            middle_sums[1],
            middle_sums[2],
            jnp.sum(cotangent.astype(F32), axis=0),
        ]
    )
    sums = sums.reshape(8, nh * nb, part).transpose(1, 0, 2)
    sums = jnp.concatenate([sums, up_b], axis=1)
    if part == extra:
        low_sums = jnp.pad(sums.astype(BF16), ((0, 0), (0, extra - 12), (0, 0)))
        low_sums = low_sums.reshape(width, part)
        grad_triple_part = jnp.concatenate([grad_triple_part, low_sums], axis=1)
    else:
        sums = lax.psum(sums, ("head", "blk"))
        sums = pick(sums, h * nb + b, 0)
    here, late_sums = scatter_blk_rows(grad_triple_part, nh, nb, late_sums)
    sum_down_w = late_sums[nh * part : nh * part + ff_part].astype(F32)
    final = [
        here,
        late_sums[: nh * part].reshape(nh, part, ff_group),
        late_sums[nh * part + ff_part :].reshape(nh, part, width),
    ]
    final = jnp.concatenate(final, axis=-1)
    slots = [pick(final, h, 0)]
    for r in range(1, nh):
        slots.append(turn(pick(final, lax.rem(h - r + nh, nh), 0), -r))
    slots, row_sums = after((slots, row_sums))
    input_grad = row_sums.astype(BF16)
    final = by_group(slots).astype(F32)
    if part == extra:
        sums = jnp.sum(final[:, :12, 3 * group : first_width], axis=0)
    sum_triple = jnp.concatenate(
        [
            final[:, :, 2 * group : 3 * group].transpose(1, 0, 2).reshape(part, width),
            final[:, :, :group].transpose(1, 0, 2).reshape(part, width),
            final[:, :, group : 2 * group].transpose(1, 0, 2).reshape(part, width),
        ],
        axis=1,
    )
    sum_up_w = final[:, :, first_width : first_width + ff_group]
    sum_up_w = sum_up_w.transpose(1, 0, 2).reshape(part, nh * ff_group)
    sum_out_w = jnp.sum(final[:, :, first_width + ff_group :], axis=0)
    return (
        output_rows,
        input_grad,
        sums[0],
        sums[1],
        sum_triple,
        sums[2],
        sums[3],
        sum_out_w,
        sums[4],
        sums[5],
        sums[6],
        sum_up_w,
        sums[8:].reshape(ff_part),
        sum_down_w,
        sums[7],
    )


def solution(mesh):
    wide = P(("head", "blk"), None)
    thin = P(("head", "blk"))
    in_specs = (
        wide,
        wide,
        P(),
        thin,
        thin,
        wide,
        thin,
        thin,
        wide,
        thin,
        thin,
        thin,
        wide,
        thin,
        wide,
        thin,
    )
    out_specs = (
        wide,
        wide,
        thin,
        thin,
        wide,
        thin,
        thin,
        wide,
        thin,
        thin,
        thin,
        wide,
        thin,
        wide,
        thin,
    )
    return jax.shard_map(shards, mesh=mesh, in_specs=in_specs, out_specs=out_specs, check_vma=False)
```

```python
import functools

import jax
import jax.numpy as jnp
from jax import lax
from jax.experimental import pallas as pl
from jax.experimental.pallas import tpu as pltpu
from jax.sharding import PartitionSpec as P

HEADS = 12
HEAD_DIM = 64

epsilon = 1e-06
neg_fill = -1e30
root_half = 0.7071067811865476
inv_root_two_pi = 0.3989422804014327

F32 = jnp.float32
BF16 = jnp.bfloat16
WIN = 256
TILE_BLOCKS = 6
TILE_PARTS = ((0, 4), (4, 2))
CONTRACT_LAST = (((1,), (1,)), ((), ()))
FORWARD_BLOCKS = 6
CONTRACT_FIRST = (((0,), (0,)), ((), ()))
PLAIN = (((1,), (0,)), ((), ()))


def norm_parts(values):
    centre = jnp.mean(values, axis=-1, keepdims=True)
    offset = values - centre
    inv_spread = lax.rsqrt(jnp.mean(offset * offset, axis=-1, keepdims=True) + epsilon)
    return (offset * inv_spread, inv_spread)


def norm_pull(grad_out, normed, inv_spread, gain_full):
    grad_normed = grad_out * gain_full
    return inv_spread * (
        grad_normed
        - jnp.mean(grad_normed, axis=-1, keepdims=True)
        - normed * jnp.mean(grad_normed * normed, axis=-1, keepdims=True)
    )


def gelu_pair(hidden):
    normal_cdf = 0.5 * (1.0 + lax.erf(hidden * root_half))
    return (
        hidden * normal_cdf,
        normal_cdf + hidden * inv_root_two_pi * jnp.exp(-0.5 * hidden * hidden),
    )


def mat(left, right, dims=PLAIN):
    return lax.dot_general(left, right, dims, preferred_element_type=F32)


def exchange(x):
    return lax.all_to_all(x, "head", 0, 0, tiled=True)


def share(x):
    return exchange(jnp.broadcast_to(x[None], (lax.axis_size("head"),) + x.shape))


def turn(x, step):
    size = lax.axis_size("head")
    return lax.ppermute(x, "head", [(i, (i + step) % size) for i in range(size)])


def by_head(slots):
    size = len(slots)
    doubled = jnp.stack([slots[(size - 1 - i) % size] for i in range(2 * size - 1)])
    return lax.dynamic_slice_in_dim(doubled, size - 1 - lax.axis_index("head"), size, 0)


def spread(x):
    return by_head([x] + [turn(x, r) for r in range(1, lax.axis_size("head"))])


def by_group(slots):
    size = len(slots)
    doubled = jnp.stack([slots[i % size] for i in range(2 * size - 1)])
    start = lax.rem(size - lax.axis_index("head"), size)
    return lax.dynamic_slice_in_dim(doubled, start, size, 0)


def swap(x, bits):
    size = lax.axis_size("blk")
    return lax.ppermute(x, "blk", [(i, i ^ bits) for i in range(size)])


def in_pair(bit, mine, other):
    return jnp.where(bit == 0, jnp.stack([mine, other]), jnp.stack([other, mine]))


def pick(x, index, axis):
    return lax.dynamic_index_in_dim(x, index, axis, keepdims=False)


def after(value, *earlier):
    flat, tree = jax.tree.flatten(value)
    held = lax.optimization_barrier((tuple(flat), earlier))[0]
    return jax.tree.unflatten(tree, held)


def gather_pieces(x, *earlier):
    if lax.axis_size("blk") != 8:
        return [lax.all_gather(x, "blk", axis=0, tiled=False)]
    pieces = [None] * 8
    pieces[0] = x
    for bits in (2, 4, 6):
        pieces[bits] = swap(x, bits)
    for bits in (0, 2, 4, 6):
        pieces[bits + 1] = swap(after(pieces[bits], *earlier) if bits else x, 1)
    return pieces


def doc_range(meta, first, last, total):
    low, high = jnp.int32(0), jnp.int32(total)
    for i in range(meta.shape[0] - 1):
        start = meta[1 + i]
        low = jnp.where(start <= first, start, low)
        high = jnp.where(start > last, jnp.minimum(high, start), high)
    return low, high


def row_ranges(meta, first, rows, total):
    place = first + lax.broadcasted_iota(jnp.int32, (rows, 1), 0)
    low = jnp.zeros((rows, 1), jnp.int32)
    high = jnp.full((rows, 1), total, jnp.int32)
    for i in range(meta.shape[0] - 1):
        start = meta[1 + i]
        low = jnp.where(place >= start, start, low)
        high = jnp.where(place < start, jnp.minimum(high, start), high)
    return low, high


def head_rows(width, shift, scale):
    lane = lax.broadcasted_iota(jnp.int32, (1, width), 1)
    return [
        jnp.where((lane >= shift + 64 * i) & (lane < shift + 64 * (i + 1)), scale, 0.0).astype(F32)
        for i in range(3)
    ]


def spread_heads(block, rows):
    wide = block.astype(F32)
    return jnp.concatenate([wide * row for row in rows], axis=0).astype(BF16)


def block_of(stack, i, rows):
    return stack[i * rows : (i + 1) * rows]


def fold_heads(stack, rows):
    return stack[0] * rows[0] + stack[1] * rows[1] + stack[2] * rows[2]


def block_copies(meta, nh, nb, pieces, place, sems):
    b = meta[0]
    copies = []
    if len(pieces) == nb:
        for m, piece in enumerate(pieces):
            for r in range(nh):
                block = r * nb + jnp.bitwise_xor(b, m)
                copies.append(pltpu.make_async_copy(*place(piece, None, r, block), sems.at[m, r]))
        for copy in copies:
            copy.start()
        return copies

    def run(which):
        def one(i, carry):
            for r in range(nh):
                block = r * nb + i
                copy = pltpu.make_async_copy(*place(pieces[0], i, r, block), sems.at[i, r])
                (copy.start if which == 0 else copy.wait)()
            return carry

        lax.fori_loop(0, nb, one, 0)

    run(0)

    class Rest:
        def wait(self):
            run(1)

    return [Rest()]


def row_place(target, rows):
    def place(piece, index, r, block):
        source = piece if index is None else piece.at[index]
        return source.at[pl.ds(r * rows, rows), :], target.at[block]

    return place


def tile_bounds(meta, first, rows, total, blocks=TILE_BLOCKS):
    low, high = doc_range(meta, first, first + rows - 1, total)
    start = lax.div(low, rows)
    tile = blocks * rows
    return start, lax.div(high - start * rows + tile - 1, tile)


def tile_at(start, t, rows, total, blocks=TILE_BLOCKS):
    begin = start + t * blocks
    block = jnp.minimum(begin, total // rows - blocks)
    place = block * rows + lax.broadcasted_iota(jnp.int32, (1, blocks * rows), 1)
    return block, begin * rows, place


def lane_is(index):
    lane = lax.broadcasted_iota(jnp.int32, (1, 128), 1)
    return jnp.where(lane == index, 1.0, 0.0).astype(F32)


def in_lanes(columns):
    total = columns[0] * lane_is(0)
    for i in range(1, len(columns)):
        total = total + columns[i] * lane_is(i)
    return total


def in_parts(block):
    high = block.astype(BF16).astype(F32)
    middle = (block - high).astype(BF16).astype(F32)
    low = (block - high - middle).astype(BF16).astype(F32)
    return high + pltpu.roll(middle, 8, axis=1) + pltpu.roll(low, 16, axis=1)


def add_parts(block, lane):
    return block[:, lane : lane + 1] + block[:, lane + 8 : lane + 9] + block[:, lane + 16 : lane + 17]


def forward_kernel(nh, nb, count, meta, q_ref, *rest):
    pieces, (wide_ref, low_ref), (kv, sems) = rest[:count], rest[count : count + 2], rest[count + 2 :]
    rows = q_ref.shape[0] // nh
    total = nh * nb * rows
    tile = FORWARD_BLOCKS * rows
    b = meta[0]
    for copy in block_copies(meta, nh, nb, pieces, row_place(kv, rows), sems):
        copy.wait()
    query_rows = head_rows(WIN, 0, HEAD_DIM**-0.5)
    value_rows = head_rows(WIN, 64, 1.0)

    def one_block(r):
        first = (r * nb + b) * rows
        start, tiles = tile_bounds(meta, first, rows, total, FORWARD_BLOCKS)
        low, high = row_ranges(meta, first, rows, total)
        masked = spread_heads(q_ref[r * rows : (r + 1) * rows, :], query_rows)

        def step(t, state):
            top, norm, out = state
            block, begin, place = tile_at(start, t, rows, total, FORWARD_BLOCKS)
            keys = kv[pl.ds(block, FORWARD_BLOCKS), :, 0:WIN].reshape(tile, WIN)
            values = kv[pl.ds(block, FORWARD_BLOCKS), :, 128 : 128 + WIN].reshape(tile, WIN)
            allowed = (place >= jnp.maximum(low, begin)) & (place < high)
            scores = [mat(block_of(masked, i, rows), keys, CONTRACT_LAST) for i in range(3)]
            result = []
            for i in range(3):
                score = jnp.where(allowed, scores[i], neg_fill)
                new_top = jnp.maximum(top[i], jnp.max(score, axis=-1, keepdims=True))
                weights = jnp.exp(score - new_top)
                factor = jnp.exp(top[i] - new_top)
                new_norm = norm[i] * factor + jnp.sum(weights, axis=-1, keepdims=True)
                result.append((new_top, new_norm, out[i] * factor + mat(weights.astype(BF16), values)))
            return tuple(zip(*result))

        top, norm, out = lax.fori_loop(
            0,
            tiles,
            step,
            (
                (jnp.full((rows, 1), neg_fill, F32),) * 3,
                (jnp.zeros((rows, 1), F32),) * 3,
                (jnp.zeros((rows, WIN), F32),) * 3,
            ),
        )
        attended = fold_heads([out[i] / norm[i] for i in range(3)], value_rows)
        log_total = [top[i] + jnp.log(norm[i]) for i in range(3)]
        extra = in_lanes(log_total)
        wide_ref[r * rows : (r + 1) * rows, 0:128] = attended[:, 0:128] + extra
        wide_ref[r * rows : (r + 1) * rows, 128:256] = attended[:, 128:256]
        return attended

    half = nh // 2
    for r in range(half):
        left = pltpu.roll(one_block(r), WIN - 64, axis=1)
        right = one_block(r + half)
        span = slice(r * rows, (r + 1) * rows)
        low_ref[span, 0:128] = left[:, 0:128].astype(BF16)
        low_ref[span, 128:256] = (left[:, 128:256] + right[:, 0:128]).astype(BF16)
        low_ref[span, 256:384] = right[:, 128:256].astype(BF16)


def delta_kernel(nh, wide_ref, *rest):
    slots, grad_ref = rest[:nh], rest[nh]
    rows = wide_ref.shape[0] // nh
    half = nh // 2
    value_rows = head_rows(WIN, 64, 1.0)
    every = value_rows[0] + value_rows[1] + value_rows[2]

    def one_block(r, grad):
        span = slice(r * rows, (r + 1) * rows)
        grad = (grad * every).astype(BF16).astype(F32)
        wide = wide_ref[span, :]
        product = grad * wide
        stats = wide[:, 0:128] * (lane_is(0) + lane_is(1) + lane_is(2))
        for i in range(3):
            stats = stats + jnp.sum(product * value_rows[i], axis=-1, keepdims=True) * lane_is(3 + i)
        grad_ref[span, 0:128] = (grad[:, 0:128] + in_parts(stats)).astype(BF16)
        grad_ref[span, 128:256] = grad[:, 128:256].astype(BF16)

    for r in range(half):
        total = slots[0][r * rows : (r + 1) * rows, :].astype(F32)
        for i in range(1, nh):
            total = total + slots[i][r * rows : (r + 1) * rows, :].astype(F32)
        one_block(r, pltpu.roll(total[:, 0:WIN], 64, axis=1))
        one_block(r + half, total[:, 128 : 128 + WIN])


def query_kernel(nh, nb, count, meta, q_ref, g_ref, *rest):
    pieces, out_ref, (kv, sems) = rest[:count], rest[count], rest[count + 1 :]
    rows = q_ref.shape[0] // nh
    total = nh * nb * rows
    tile = TILE_BLOCKS * rows
    b = meta[0]
    for copy in block_copies(meta, nh, nb, pieces, row_place(kv, rows), sems):
        copy.wait()
    query_rows = head_rows(WIN, 0, HEAD_DIM**-0.5)
    value_rows = head_rows(WIN, 64, 1.0)
    for r in range(nh):
        span = slice(r * rows, (r + 1) * rows)
        first = (r * nb + b) * rows
        start, tiles = tile_bounds(meta, first, rows, total)
        low, high = row_ranges(meta, first, rows, total)
        masked = spread_heads(q_ref[span, :], query_rows)
        grads = spread_heads(g_ref[span, :], value_rows)
        stats = g_ref[span, 0:128].astype(F32)
        log_total = jnp.stack([add_parts(stats, i) for i in range(3)])
        delta = jnp.stack([add_parts(stats, 3 + i) for i in range(3)])

        def step(t, state):
            block, begin, place = tile_at(start, t, rows, total)
            allowed = (place >= jnp.maximum(low, begin)) & (place < high)
            parts = []
            for first_one, count_now in TILE_PARTS:
                keys = kv[pl.ds(block + first_one, count_now), :, 0:WIN].reshape(-1, WIN)
                values = kv[pl.ds(block + first_one, count_now), :, 128 : 128 + WIN].reshape(-1, WIN)
                scores = mat(masked, keys, CONTRACT_LAST)
                parts.append((keys, scores, mat(grads, values, CONTRACT_LAST)))
            for (first_one, count_now), (keys, scores, grad_probs) in zip(TILE_PARTS, parts):
                inside = allowed[:, first_one * rows : (first_one + count_now) * rows]
                scores = scores.reshape(3, rows, count_now * rows)
                grad_probs = grad_probs.reshape(3, rows, count_now * rows)
                probs = jnp.exp(jnp.where(inside[None], scores, neg_fill) - log_total)
                grad_scores = (probs * (grad_probs - delta)).astype(BF16)
                part = mat(grad_scores.reshape(3 * rows, count_now * rows), keys)
                state = state + part.reshape(3, rows, WIN)
            return state

        total_grad = lax.fori_loop(0, tiles, step, jnp.zeros((3, rows, WIN), F32))
        out_ref[span, :] = fold_heads(total_grad, query_rows).astype(BF16)


def key_kernel(nh, nb, counts, meta, kv_ref, *rest):
    both = counts[0] + counts[1]
    q_in, g_in, out_ref = rest[: counts[0]], rest[counts[0] : both], rest[both]
    queries_all, grads_all, q_sems, g_sems = rest[both + 1 :]
    rows = kv_ref.shape[0] // nh
    total = nh * nb * rows
    tile = TILE_BLOCKS * rows
    b = meta[0]
    copies = block_copies(meta, nh, nb, q_in, row_place(queries_all, rows), q_sems)
    copies += block_copies(meta, nh, nb, g_in, row_place(grads_all, rows), g_sems)
    for copy in copies:
        copy.wait()
    key_rows = head_rows(WIN, 0, HEAD_DIM**-0.5)
    value_rows = head_rows(WIN, 64, 1.0)
    line = lax.broadcasted_iota(jnp.int32, (8, WIN), 0)
    lane = lax.broadcasted_iota(jnp.int32, (8, WIN), 1)
    picked = (lane == line) | (lane == line + 8) | (lane == line + 16)
    choose = jnp.where(picked & (line < 6), 1.0, 0.0).astype(BF16)
    for r in range(nh):
        span = slice(r * rows, (r + 1) * rows)
        first = (r * nb + b) * rows
        start, tiles = tile_bounds(meta, first, rows, total)
        low, high = row_ranges(meta, first, rows, total)
        keys = spread_heads(kv_ref[span, 0:WIN], key_rows)
        values = spread_heads(kv_ref[span, 128 : 128 + WIN], value_rows)

        def step(t, state):
            grad_keys, grad_values = state
            block, begin, place = tile_at(start, t, rows, total)
            allowed = (place >= jnp.maximum(low, begin)) & (place < high)
            parts = []
            for first_one, count_now in TILE_PARTS:
                queries = queries_all[pl.ds(block + first_one, count_now)].reshape(-1, WIN)
                grads = grads_all[pl.ds(block + first_one, count_now)].reshape(-1, WIN)
                stats = mat(choose, grads, CONTRACT_LAST)
                scores = mat(keys, queries, CONTRACT_LAST)
                parts.append((queries, grads, stats, scores, mat(values, grads, CONTRACT_LAST)))
            for (first_one, count_now), (queries, grads, stats, scores, grad_probs) in zip(TILE_PARTS, parts):
                inside = allowed[:, first_one * rows : (first_one + count_now) * rows]
                scores = scores.reshape(3, rows, count_now * rows)
                grad_probs = grad_probs.reshape(3, rows, count_now * rows)
                log_total = jnp.stack([stats[i : i + 1] for i in range(3)])
                delta = jnp.stack([stats[3 + i : 4 + i] for i in range(3)])
                probs = jnp.exp(jnp.where(inside[None], scores, neg_fill) - log_total)
                grad_scores = (probs * (grad_probs - delta)).astype(BF16)
                part_value = mat(probs.astype(BF16).reshape(3 * rows, count_now * rows), grads)
                part_key = mat(grad_scores.reshape(3 * rows, count_now * rows), queries)
                grad_keys = grad_keys + part_key.reshape(3, rows, WIN)
                grad_values = grad_values + part_value.reshape(3, rows, WIN)
            return grad_keys, grad_values

        zero = jnp.zeros((3, rows, WIN), F32)
        grad_keys, grad_values = lax.fori_loop(0, tiles, step, (zero, zero))
        key_out = fold_heads(grad_keys, key_rows)
        value_out = fold_heads(grad_values, value_rows)
        out_ref[span, 0:128] = key_out[:, 0:128].astype(BF16)
        out_ref[span, 128:256] = (key_out[:, 128:256] + value_out[:, 0:128]).astype(BF16)
        out_ref[span, 256:384] = value_out[:, 128:256].astype(BF16)


SMEM_SPEC = pl.BlockSpec(memory_space=pltpu.SMEM)
VMEM_SPEC = pl.BlockSpec(memory_space=pltpu.VMEM)
ANY_SPEC = pl.BlockSpec(memory_space=pl.ANY)


def kernel_params():
    return pltpu.CompilerParams(vmem_limit_bytes=56 * 1024 * 1024)


def cost(matmuls, nh, nb, rows):
    flops = matmuls * 2 * 3 * rows * WIN * 1 * TILE_BLOCKS * rows * nh
    return pl.CostEstimate(flops=flops, bytes_accessed=nh * nb * rows * 384 * 2, transcendentals=0)


def attend(meta, queries, pieces, nh, nb):
    length = queries.shape[0]
    rows = length // nh
    count = len(pieces)
    return pl.pallas_call(
        functools.partial(forward_kernel, nh, nb, count),
        out_shape=(
            jax.ShapeDtypeStruct((length, WIN), F32),
            jax.ShapeDtypeStruct((length // 2, 384), BF16),
        ),
        in_specs=[SMEM_SPEC, VMEM_SPEC] + [ANY_SPEC] * count,
        out_specs=(VMEM_SPEC,) * 2,
        scratch_shapes=[
            pltpu.VMEM((nh * nb, rows, 384), BF16),
            pltpu.SemaphoreType.DMA((nb, nh)),
        ],
        compiler_params=kernel_params(),
        cost_estimate=cost(2, nh, nb, rows),
        name="attend",
    )(meta, queries, *pieces)


def delta_rows(wide, slots):
    nh = len(slots)
    return pl.pallas_call(
        functools.partial(delta_kernel, nh),
        out_shape=jax.ShapeDtypeStruct(wide.shape, BF16),
        in_specs=[VMEM_SPEC] * (1 + nh),
        out_specs=VMEM_SPEC,
        compiler_params=kernel_params(),
        name="delta",
    )(wide, *slots)


def middle_kernel(
    nh, place, att_ref, x_ref, cot_ref, wo_ref, up_ref, down_ref, line_ref, joined_ref, own_ref, a2_ref, act_ref,
    hid_ref, low_ref, grad_ref, sum_ref, *rest
):
    outs, (mid, wide, packed) = rest[:nh], rest[nh:]
    h = place[0]
    length, width = x_ref.shape
    half = length // 2
    rows = length // nh
    group = width // nh
    lane = lax.broadcasted_iota(jnp.int32, (1, 128), 1)
    left = jnp.where(lane < 64, 1.0, 0.0).astype(F32)
    right = 1.0 - left
    for side in range(2):
        span = slice(side * half, (side + 1) * half)
        for pair in range(nh // 2):
            first = att_ref[2 * pair, :, 128 * side : 128 * side + WIN].astype(F32)
            second = att_ref[2 * pair + 1, :, 128 * side : 128 * side + WIN].astype(F32)
            if side == 0:
                second = pltpu.roll(second, 64, axis=1)
            else:
                first = pltpu.roll(first, WIN - 64, axis=1)
            at = 2 * pair * group
            joined_ref[span, at : at + 128] = first[:, 0:128].astype(BF16)
            joined_ref[span, at + 128 : at + 256] = (first[:, 128:256] * left + second[:, 0:128] * right).astype(BF16)
            joined_ref[span, at + 256 : at + 384] = second[:, 128:256].astype(BF16)
    out_bias, gain, shift, up_bias = (line_ref[i : i + 1, :] for i in range(4))
    sum_ref[...] = jnp.zeros(sum_ref.shape, F32)

    def mean(value):
        return jnp.mean(value, axis=-1, keepdims=True)

    def one_half(side, carry):
        span = pl.ds(pl.multiple_of(side * half, half), half)
        middle = x_ref[span, :].astype(F32) + (mat(joined_ref[span, :], wo_ref[...]) + out_bias)
        mid[span, :] = middle
        normed, inv_spread = norm_parts(middle)
        second_low = (normed * gain + shift).astype(BF16)
        a2_ref[span, :] = second_low
        active, slope = gelu_pair(mat(second_low, up_ref[...]) + up_bias)
        act_ref[span, :] = active.astype(BF16)
        each = nh // 2
        cot = jnp.concatenate([cot_ref[side * each + i, 0:rows, :] for i in range(each)], axis=0)
        grad_hidden = (mat(cot, down_ref[...], CONTRACT_LAST) * slope).astype(BF16)
        hid_ref[span, :] = grad_hidden
        grad_second = mat(grad_hidden, up_ref[...], CONTRACT_LAST)
        row = side * half + lax.broadcasted_iota(jnp.int32, (half, 1), 0)
        is_own = (row >= h * rows) & (row < (h + 1) * rows)
        grad_middle = norm_pull(grad_second, normed, inv_spread, gain)
        grad_middle = grad_middle + jnp.where(is_own, cot.astype(F32), 0.0)
        grad_ref[span, :] = grad_middle
        low = grad_middle.astype(BF16)
        low_ref[span, :] = low
        wide[span, :] = mat(low, wo_ref[...], CONTRACT_LAST)
        sum_ref[0:1, :] += jnp.sum(low.astype(F32), axis=0, keepdims=True)
        sum_ref[1:2, :] += jnp.sum(grad_second * normed, axis=0, keepdims=True)
        sum_ref[2:3, :] += jnp.sum(grad_second, axis=0, keepdims=True)
        sum_ref[3:4, :] += jnp.sum(grad_hidden.astype(F32), axis=0, keepdims=True)
        return carry

    lax.fori_loop(0, 2, one_half, 0)
    own_ref[...] = mid[pl.ds(pl.multiple_of(h * rows, rows), rows), :]
    for g in range(nh):
        shift_now = g * group % 128
        at = g * group - shift_now
        top = wide[0:half, at : at + WIN]
        if shift_now:
            top = pltpu.roll(top, WIN - shift_now, axis=1)
        bottom = wide[half:length, at : at + WIN]
        if shift_now != 64:
            bottom = pltpu.roll(bottom, 64 - shift_now, axis=1)
        packed[g, :, 0:128] = top[:, 0:128].astype(BF16)
        packed[g, :, 128:256] = (top[:, 128:256] * left + bottom[:, 0:128] * right).astype(BF16)
        packed[g, :, 256:384] = bottom[:, 128:256].astype(BF16)
    for r in range(nh):
        outs[r][...] = packed[lax.rem(h - r + nh, nh)]


def middle_stage(place, attended, tokens, cot, wo, up, down, lines, nh):
    length, width = tokens.shape
    full = jax.ShapeDtypeStruct((length, width), BF16)
    piece = jax.ShapeDtypeStruct(attended.shape[1:], BF16)
    shapes = (
        full,
        jax.ShapeDtypeStruct((length // nh, width), F32),
        full,
        full,
        full,
        full,
        jax.ShapeDtypeStruct((length, width), F32),
        jax.ShapeDtypeStruct((8, width), F32),
    ) + (piece,) * nh
    return pl.pallas_call(
        functools.partial(middle_kernel, nh),
        out_shape=shapes,
        in_specs=[SMEM_SPEC] + [VMEM_SPEC] * 7,
        out_specs=(VMEM_SPEC,) * len(shapes),
        scratch_shapes=[
            pltpu.VMEM((length, width), F32),
            pltpu.VMEM((length, width), F32),
            pltpu.VMEM(attended.shape, BF16),
        ],
        compiler_params=kernel_params(),
        cost_estimate=pl.CostEstimate(flops=12 * length * width * width, bytes_accessed=12 * 2**20, transcendentals=0),
        name="middle",
    )(place, attended, tokens, cot, wo, up, down, lines)


def query_grads(meta, queries, grads, pieces, nh, nb):
    length = queries.shape[0]
    rows = length // nh
    count = len(pieces)
    return pl.pallas_call(
        functools.partial(query_kernel, nh, nb, count),
        out_shape=jax.ShapeDtypeStruct((length, WIN), BF16),
        in_specs=[SMEM_SPEC] + [VMEM_SPEC] * 2 + [ANY_SPEC] * count,
        out_specs=VMEM_SPEC,
        scratch_shapes=[
            pltpu.VMEM((nh * nb, rows, 384), BF16),
            pltpu.SemaphoreType.DMA((nb, nh)),
        ],
        compiler_params=kernel_params(),
        cost_estimate=cost(3, nh, nb, rows),
        name="query_grads",
    )(meta, queries, grads, *pieces)


def key_grads(meta, own, queries, grads, nh, nb):
    length = own.shape[0]
    rows = length // nh
    counts = (len(queries), len(grads))
    return pl.pallas_call(
        functools.partial(key_kernel, nh, nb, counts),
        out_shape=jax.ShapeDtypeStruct((length, 384), BF16),
        in_specs=[SMEM_SPEC, VMEM_SPEC] + [ANY_SPEC] * sum(counts),
        out_specs=VMEM_SPEC,
        scratch_shapes=[
            pltpu.VMEM((nh * nb, rows, WIN), BF16),
            pltpu.VMEM((nh * nb, rows, WIN), BF16),
            pltpu.SemaphoreType.DMA((nb, nh)),
            pltpu.SemaphoreType.DMA((nb, nh)),
        ],
        compiler_params=kernel_params(),
        cost_estimate=cost(4, nh, nb, rows),
        name="key_grads",
    )(meta, own, *queries, *grads)


def gather_blk_rows(here):
    if lax.axis_size("blk") != 8:
        whole = lax.all_gather(here, "blk", axis=0, tiled=False)
        return jnp.moveaxis(whole, 0, 1).reshape(-1, here.shape[-1])
    b = lax.axis_index("blk")
    core, x_bit, y_bit = b & 1, (b >> 1) & 1, b >> 2
    side, up, cross = swap(here, 2), swap(here, 4), swap(here, 6)
    square = in_pair(y_bit, in_pair(x_bit, here, side), in_pair(x_bit, up, cross))
    whole = in_pair(core, square, swap(square, 1))
    return whole.transpose(3, 1, 2, 0, 4, 5).reshape(-1, here.shape[-1])


def scatter_blk_rows(grad, nh, nb, late):
    width = grad.shape[-1]
    if nb != 8:
        parts = grad.reshape(nh, nb, -1, width)
        return lax.psum_scatter(parts, "blk", scatter_dimension=1, tiled=False).astype(BF16), late
    b = lax.axis_index("blk")
    core, x_bit, y_bit = b & 1, (b >> 1) & 1, b >> 2
    parts = grad.astype(BF16).reshape(nh, 2, 2, 2, -1, width)
    sent = swap(pick(parts, 1 - core, 3), 1)
    chip = (pick(parts, core, 3).astype(F32) + sent.astype(F32)).astype(BF16)
    chip, late = after((chip, late))

    def part(y, x):
        return pick(pick(chip, y, 1), x, 1)

    side = swap(part(y_bit, 1 - x_bit), 2)
    up = swap(part(1 - y_bit, x_bit), 4)
    cross = swap(part(1 - y_bit, 1 - x_bit), 6)
    mine = part(y_bit, x_bit).astype(F32) + side.astype(F32)
    return (mine + up.astype(F32) + cross.astype(F32)).astype(BF16), late


def shards(
    tokens,
    cotangent,
    doc_starts,
    norm_gain,
    norm_shift,
    triple_weight,
    query_bias,
    value_bias,
    output_weight,
    output_bias,
    final_gain,
    final_shift,
    up_weight,
    up_bias,
    down_weight,
    down_bias,
):
    nh = lax.axis_size("head")
    nb = lax.axis_size("blk")
    h = lax.axis_index("head")
    b = lax.axis_index("blk")
    rows, width = tokens.shape
    part = norm_gain.shape[0]
    group = HEADS // nh * HEAD_DIM
    ff_part = up_bias.shape[0]
    ff_group = nb * ff_part
    extra = max(part, 12)
    meta = jnp.concatenate([b.astype(jnp.int32)[None], doc_starts])

    packed = jnp.stack(
        [
            norm_gain,
            norm_shift,
            query_bias,
            value_bias,
            output_bias,
            final_gain,
            final_shift,
            down_bias,
        ]
    )
    packed = jnp.concatenate([packed, up_bias.reshape(4, part)], axis=0)
    if extra > 12:
        packed = jnp.pad(packed, ((0, extra - 12), (0, 0)))
    columns = triple_weight.reshape(part, 3, nh, group)
    pieces = [columns[:, 1], columns[:, 2], columns[:, 0]]
    if part == extra:
        pieces.append(jnp.broadcast_to(packed[:, None], (part, nh, part)))
    pieces.append(up_weight.reshape(part, nh, ff_group))
    pieces.append(jnp.broadcast_to(output_weight[:, None], (part, nh, width)))
    columns = exchange(jnp.concatenate(pieces, axis=-1).transpose(1, 0, 2))
    token_rows = spread(tokens).reshape(nh * rows, width)
    first_width = 3 * group + (part if part == extra else 0)
    group_weight = gather_blk_rows(columns[..., :first_width])

    late = jnp.concatenate(
        [
            columns[..., first_width : first_width + ff_group].reshape(-1, ff_group),
            down_weight,
            columns[..., first_width + ff_group :].reshape(-1, width),
        ],
        axis=0,
    )
    if part == extra:
        vectors = group_weight[:, 3 * group :].reshape(nh * nb, extra, part)[:, :12]
    else:
        vectors = lax.all_gather(packed, ("head", "blk"), axis=0, tiled=False)
    group_weight = group_weight[:, : 3 * group]
    lines = vectors[:, :8].transpose(1, 0, 2).reshape(8, width).astype(F32)
    gain_one, shift_one, query_all, value_all, out_bias, gain_two, shift_two, down_bias_all = (
        lines[i] for i in range(8)
    )
    up_bias_own = pick(vectors[:, 8:].reshape(nh, nb * ff_part), h, 0).astype(F32)

    key_value_weight = group_weight[:, : 2 * group]
    query_weight = jnp.pad(group_weight[:, 2 * group :], ((0, 0), (0, WIN - group)))
    token_wide = token_rows.astype(F32)
    normed_one, spread_one = norm_parts(token_wide)
    first_low = (normed_one * gain_one + shift_one).astype(BF16)
    value_bias_own = lax.dynamic_slice_in_dim(value_all, h * group, group)
    query_bias_own = lax.dynamic_slice_in_dim(query_all, h * group, group)
    kv_bias = jnp.concatenate([jnp.zeros((group,), F32), value_bias_own])
    key_values = (mat(first_low, key_value_weight) + kv_bias).astype(BF16)
    kv_pieces = gather_pieces(key_values)
    q_bias = jnp.pad(query_bias_own, (0, WIN - group))
    queries = (mat(first_low, query_weight) + q_bias).astype(BF16)
    late = lax.all_gather(after(late, kv_pieces[1 if nb == 8 else 0]), "blk", axis=0, tiled=False)
    up_own = jnp.moveaxis(late[:, : nh * part].reshape(nb, nh, part, ff_group), 0, 1)
    up_own = up_own.reshape(width, ff_group)
    down_own = late[:, nh * part : nh * part + ff_part].reshape(ff_group, width)
    out_own = jnp.moveaxis(late[:, nh * part + ff_part :].reshape(nb, nh, part, width), 0, 1)
    out_own = out_own.reshape(width, width)
    slow = jnp.concatenate([cotangent, jnp.zeros((rows // 8 * 3, width), BF16)], axis=0)
    slow = lax.all_gather(after(slow, token_rows), "head", axis=0, tiled=False)
    cot_all = slow[:, :rows].reshape(nh * rows, width)
    wide, attended = attend(meta, queries, kv_pieces, nh, nb)
    query_pieces = [lax.all_gather(after(queries, attended), "blk", axis=0, tiled=False)]

    lines_two = jnp.stack([out_bias, gain_two, shift_two, up_bias_own])
    head_slots = [attended] + [turn(attended, r) for r in range(1, nh)]
    head_slots, out_own, up_own, down_own = after((head_slots, out_own, up_own, down_own))
    (
        joined,
        output_own,
        second_low,
        active_low,
        grad_hidden,
        branch_grad,
        grad_middle,
        middle_sums,
        *grad_slots,
    ) = middle_stage(
        h.astype(jnp.int32)[None], by_head(head_slots), token_rows, slow, out_own, up_own, down_own, lines_two, nh
    )
    for r in range(1, nh):
        grad_slots[r] = turn(grad_slots[r], -r)

    branch_late, joined_late = branch_grad, joined
    cot_late, second_late, grad_slots[1] = after((cot_all, second_low, grad_slots[1]))
    output_part = mat(active_low, down_own).astype(BF16).reshape(nh, rows, width)
    grad_up_own = mat(second_late, grad_hidden, CONTRACT_FIRST).astype(BF16)
    grad_down_own = mat(active_low, cot_late, CONTRACT_FIRST).astype(BF16)
    grad_out = mat(joined_late, branch_late, CONTRACT_FIRST).astype(BF16).reshape(nh, nb, part, width)
    late_grads = jnp.concatenate(
        [
            jnp.moveaxis(grad_up_own.reshape(nh, nb, part, ff_group), 0, 1).reshape(nb, -1, width),
            grad_down_own.reshape(nb, ff_part, width),
            jnp.moveaxis(grad_out, 0, 1).reshape(nb, -1, width),
        ],
        axis=1,
    )
    late_sums = lax.psum_scatter(late_grads, "blk", scatter_dimension=0, tiled=False)

    grad_attended = delta_rows(wide, after(grad_slots, late_grads, output_part))
    grad_queries = query_grads(meta, queries, grad_attended, kv_pieces, nh, nb)
    grad_pieces = gather_pieces(grad_attended, grad_queries)
    output_blocks = exchange(after(output_part, grad_attended))
    query_pieces[0], output_blocks = after((query_pieces[0], output_blocks))
    grad_key_values = key_grads(meta, key_values, query_pieces, grad_pieces, nh, nb)

    grad_group = jnp.concatenate([grad_key_values, grad_queries[:, :group]], axis=1)
    first_part = mat(grad_group, group_weight, CONTRACT_LAST)
    grad_in = grad_middle + norm_pull(first_part, normed_one, spread_one, gain_one)
    grad_in = grad_in.astype(BF16).reshape(nh, rows, width)
    output_sum = jnp.sum(output_blocks.astype(F32), axis=0)
    output_rows = (output_own + output_sum + down_bias_all).astype(BF16)
    row_sums = pick(grad_in, h, 0).astype(F32)
    for r in range(1, nh):
        row_sums = row_sums + turn(pick(grad_in, lax.rem(h - r + nh, nh), 0), -r).astype(F32)
    first_late, grad_group = after((first_low, grad_group), grad_in)
    grad_triple_part = mat(first_late, grad_group, CONTRACT_FIRST).astype(BF16)

    group_sums = jnp.sum(grad_group.astype(F32), axis=0)
    placed = jnp.where(
        jnp.arange(nh)[None, :, None] == h,
        jnp.stack([group_sums[2 * group :], group_sums[group : 2 * group]])[:, None],
        0.0,
    ).reshape(2, width)
    up_b = middle_sums[3]
    up_b = jnp.where(jnp.arange(nh)[:, None] == h, up_b[None], 0.0).reshape(nh * nb, 4, part)
    sums = jnp.stack(
        [
            jnp.sum(first_part * normed_one, axis=0),
            jnp.sum(first_part, axis=0),
            placed[0],
            placed[1],
            middle_sums[0],
            middle_sums[1],
            middle_sums[2],
            jnp.sum(cotangent.astype(F32), axis=0),
        ]
    )
    sums = sums.reshape(8, nh * nb, part).transpose(1, 0, 2)
    sums = jnp.concatenate([sums, up_b], axis=1)
    if part == extra:
        low_sums = jnp.pad(sums.astype(BF16), ((0, 0), (0, extra - 12), (0, 0)))
        low_sums = low_sums.reshape(width, part)
        grad_triple_part = jnp.concatenate([grad_triple_part, low_sums], axis=1)
    else:
        sums = lax.psum(sums, ("head", "blk"))
        sums = pick(sums, h * nb + b, 0)
    here, late_sums = scatter_blk_rows(grad_triple_part, nh, nb, late_sums)
    sum_down_w = late_sums[nh * part : nh * part + ff_part].astype(F32)
    final = [
        here,
        late_sums[: nh * part].reshape(nh, part, ff_group),
        late_sums[nh * part + ff_part :].reshape(nh, part, width),
    ]
    final = jnp.concatenate(final, axis=-1)
    slots = [pick(final, h, 0)]
    for r in range(1, nh):
        slots.append(turn(pick(final, lax.rem(h - r + nh, nh), 0), -r))
    slots, row_sums = after((slots, row_sums))
    input_grad = row_sums.astype(BF16)
    final = by_group(slots).astype(F32)
    if part == extra:
        sums = jnp.sum(final[:, :12, 3 * group : first_width], axis=0)
    sum_triple = jnp.concatenate(
        [
            final[:, :, 2 * group : 3 * group].transpose(1, 0, 2).reshape(part, width),
            final[:, :, :group].transpose(1, 0, 2).reshape(part, width),
            final[:, :, group : 2 * group].transpose(1, 0, 2).reshape(part, width),
        ],
        axis=1,
    )
    sum_up_w = final[:, :, first_width : first_width + ff_group]
    sum_up_w = sum_up_w.transpose(1, 0, 2).reshape(part, nh * ff_group)
    sum_out_w = jnp.sum(final[:, :, first_width + ff_group :], axis=0)
    return (
        output_rows,
        input_grad,
        sums[0],
        sums[1],
        sum_triple,
        sums[2],
        sums[3],
        sum_out_w,
        sums[4],
        sums[5],
        sums[6],
        sum_up_w,
        sums[8:].reshape(ff_part),
        sum_down_w,
        sums[7],
    )


def solution(mesh):
    wide = P(("head", "blk"), None)
    thin = P(("head", "blk"))
    in_specs = (
        wide,
        wide,
        P(),
        thin,
        thin,
        wide,
        thin,
        thin,
        wide,
        thin,
        thin,
        thin,
        wide,
        thin,
        wide,
        thin,
    )
    out_specs = (
        wide,
        wide,
        thin,
        thin,
        wide,
        thin,
        thin,
        wide,
        thin,
        thin,
        thin,
        wide,
        thin,
        wide,
        thin,
    )
    return jax.shard_map(shards, mesh=mesh, in_specs=in_specs, out_specs=out_specs, check_vma=False)
```

```python
import functools

import jax
import jax.numpy as jnp
from jax import lax
from jax.experimental import pallas as pl
from jax.experimental.pallas import tpu as pltpu
from jax.sharding import PartitionSpec as P

HEADS = 12
HEAD_DIM = 64

epsilon = 1e-06
neg_fill = -1e30
root_half = 0.7071067811865476
inv_root_two_pi = 0.3989422804014327

F32 = jnp.float32
BF16 = jnp.bfloat16
WIN = 256
TILE_BLOCKS = 6
TILE_PARTS = ((0, 4), (4, 2))
CONTRACT_LAST = (((1,), (1,)), ((), ()))
FORWARD_BLOCKS = 6
CONTRACT_FIRST = (((0,), (0,)), ((), ()))
PLAIN = (((1,), (0,)), ((), ()))


def norm_parts(values):
    centre = jnp.mean(values, axis=-1, keepdims=True)
    offset = values - centre
    inv_spread = lax.rsqrt(jnp.mean(offset * offset, axis=-1, keepdims=True) + epsilon)
    return (offset * inv_spread, inv_spread)


def norm_pull(grad_out, normed, inv_spread, gain_full):
    grad_normed = grad_out * gain_full
    return inv_spread * (
        grad_normed
        - jnp.mean(grad_normed, axis=-1, keepdims=True)
        - normed * jnp.mean(grad_normed * normed, axis=-1, keepdims=True)
    )


def gelu_pair(hidden):
    normal_cdf = 0.5 * (1.0 + lax.erf(hidden * root_half))
    return (
        hidden * normal_cdf,
        normal_cdf + hidden * inv_root_two_pi * jnp.exp(-0.5 * hidden * hidden),
    )


def mat(left, right, dims=PLAIN):
    return lax.dot_general(left, right, dims, preferred_element_type=F32)


def exchange(x):
    return lax.all_to_all(x, "head", 0, 0, tiled=True)


def share(x):
    return exchange(jnp.broadcast_to(x[None], (lax.axis_size("head"),) + x.shape))


def turn(x, step):
    size = lax.axis_size("head")
    return lax.ppermute(x, "head", [(i, (i + step) % size) for i in range(size)])


def by_head(slots):
    size = len(slots)
    doubled = jnp.stack([slots[(size - 1 - i) % size] for i in range(2 * size - 1)])
    return lax.dynamic_slice_in_dim(doubled, size - 1 - lax.axis_index("head"), size, 0)


def spread(x):
    return by_head([x] + [turn(x, r) for r in range(1, lax.axis_size("head"))])


def by_group(slots):
    size = len(slots)
    doubled = jnp.stack([slots[i % size] for i in range(2 * size - 1)])
    start = lax.rem(size - lax.axis_index("head"), size)
    return lax.dynamic_slice_in_dim(doubled, start, size, 0)


def swap(x, bits):
    size = lax.axis_size("blk")
    return lax.ppermute(x, "blk", [(i, i ^ bits) for i in range(size)])


def in_pair(bit, mine, other):
    return jnp.where(bit == 0, jnp.stack([mine, other]), jnp.stack([other, mine]))


def pick(x, index, axis):
    return lax.dynamic_index_in_dim(x, index, axis, keepdims=False)


def after(value, *earlier):
    flat, tree = jax.tree.flatten(value)
    held = lax.optimization_barrier((tuple(flat), earlier))[0]
    return jax.tree.unflatten(tree, held)


def gather_pieces(x, *earlier):
    if lax.axis_size("blk") != 8:
        return [lax.all_gather(x, "blk", axis=0, tiled=False)]
    pieces = [None] * 8
    pieces[0] = x
    for bits in (2, 4, 6):
        pieces[bits] = swap(x, bits)
    for bits in (0, 2, 4, 6):
        pieces[bits + 1] = swap(after(pieces[bits], *earlier) if bits else x, 1)
    return pieces


def doc_range(meta, first, last, total):
    low, high = jnp.int32(0), jnp.int32(total)
    for i in range(meta.shape[0] - 1):
        start = meta[1 + i]
        low = jnp.where(start <= first, start, low)
        high = jnp.where(start > last, jnp.minimum(high, start), high)
    return low, high


def row_ranges(meta, first, rows, total):
    place = first + lax.broadcasted_iota(jnp.int32, (rows, 1), 0)
    low = jnp.zeros((rows, 1), jnp.int32)
    high = jnp.full((rows, 1), total, jnp.int32)
    for i in range(meta.shape[0] - 1):
        start = meta[1 + i]
        low = jnp.where(place >= start, start, low)
        high = jnp.where(place < start, jnp.minimum(high, start), high)
    return low, high


def head_rows(width, shift, scale):
    lane = lax.broadcasted_iota(jnp.int32, (1, width), 1)
    return [
        jnp.where((lane >= shift + 64 * i) & (lane < shift + 64 * (i + 1)), scale, 0.0).astype(F32)
        for i in range(3)
    ]


def spread_heads(block, rows):
    wide = block.astype(F32)
    return jnp.concatenate([wide * row for row in rows], axis=0).astype(BF16)


def block_of(stack, i, rows):
    return stack[i * rows : (i + 1) * rows]


def fold_heads(stack, rows):
    return stack[0] * rows[0] + stack[1] * rows[1] + stack[2] * rows[2]


def block_copies(meta, nh, nb, pieces, place, sems):
    b = meta[0]
    copies = []
    if len(pieces) == nb:
        for m, piece in enumerate(pieces):
            for r in range(nh):
                block = r * nb + jnp.bitwise_xor(b, m)
                copies.append(pltpu.make_async_copy(*place(piece, None, r, block), sems.at[m, r]))
        for copy in copies:
            copy.start()
        return copies

    def run(which):
        def one(i, carry):
            for r in range(nh):
                block = r * nb + i
                copy = pltpu.make_async_copy(*place(pieces[0], i, r, block), sems.at[i, r])
                (copy.start if which == 0 else copy.wait)()
            return carry

        lax.fori_loop(0, nb, one, 0)

    run(0)

    class Rest:
        def wait(self):
            run(1)

    return [Rest()]


def row_place(target, rows):
    def place(piece, index, r, block):
        source = piece if index is None else piece.at[index]
        return source.at[pl.ds(r * rows, rows), :], target.at[block]

    return place


def tile_bounds(meta, first, rows, total, blocks=TILE_BLOCKS):
    low, high = doc_range(meta, first, first + rows - 1, total)
    start = lax.div(low, rows)
    tile = blocks * rows
    return start, lax.div(high - start * rows + tile - 1, tile)


def tile_at(start, t, rows, total, blocks=TILE_BLOCKS):
    begin = start + t * blocks
    block = jnp.minimum(begin, total // rows - blocks)
    place = block * rows + lax.broadcasted_iota(jnp.int32, (1, blocks * rows), 1)
    return block, begin * rows, place


def lane_is(index):
    lane = lax.broadcasted_iota(jnp.int32, (1, 128), 1)
    return jnp.where(lane == index, 1.0, 0.0).astype(F32)


def in_lanes(columns):
    total = columns[0] * lane_is(0)
    for i in range(1, len(columns)):
        total = total + columns[i] * lane_is(i)
    return total


def in_parts(block):
    high = block.astype(BF16).astype(F32)
    middle = (block - high).astype(BF16).astype(F32)
    low = (block - high - middle).astype(BF16).astype(F32)
    return high + pltpu.roll(middle, 8, axis=1) + pltpu.roll(low, 16, axis=1)


def add_parts(block, lane):
    return block[:, lane : lane + 1] + block[:, lane + 8 : lane + 9] + block[:, lane + 16 : lane + 17]


def forward_kernel(nh, nb, count, meta, q_ref, *rest):
    pieces, (wide_ref, low_ref), (kv, sems) = rest[:count], rest[count : count + 2], rest[count + 2 :]
    rows = q_ref.shape[0] // nh
    total = nh * nb * rows
    tile = FORWARD_BLOCKS * rows
    b = meta[0]
    for copy in block_copies(meta, nh, nb, pieces, row_place(kv, rows), sems):
        copy.wait()
    query_rows = head_rows(WIN, 0, HEAD_DIM**-0.5)
    value_rows = head_rows(WIN, 64, 1.0)

    def one_block(r):
        first = (r * nb + b) * rows
        start, tiles = tile_bounds(meta, first, rows, total, FORWARD_BLOCKS)
        low, high = row_ranges(meta, first, rows, total)
        masked = spread_heads(q_ref[r * rows : (r + 1) * rows, :], query_rows)

        def step(t, state):
            top, norm, out = state
            block, begin, place = tile_at(start, t, rows, total, FORWARD_BLOCKS)
            keys = kv[pl.ds(block, FORWARD_BLOCKS), :, 0:WIN].reshape(tile, WIN)
            values = kv[pl.ds(block, FORWARD_BLOCKS), :, 128 : 128 + WIN].reshape(tile, WIN)
            allowed = (place >= jnp.maximum(low, begin)) & (place < high)
            scores = [mat(block_of(masked, i, rows), keys, CONTRACT_LAST) for i in range(3)]
            result = []
            for i in range(3):
                score = jnp.where(allowed, scores[i], neg_fill)
                new_top = jnp.maximum(top[i], jnp.max(score, axis=-1, keepdims=True))
                weights = jnp.exp(score - new_top)
                factor = jnp.exp(top[i] - new_top)
                new_norm = norm[i] * factor + jnp.sum(weights, axis=-1, keepdims=True)
                result.append((new_top, new_norm, out[i] * factor + mat(weights.astype(BF16), values)))
            return tuple(zip(*result))

        top, norm, out = lax.fori_loop(
            0,
            tiles,
            step,
            (
                (jnp.full((rows, 1), neg_fill, F32),) * 3,
                (jnp.zeros((rows, 1), F32),) * 3,
                (jnp.zeros((rows, WIN), F32),) * 3,
            ),
        )
        attended = fold_heads([out[i] / norm[i] for i in range(3)], value_rows)
        log_total = [top[i] + jnp.log(norm[i]) for i in range(3)]
        extra = in_lanes(log_total)
        wide_ref[r * rows : (r + 1) * rows, 0:128] = attended[:, 0:128] + extra
        wide_ref[r * rows : (r + 1) * rows, 128:256] = attended[:, 128:256]
        return attended

    half = nh // 2
    for r in range(half):
        left = pltpu.roll(one_block(r), WIN - 64, axis=1)
        right = one_block(r + half)
        span = slice(r * rows, (r + 1) * rows)
        low_ref[span, 0:128] = left[:, 0:128].astype(BF16)
        low_ref[span, 128:256] = (left[:, 128:256] + right[:, 0:128]).astype(BF16)
        low_ref[span, 256:384] = right[:, 128:256].astype(BF16)


def delta_kernel(nh, wide_ref, *rest):
    slots, grad_ref = rest[:nh], rest[nh]
    rows = wide_ref.shape[0] // nh
    half = nh // 2
    value_rows = head_rows(WIN, 64, 1.0)
    every = value_rows[0] + value_rows[1] + value_rows[2]

    def one_block(r, grad):
        span = slice(r * rows, (r + 1) * rows)
        grad = (grad * every).astype(BF16).astype(F32)
        wide = wide_ref[span, :]
        product = grad * wide
        stats = wide[:, 0:128] * (lane_is(0) + lane_is(1) + lane_is(2))
        for i in range(3):
            stats = stats + jnp.sum(product * value_rows[i], axis=-1, keepdims=True) * lane_is(3 + i)
        grad_ref[span, 0:128] = (grad[:, 0:128] + in_parts(stats)).astype(BF16)
        grad_ref[span, 128:256] = grad[:, 128:256].astype(BF16)

    for r in range(half):
        total = slots[0][r * rows : (r + 1) * rows, :].astype(F32)
        for i in range(1, nh):
            total = total + slots[i][r * rows : (r + 1) * rows, :].astype(F32)
        one_block(r, pltpu.roll(total[:, 0:WIN], 64, axis=1))
        one_block(r + half, total[:, 128 : 128 + WIN])


def query_kernel(nh, nb, count, meta, q_ref, g_ref, *rest):
    pieces, out_ref, (kv, sems) = rest[:count], rest[count], rest[count + 1 :]
    rows = q_ref.shape[0] // nh
    total = nh * nb * rows
    tile = TILE_BLOCKS * rows
    b = meta[0]
    for copy in block_copies(meta, nh, nb, pieces, row_place(kv, rows), sems):
        copy.wait()
    query_rows = head_rows(WIN, 0, HEAD_DIM**-0.5)
    value_rows = head_rows(WIN, 64, 1.0)
    for r in range(nh):
        span = slice(r * rows, (r + 1) * rows)
        first = (r * nb + b) * rows
        start, tiles = tile_bounds(meta, first, rows, total)
        low, high = row_ranges(meta, first, rows, total)
        masked = spread_heads(q_ref[span, :], query_rows)
        grads = spread_heads(g_ref[span, :], value_rows)
        stats = g_ref[span, 0:128].astype(F32)
        log_total = jnp.stack([add_parts(stats, i) for i in range(3)])
        delta = jnp.stack([add_parts(stats, 3 + i) for i in range(3)])

        def step(t, state):
            block, begin, place = tile_at(start, t, rows, total)
            allowed = (place >= jnp.maximum(low, begin)) & (place < high)
            parts = []
            for first_one, count_now in TILE_PARTS:
                keys = kv[pl.ds(block + first_one, count_now), :, 0:WIN].reshape(-1, WIN)
                values = kv[pl.ds(block + first_one, count_now), :, 128 : 128 + WIN].reshape(-1, WIN)
                scores = mat(masked, keys, CONTRACT_LAST)
                parts.append((keys, scores, mat(grads, values, CONTRACT_LAST)))
            for (first_one, count_now), (keys, scores, grad_probs) in zip(TILE_PARTS, parts):
                inside = allowed[:, first_one * rows : (first_one + count_now) * rows]
                scores = scores.reshape(3, rows, count_now * rows)
                grad_probs = grad_probs.reshape(3, rows, count_now * rows)
                probs = jnp.exp(jnp.where(inside[None], scores, neg_fill) - log_total)
                grad_scores = (probs * (grad_probs - delta)).astype(BF16)
                part = mat(grad_scores.reshape(3 * rows, count_now * rows), keys)
                state = state + part.reshape(3, rows, WIN)
            return state

        total_grad = lax.fori_loop(0, tiles, step, jnp.zeros((3, rows, WIN), F32))
        out_ref[span, :] = fold_heads(total_grad, query_rows).astype(BF16)


def key_kernel(nh, nb, counts, meta, kv_ref, *rest):
    both = counts[0] + counts[1]
    q_in, g_in, out_ref = rest[: counts[0]], rest[counts[0] : both], rest[both]
    queries_all, grads_all, q_sems, g_sems = rest[both + 1 :]
    rows = kv_ref.shape[0] // nh
    total = nh * nb * rows
    tile = TILE_BLOCKS * rows
    b = meta[0]
    copies = block_copies(meta, nh, nb, q_in, row_place(queries_all, rows), q_sems)
    copies += block_copies(meta, nh, nb, g_in, row_place(grads_all, rows), g_sems)
    for copy in copies:
        copy.wait()
    key_rows = head_rows(WIN, 0, HEAD_DIM**-0.5)
    value_rows = head_rows(WIN, 64, 1.0)
    line = lax.broadcasted_iota(jnp.int32, (8, WIN), 0)
    lane = lax.broadcasted_iota(jnp.int32, (8, WIN), 1)
    picked = (lane == line) | (lane == line + 8) | (lane == line + 16)
    choose = jnp.where(picked & (line < 6), 1.0, 0.0).astype(BF16)
    for r in range(nh):
        span = slice(r * rows, (r + 1) * rows)
        first = (r * nb + b) * rows
        start, tiles = tile_bounds(meta, first, rows, total)
        low, high = row_ranges(meta, first, rows, total)
        keys = spread_heads(kv_ref[span, 0:WIN], key_rows)
        values = spread_heads(kv_ref[span, 128 : 128 + WIN], value_rows)

        def step(t, state):
            grad_keys, grad_values = state
            block, begin, place = tile_at(start, t, rows, total)
            allowed = (place >= jnp.maximum(low, begin)) & (place < high)
            parts = []
            for first_one, count_now in TILE_PARTS:
                queries = queries_all[pl.ds(block + first_one, count_now)].reshape(-1, WIN)
                grads = grads_all[pl.ds(block + first_one, count_now)].reshape(-1, WIN)
                stats = mat(choose, grads, CONTRACT_LAST)
                scores = mat(keys, queries, CONTRACT_LAST)
                parts.append((queries, grads, stats, scores, mat(values, grads, CONTRACT_LAST)))
            for (first_one, count_now), (queries, grads, stats, scores, grad_probs) in zip(TILE_PARTS, parts):
                inside = allowed[:, first_one * rows : (first_one + count_now) * rows]
                scores = scores.reshape(3, rows, count_now * rows)
                grad_probs = grad_probs.reshape(3, rows, count_now * rows)
                log_total = jnp.stack([stats[i : i + 1] for i in range(3)])
                delta = jnp.stack([stats[3 + i : 4 + i] for i in range(3)])
                probs = jnp.exp(jnp.where(inside[None], scores, neg_fill) - log_total)
                grad_scores = (probs * (grad_probs - delta)).astype(BF16)
                part_value = mat(probs.astype(BF16).reshape(3 * rows, count_now * rows), grads)
                part_key = mat(grad_scores.reshape(3 * rows, count_now * rows), queries)
                grad_keys = grad_keys + part_key.reshape(3, rows, WIN)
                grad_values = grad_values + part_value.reshape(3, rows, WIN)
            return grad_keys, grad_values

        zero = jnp.zeros((3, rows, WIN), F32)
        grad_keys, grad_values = lax.fori_loop(0, tiles, step, (zero, zero))
        key_out = fold_heads(grad_keys, key_rows)
        value_out = fold_heads(grad_values, value_rows)
        out_ref[span, 0:128] = key_out[:, 0:128].astype(BF16)
        out_ref[span, 128:256] = (key_out[:, 128:256] + value_out[:, 0:128]).astype(BF16)
        out_ref[span, 256:384] = value_out[:, 128:256].astype(BF16)


SMEM_SPEC = pl.BlockSpec(memory_space=pltpu.SMEM)
VMEM_SPEC = pl.BlockSpec(memory_space=pltpu.VMEM)
ANY_SPEC = pl.BlockSpec(memory_space=pl.ANY)


def kernel_params():
    return pltpu.CompilerParams(vmem_limit_bytes=56 * 1024 * 1024)


def cost(matmuls, nh, nb, rows):
    flops = matmuls * 2 * 3 * rows * WIN * 1 * TILE_BLOCKS * rows * nh
    return pl.CostEstimate(flops=flops, bytes_accessed=nh * nb * rows * 384 * 2, transcendentals=0)


def attend(meta, queries, pieces, nh, nb):
    length = queries.shape[0]
    rows = length // nh
    count = len(pieces)
    return pl.pallas_call(
        functools.partial(forward_kernel, nh, nb, count),
        out_shape=(
            jax.ShapeDtypeStruct((length, WIN), F32),
            jax.ShapeDtypeStruct((length // 2, 384), BF16),
        ),
        in_specs=[SMEM_SPEC, VMEM_SPEC] + [ANY_SPEC] * count,
        out_specs=(VMEM_SPEC,) * 2,
        scratch_shapes=[
            pltpu.VMEM((nh * nb, rows, 384), BF16),
            pltpu.SemaphoreType.DMA((nb, nh)),
        ],
        compiler_params=kernel_params(),
        cost_estimate=cost(2, nh, nb, rows),
        name="attend",
    )(meta, queries, *pieces)


def delta_rows(wide, slots):
    nh = len(slots)
    return pl.pallas_call(
        functools.partial(delta_kernel, nh),
        out_shape=jax.ShapeDtypeStruct(wide.shape, BF16),
        in_specs=[VMEM_SPEC] * (1 + nh),
        out_specs=VMEM_SPEC,
        compiler_params=kernel_params(),
        name="delta",
    )(wide, *slots)


def middle_kernel(
    nh, place, att_ref, x_ref, cot_ref, wo_ref, up_ref, down_ref, line_ref, joined_ref, own_ref, a2_ref, act_ref,
    hid_ref, low_ref, grad_ref, sum_ref, *rest
):
    outs, (mid, wide, packed) = rest[:nh], rest[nh:]
    h = place[0]
    length, width = x_ref.shape
    half = length // 2
    rows = length // nh
    group = width // nh
    lane = lax.broadcasted_iota(jnp.int32, (1, 128), 1)
    left = jnp.where(lane < 64, 1.0, 0.0).astype(F32)
    right = 1.0 - left
    for side in range(2):
        span = slice(side * half, (side + 1) * half)
        for pair in range(nh // 2):
            first = att_ref[2 * pair, :, 128 * side : 128 * side + WIN].astype(F32)
            second = att_ref[2 * pair + 1, :, 128 * side : 128 * side + WIN].astype(F32)
            if side == 0:
                second = pltpu.roll(second, 64, axis=1)
            else:
                first = pltpu.roll(first, WIN - 64, axis=1)
            at = 2 * pair * group
            joined_ref[span, at : at + 128] = first[:, 0:128].astype(BF16)
            joined_ref[span, at + 128 : at + 256] = (first[:, 128:256] * left + second[:, 0:128] * right).astype(BF16)
            joined_ref[span, at + 256 : at + 384] = second[:, 128:256].astype(BF16)
    out_bias, gain, shift, up_bias = (line_ref[i : i + 1, :] for i in range(4))
    sum_ref[...] = jnp.zeros(sum_ref.shape, F32)

    def mean(value):
        return jnp.mean(value, axis=-1, keepdims=True)

    def one_half(side, carry):
        span = pl.ds(pl.multiple_of(side * half, half), half)
        middle = x_ref[span, :].astype(F32) + (mat(joined_ref[span, :], wo_ref[...]) + out_bias)
        mid[span, :] = middle
        normed, inv_spread = norm_parts(middle)
        second_low = (normed * gain + shift).astype(BF16)
        a2_ref[span, :] = second_low
        active, slope = gelu_pair(mat(second_low, up_ref[...]) + up_bias)
        act_ref[span, :] = active.astype(BF16)
        each = nh // 2
        cot = jnp.concatenate([cot_ref[side * each + i, 0:rows, :] for i in range(each)], axis=0)
        grad_hidden = (mat(cot, down_ref[...], CONTRACT_LAST) * slope).astype(BF16)
        hid_ref[span, :] = grad_hidden
        grad_second = mat(grad_hidden, up_ref[...], CONTRACT_LAST)
        row = side * half + lax.broadcasted_iota(jnp.int32, (half, 1), 0)
        is_own = (row >= h * rows) & (row < (h + 1) * rows)
        grad_middle = norm_pull(grad_second, normed, inv_spread, gain)
        grad_middle = grad_middle + jnp.where(is_own, cot.astype(F32), 0.0)
        grad_ref[span, :] = grad_middle
        low = grad_middle.astype(BF16)
        low_ref[span, :] = low
        wide[span, :] = mat(low, wo_ref[...], CONTRACT_LAST)
        sum_ref[0:1, :] += jnp.sum(low.astype(F32), axis=0, keepdims=True)
        sum_ref[1:2, :] += jnp.sum(grad_second * normed, axis=0, keepdims=True)
        sum_ref[2:3, :] += jnp.sum(grad_second, axis=0, keepdims=True)
        sum_ref[3:4, :] += jnp.sum(grad_hidden.astype(F32), axis=0, keepdims=True)
        return carry

    lax.fori_loop(0, 2, one_half, 0)
    own_ref[...] = mid[pl.ds(pl.multiple_of(h * rows, rows), rows), :]
    for g in range(nh):
        shift_now = g * group % 128
        at = g * group - shift_now
        top = wide[0:half, at : at + WIN]
        if shift_now:
            top = pltpu.roll(top, WIN - shift_now, axis=1)
        bottom = wide[half:length, at : at + WIN]
        if shift_now != 64:
            bottom = pltpu.roll(bottom, 64 - shift_now, axis=1)
        packed[g, :, 0:128] = top[:, 0:128].astype(BF16)
        packed[g, :, 128:256] = (top[:, 128:256] * left + bottom[:, 0:128] * right).astype(BF16)
        packed[g, :, 256:384] = bottom[:, 128:256].astype(BF16)
    for r in range(nh):
        outs[r][...] = packed[lax.rem(h - r + nh, nh)]


def middle_stage(place, attended, tokens, cot, wo, up, down, lines, nh):
    length, width = tokens.shape
    full = jax.ShapeDtypeStruct((length, width), BF16)
    piece = jax.ShapeDtypeStruct(attended.shape[1:], BF16)
    shapes = (
        full,
        jax.ShapeDtypeStruct((length // nh, width), F32),
        full,
        full,
        full,
        full,
        jax.ShapeDtypeStruct((length, width), F32),
        jax.ShapeDtypeStruct((8, width), F32),
    ) + (piece,) * nh
    return pl.pallas_call(
        functools.partial(middle_kernel, nh),
        out_shape=shapes,
        in_specs=[SMEM_SPEC] + [VMEM_SPEC] * 7,
        out_specs=(VMEM_SPEC,) * len(shapes),
        scratch_shapes=[
            pltpu.VMEM((length, width), F32),
            pltpu.VMEM((length, width), F32),
            pltpu.VMEM(attended.shape, BF16),
        ],
        compiler_params=kernel_params(),
        cost_estimate=pl.CostEstimate(flops=12 * length * width * width, bytes_accessed=12 * 2**20, transcendentals=0),
        name="middle",
    )(place, attended, tokens, cot, wo, up, down, lines)


def query_grads(meta, queries, grads, pieces, nh, nb):
    length = queries.shape[0]
    rows = length // nh
    count = len(pieces)
    return pl.pallas_call(
        functools.partial(query_kernel, nh, nb, count),
        out_shape=jax.ShapeDtypeStruct((length, WIN), BF16),
        in_specs=[SMEM_SPEC] + [VMEM_SPEC] * 2 + [ANY_SPEC] * count,
        out_specs=VMEM_SPEC,
        scratch_shapes=[
            pltpu.VMEM((nh * nb, rows, 384), BF16),
            pltpu.SemaphoreType.DMA((nb, nh)),
        ],
        compiler_params=kernel_params(),
        cost_estimate=cost(3, nh, nb, rows),
        name="query_grads",
    )(meta, queries, grads, *pieces)


def key_grads(meta, own, queries, grads, nh, nb):
    length = own.shape[0]
    rows = length // nh
    counts = (len(queries), len(grads))
    return pl.pallas_call(
        functools.partial(key_kernel, nh, nb, counts),
        out_shape=jax.ShapeDtypeStruct((length, 384), BF16),
        in_specs=[SMEM_SPEC, VMEM_SPEC] + [ANY_SPEC] * sum(counts),
        out_specs=VMEM_SPEC,
        scratch_shapes=[
            pltpu.VMEM((nh * nb, rows, WIN), BF16),
            pltpu.VMEM((nh * nb, rows, WIN), BF16),
            pltpu.SemaphoreType.DMA((nb, nh)),
            pltpu.SemaphoreType.DMA((nb, nh)),
        ],
        compiler_params=kernel_params(),
        cost_estimate=cost(4, nh, nb, rows),
        name="key_grads",
    )(meta, own, *queries, *grads)


def gather_blk_rows(here):
    if lax.axis_size("blk") != 8:
        whole = lax.all_gather(here, "blk", axis=0, tiled=False)
        return jnp.moveaxis(whole, 0, 1).reshape(-1, here.shape[-1])
    b = lax.axis_index("blk")
    core, x_bit, y_bit = b & 1, (b >> 1) & 1, b >> 2
    side, up, cross = swap(here, 2), swap(here, 4), swap(here, 6)
    square = in_pair(y_bit, in_pair(x_bit, here, side), in_pair(x_bit, up, cross))
    whole = in_pair(core, square, swap(square, 1))
    return whole.transpose(3, 1, 2, 0, 4, 5).reshape(-1, here.shape[-1])


def scatter_blk_rows(grad, nh, nb, late):
    width = grad.shape[-1]
    if nb != 8:
        parts = grad.reshape(nh, nb, -1, width)
        return lax.psum_scatter(parts, "blk", scatter_dimension=1, tiled=False).astype(BF16), late
    b = lax.axis_index("blk")
    core, x_bit, y_bit = b & 1, (b >> 1) & 1, b >> 2
    parts = grad.astype(BF16).reshape(nh, 2, 2, 2, -1, width)
    sent = swap(pick(parts, 1 - core, 3), 1)
    chip = (pick(parts, core, 3).astype(F32) + sent.astype(F32)).astype(BF16)
    chip, late = after((chip, late))

    def part(y, x):
        return pick(pick(chip, y, 1), x, 1)

    side = swap(part(y_bit, 1 - x_bit), 2)
    up = swap(part(1 - y_bit, x_bit), 4)
    cross = swap(part(1 - y_bit, 1 - x_bit), 6)
    mine = part(y_bit, x_bit).astype(F32) + side.astype(F32)
    return (mine + up.astype(F32) + cross.astype(F32)).astype(BF16), late


def shards(
    tokens,
    cotangent,
    doc_starts,
    norm_gain,
    norm_shift,
    triple_weight,
    query_bias,
    value_bias,
    output_weight,
    output_bias,
    final_gain,
    final_shift,
    up_weight,
    up_bias,
    down_weight,
    down_bias,
):
    nh = lax.axis_size("head")
    nb = lax.axis_size("blk")
    h = lax.axis_index("head")
    b = lax.axis_index("blk")
    rows, width = tokens.shape
    part = norm_gain.shape[0]
    group = HEADS // nh * HEAD_DIM
    ff_part = up_bias.shape[0]
    ff_group = nb * ff_part
    extra = max(part, 12)
    meta = jnp.concatenate([b.astype(jnp.int32)[None], doc_starts])

    packed = jnp.stack(
        [
            norm_gain,
            norm_shift,
            query_bias,
            value_bias,
            output_bias,
            final_gain,
            final_shift,
            down_bias,
        ]
    )
    packed = jnp.concatenate([packed, up_bias.reshape(4, part)], axis=0)
    if extra > 12:
        packed = jnp.pad(packed, ((0, extra - 12), (0, 0)))
    columns = triple_weight.reshape(part, 3, nh, group)
    pieces = [columns[:, 1], columns[:, 2], columns[:, 0]]
    if part == extra:
        pieces.append(jnp.broadcast_to(packed[:, None], (part, nh, part)))
    pieces.append(up_weight.reshape(part, nh, ff_group))
    pieces.append(jnp.broadcast_to(output_weight[:, None], (part, nh, width)))
    columns = exchange(jnp.concatenate(pieces, axis=-1).transpose(1, 0, 2))
    token_rows = spread(tokens).reshape(nh * rows, width)
    first_width = 3 * group + (part if part == extra else 0)
    group_weight = gather_blk_rows(columns[..., :first_width])

    late = jnp.concatenate(
        [
            columns[..., first_width : first_width + ff_group].reshape(-1, ff_group),
            down_weight,
            columns[..., first_width + ff_group :].reshape(-1, width),
        ],
        axis=0,
    )
    if part == extra:
        vectors = group_weight[:, 3 * group :].reshape(nh * nb, extra, part)[:, :12]
    else:
        vectors = lax.all_gather(packed, ("head", "blk"), axis=0, tiled=False)
    group_weight = group_weight[:, : 3 * group]
    lines = vectors[:, :8].transpose(1, 0, 2).reshape(8, width).astype(F32)
    gain_one, shift_one, query_all, value_all, out_bias, gain_two, shift_two, down_bias_all = (
        lines[i] for i in range(8)
    )
    up_bias_own = pick(vectors[:, 8:].reshape(nh, nb * ff_part), h, 0).astype(F32)

    key_value_weight = group_weight[:, : 2 * group]
    query_weight = jnp.pad(group_weight[:, 2 * group :], ((0, 0), (0, WIN - group)))
    token_wide = token_rows.astype(F32)
    normed_one, spread_one = norm_parts(token_wide)
    first_low = (normed_one * gain_one + shift_one).astype(BF16)
    value_bias_own = lax.dynamic_slice_in_dim(value_all, h * group, group)
    query_bias_own = lax.dynamic_slice_in_dim(query_all, h * group, group)
    kv_bias = jnp.concatenate([jnp.zeros((group,), F32), value_bias_own])
    key_values = (mat(first_low, key_value_weight) + kv_bias).astype(BF16)
    kv_pieces = gather_pieces(key_values)
    q_bias = jnp.pad(query_bias_own, (0, WIN - group))
    queries = (mat(first_low, query_weight) + q_bias).astype(BF16)
    late = lax.all_gather(after(late, kv_pieces[1 if nb == 8 else 0]), "blk", axis=0, tiled=False)
    up_own = jnp.moveaxis(late[:, : nh * part].reshape(nb, nh, part, ff_group), 0, 1)
    up_own = up_own.reshape(width, ff_group)
    down_own = late[:, nh * part : nh * part + ff_part].reshape(ff_group, width)
    out_own = jnp.moveaxis(late[:, nh * part + ff_part :].reshape(nb, nh, part, width), 0, 1)
    out_own = out_own.reshape(width, width)
    slow = jnp.concatenate([cotangent, jnp.zeros((rows // 8 * 3, width), BF16)], axis=0)
    slow = lax.all_gather(after(slow, token_rows), "head", axis=0, tiled=False)
    cot_all = slow[:, :rows].reshape(nh * rows, width)
    wide, attended = attend(meta, queries, kv_pieces, nh, nb)
    query_pieces = [lax.all_gather(after(queries, attended), "blk", axis=0, tiled=False)]

    lines_two = jnp.stack([out_bias, gain_two, shift_two, up_bias_own])
    head_slots = [attended] + [turn(attended, r) for r in range(1, nh)]
    head_slots, out_own, up_own, down_own = after((head_slots, out_own, up_own, down_own))
    (
        joined,
        output_own,
        second_low,
        active_low,
        grad_hidden,
        branch_grad,
        grad_middle,
        middle_sums,
        *grad_slots,
    ) = middle_stage(
        h.astype(jnp.int32)[None], by_head(head_slots), token_rows, slow, out_own, up_own, down_own, lines_two, nh
    )
    for r in range(1, nh):
        grad_slots[r] = turn(grad_slots[r], -r)

    cot_late, second_late, branch_late, grad_slots[1] = after((cot_all, second_low, branch_grad, grad_slots[1]))
    output_part = mat(active_low, down_own).astype(BF16).reshape(nh, rows, width)
    grad_up_own = mat(second_late, grad_hidden, CONTRACT_FIRST).astype(BF16)
    grad_down_own = mat(active_low, cot_late, CONTRACT_FIRST).astype(BF16)
    grad_out = mat(joined, branch_late, CONTRACT_FIRST).astype(BF16).reshape(nh, nb, part, width)
    late_grads = jnp.concatenate(
        [
            jnp.moveaxis(grad_up_own.reshape(nh, nb, part, ff_group), 0, 1).reshape(nb, -1, width),
            grad_down_own.reshape(nb, ff_part, width),
            jnp.moveaxis(grad_out, 0, 1).reshape(nb, -1, width),
        ],
        axis=1,
    )
    late_sums = lax.psum_scatter(late_grads, "blk", scatter_dimension=0, tiled=False)

    grad_attended = delta_rows(wide, after(grad_slots, late_grads, output_part))
    grad_queries = query_grads(meta, queries, grad_attended, kv_pieces, nh, nb)
    grad_pieces = gather_pieces(grad_attended, grad_queries)
    output_blocks = exchange(after(output_part, grad_attended))
    query_pieces[0], output_blocks = after((query_pieces[0], output_blocks))
    grad_key_values = key_grads(meta, key_values, query_pieces, grad_pieces, nh, nb)

    grad_group = jnp.concatenate([grad_key_values, grad_queries[:, :group]], axis=1)
    first_part = mat(grad_group, group_weight, CONTRACT_LAST)
    grad_in = grad_middle + norm_pull(first_part, normed_one, spread_one, gain_one)
    grad_in = grad_in.astype(BF16).reshape(nh, rows, width)
    output_sum = jnp.sum(output_blocks.astype(F32), axis=0)
    output_rows = (output_own + output_sum + down_bias_all).astype(BF16)
    row_sums = pick(grad_in, h, 0).astype(F32)
    for r in range(1, nh):
        row_sums = row_sums + turn(pick(grad_in, lax.rem(h - r + nh, nh), 0), -r).astype(F32)
    first_late, grad_group = after((first_low, grad_group), grad_in)
    grad_triple_part = mat(first_late, grad_group, CONTRACT_FIRST).astype(BF16)

    group_sums = jnp.sum(grad_group.astype(F32), axis=0)
    placed = jnp.where(
        jnp.arange(nh)[None, :, None] == h,
        jnp.stack([group_sums[2 * group :], group_sums[group : 2 * group]])[:, None],
        0.0,
    ).reshape(2, width)
    up_b = middle_sums[3]
    up_b = jnp.where(jnp.arange(nh)[:, None] == h, up_b[None], 0.0).reshape(nh * nb, 4, part)
    sums = jnp.stack(
        [
            jnp.sum(first_part * normed_one, axis=0),
            jnp.sum(first_part, axis=0),
            placed[0],
            placed[1],
            middle_sums[0],
            middle_sums[1],
            middle_sums[2],
            jnp.sum(cotangent.astype(F32), axis=0),
        ]
    )
    sums = sums.reshape(8, nh * nb, part).transpose(1, 0, 2)
    sums = jnp.concatenate([sums, up_b], axis=1)
    if part == extra:
        low_sums = jnp.pad(sums.astype(BF16), ((0, 0), (0, extra - 12), (0, 0)))
        low_sums = low_sums.reshape(width, part)
        grad_triple_part = jnp.concatenate([grad_triple_part, low_sums], axis=1)
    else:
        sums = lax.psum(sums, ("head", "blk"))
        sums = pick(sums, h * nb + b, 0)
    here, late_sums = scatter_blk_rows(grad_triple_part, nh, nb, late_sums)
    sum_down_w = late_sums[nh * part : nh * part + ff_part].astype(F32)
    final = [
        here,
        late_sums[: nh * part].reshape(nh, part, ff_group),
        late_sums[nh * part + ff_part :].reshape(nh, part, width),
    ]
    final = jnp.concatenate(final, axis=-1)
    slots = [pick(final, h, 0)]
    for r in range(1, nh):
        slots.append(turn(pick(final, lax.rem(h - r + nh, nh), 0), -r))
    slots, row_sums = after((slots, row_sums))
    input_grad = row_sums.astype(BF16)
    final = by_group(slots).astype(F32)
    if part == extra:
        sums = jnp.sum(final[:, :12, 3 * group : first_width], axis=0)
    sum_triple = jnp.concatenate(
        [
            final[:, :, 2 * group : 3 * group].transpose(1, 0, 2).reshape(part, width),
            final[:, :, :group].transpose(1, 0, 2).reshape(part, width),
            final[:, :, group : 2 * group].transpose(1, 0, 2).reshape(part, width),
        ],
        axis=1,
    )
    sum_up_w = final[:, :, first_width : first_width + ff_group]
    sum_up_w = sum_up_w.transpose(1, 0, 2).reshape(part, nh * ff_group)
    sum_out_w = jnp.sum(final[:, :, first_width + ff_group :], axis=0)
    return (
        output_rows,
        input_grad,
        sums[0],
        sums[1],
        sum_triple,
        sums[2],
        sums[3],
        sum_out_w,
        sums[4],
        sums[5],
        sums[6],
        sum_up_w,
        sums[8:].reshape(ff_part),
        sum_down_w,
        sums[7],
    )


def solution(mesh):
    wide = P(("head", "blk"), None)
    thin = P(("head", "blk"))
    in_specs = (
        wide,
        wide,
        P(),
        thin,
        thin,
        wide,
        thin,
        thin,
        wide,
        thin,
        thin,
        thin,
        wide,
        thin,
        wide,
        thin,
    )
    out_specs = (
        wide,
        wide,
        thin,
        thin,
        wide,
        thin,
        thin,
        wide,
        thin,
        thin,
        thin,
        wide,
        thin,
        wide,
        thin,
    )
    return jax.shard_map(shards, mesh=mesh, in_specs=in_specs, out_specs=out_specs, check_vma=False)
```
